128 devices in a mesh: ctx: 8 (over y, x_lo), tp: 16 (over x_hi, z, core).
Axes of the slice: x: 4 (x_hi: 2, x_lo: 2; x = x_hi * 2 + x_lo), y: 4, z: 4, core: 2. Of those that a mesh axis runs over, the one named last changes fastest.
Arguments:
- tokens: bfloat16 [4096, 4096], P(('ctx', 'tp')), may hold values from -16 to 16
- upstream: bfloat16 [4096, 4096], P('ctx', 'tp'), may hold values from -6 to 6
- w_query: bfloat16 [4096, 4096], P('ctx', 'tp')
- w_keyval: bfloat16 [4096, 2048], P('ctx', 'tp')
- positions: int32 [4096], replicated, may hold values from 0 to 4095, as said below
- documents: int32 [4096], replicated, may hold values from 0 to 3, never falling along the last dimension, each value on 1 to 2048 neighbouring positions
Outputs:
- token_grad: bfloat16 [4096, 4096], P(('ctx', 'tp'))
- query_grad: float32 [4096, 4096], P('ctx', 'tp')
- keyval_grad: float32 [4096, 2048], P('ctx', 'tp')
The draws below stay inside these ranges and needn't reach their ends.
Inputs may be any that keep to these rules, and one draw needn't show every extreme that they name: Each stored run of 512 tokens holds consecutive increasing positions; the two runs of the tokens of one context rank are the blocks k and 15 - k of the sequence for some k; all runs together hold every position once.
All inputs are finite; a program needn't handle non-finite values.
Results may differ from the reference program's by a relative error of at most 0.02.
The reference program's roundings to bfloat16 on the way count: a program that leaves them out, or rounds other values in their place, can miss the bound.
Values may be sent and summed in bfloat16 or wider, within the bound.
A program may use at most 128 MiB of HBM per device.

```python
import math
import jax
import jax.numpy as jnp
import numpy as np
from jax import lax

MODEL_DIMENSION = 4096
QUERY_HEADS = 32
KEY_VALUE_HEADS = 8
HEAD_DIMENSION = 128
TOK_CTX = 512
DOCS = 4
SEQUENCE_TOKENS = 4096
BLOCK = 256
BLOCKS = 16
N_CTX = 8


def query_weight_matrix(key):
    rotary_base = jax.random.normal(jax.random.fold_in(key, 11), (MODEL_DIMENSION, QUERY_HEADS * HEAD_DIMENSION), jnp.float32)
    return jnp.clip(rotary_base, -6.0, 6.0) * MODEL_DIMENSION ** (-0.5)


def draw_tokens(key, part):
    rotary_base = jax.random.normal(jax.random.fold_in(key, 21), (SEQUENCE_TOKENS, MODEL_DIMENSION), jnp.float32)
    return jnp.clip(rotary_base, -16.0, 16.0).astype(jnp.bfloat16)


def draw_w_query(key, part):
    return query_weight_matrix(key).astype(jnp.bfloat16)


def draw_w_keyval(key, part):
    rotary_base = jax.random.normal(jax.random.fold_in(key, 12), (MODEL_DIMENSION, KEY_VALUE_HEADS, 2, HEAD_DIMENSION), jnp.float32)
    rotary_base = jnp.clip(rotary_base, -6.0, 6.0) * MODEL_DIMENSION ** (-0.5)
    return rotary_base.reshape(MODEL_DIMENSION, 2 * KEY_VALUE_HEADS * HEAD_DIMENSION).astype(jnp.bfloat16)


def draw_positions(key, part):
    pair_count = BLOCKS // 2
    pairs = jax.random.permutation(jax.random.fold_in(key, 31), pair_count).astype(jnp.int32)
    flips = jax.random.randint(jax.random.fold_in(key, 32), (pair_count,), 0, 2).astype(jnp.int32)
    leading = jnp.where(flips == 0, pairs, BLOCKS - 1 - pairs)
    trailing = BLOCKS - 1 - leading
    order = jnp.stack([leading, trailing], axis=1).reshape(BLOCKS)
    offsets = jnp.arange(BLOCK, dtype=jnp.int32)
    return (order[:, None] * BLOCK + offsets[None, :]).reshape(BLOCKS * BLOCK).astype(jnp.int32)


def with_spikes(values, own_key, source, target, shards_of, factor):
    def block_of(position):
        return (jnp.arange(values.shape[position]) // (values.shape[position] // shards_of)).reshape((-1,) + (1,) * (values.ndim - 1 - position))

    first = jax.random.permutation(own_key, shards_of)[block_of(target)]
    other_side = (block_of(target) + shards_of // 2) % shards_of
    return jnp.where((block_of(source) == first) | (block_of(source) == other_side), factor * values, values)


def levels(own_key, dims, cuts, smallest, high):
    gain = 1.0
    for axis_at, shards_of in cuts:
        heights = jax.random.uniform(jax.random.fold_in(jax.random.fold_in(own_key, 6), axis_at), (shards_of,), jnp.float32, smallest / len(cuts), high / len(cuts))
        gain = gain * jnp.repeat(jnp.exp(heights), dims[axis_at] // shards_of).reshape((-1,) + (1,) * (len(dims) - 1 - axis_at))
    return gain


def split_up(amount, total, limit, slope):
    portions = [(1 << 20) // math.isqrt(grade ** slope) + 1 for grade in range(2, amount + 1)]
    spare, holding = total - limit - (amount - 1), [1] * (amount - 1)
    while spare > 0:
        candidates = [i for i in range(amount - 1) if holding[i] < limit]
        pool, left = sum([portions[i] for i in candidates]), spare
        for i in candidates:
            more = min(limit - holding[i], max(1, left * portions[i] // pool), spare)
            holding[i] = holding[i] + more
            spare = spare - more
    return np.array([limit] + holding)


def uneven_parts(key, number_of, total, limit, skew):
    if number_of == 2:
        one = jax.random.randint(key, (), max(1, total - limit), min(limit, total - 1) + 1)
        return jnp.stack([one, total - one])
    sizes = jnp.asarray(split_up(number_of, total, limit, skew), jnp.int32)
    couples = (number_of - 1) // 2
    donor, sink = sizes[1:1 + 2 * couples:2], sizes[2:2 + 2 * couples:2]
    slack = jnp.minimum(donor - 1, limit - sink)
    shifted = jax.random.randint(jax.random.fold_in(key, 1), (couples,), 0, 1 << 20) % (slack + 1)
    sizes = sizes.at[1:1 + 2 * couples:2].set(donor - shifted).at[2:2 + 2 * couples:2].set(sink + shifted)
    return sizes[jax.random.permutation(jax.random.fold_in(key, 2), number_of)]


def bell_draw_with(stream_key, extent, spread, most, pieces, heavy, held_as=jnp.bfloat16):
    entries = spread * jax.random.normal(stream_key, extent, jnp.float32)
    if pieces:
        entries = entries * levels(stream_key, extent, pieces, -0.22, 0.18)
    return jnp.clip(with_spikes(entries, jax.random.fold_in(stream_key, 3), *heavy), -most, most).astype(held_as)


def setup_inputs(seed: int = 0) -> dict:
    splits = jax.random.split(jax.random.key(seed), 7)
    tokens = draw_tokens(jax.random.fold_in(splits[6], 71), 0)
    upstream = bell_draw_with(splits[1], (SEQUENCE_TOKENS, QUERY_HEADS * HEAD_DIMENSION), 1.0, 6.0, ((0, 8), (1, 16)), (1, 0, 16, 2.0))
    w_query = draw_w_query(jax.random.fold_in(splits[6], 71), 0)
    w_keyval = draw_w_keyval(jax.random.fold_in(splits[6], 71), 0)
    positions = draw_positions(jax.random.fold_in(splits[6], 71), 0)
    documents = jnp.searchsorted(jnp.cumsum(uneven_parts(splits[5], DOCS, SEQUENCE_TOKENS, SEQUENCE_TOKENS // 2, 2)), jnp.arange(SEQUENCE_TOKENS), side="right").astype(jnp.int32)
    return {"tokens": tokens, "upstream": upstream, "w_query": w_query, "w_keyval": w_keyval, "positions": positions, "documents": documents}


rope_base = 500000.0


def rotation_tables(positions):
    half_width = HEAD_DIMENSION // 2
    frequency = rope_base ** (-(jnp.arange(half_width, dtype=jnp.float32) * 2.0 / HEAD_DIMENSION))
    angles = positions.astype(jnp.float32)[:, None] * frequency[None, :]
    cosine = jnp.concatenate([jnp.cos(angles), jnp.cos(angles)], axis=1)
    sine = jnp.concatenate([jnp.sin(angles), jnp.sin(angles)], axis=1)
    return cosine, sine


def rotate(values, cosine, sine):
    half_width = values.shape[-1] // 2
    turned = jnp.concatenate([-values[..., half_width:], values[..., :half_width]], axis=-1)
    return values * cosine[:, None, :] + turned * sine[:, None, :]


def rotate_back(gradient, cosine, sine):
    half_width = gradient.shape[-1] // 2
    scaled = gradient * sine[:, None, :]
    turned = jnp.concatenate([scaled[..., half_width:], -scaled[..., :half_width]], axis=-1)
    return gradient * cosine[:, None, :] + turned


def reference(tokens, upstream, w_query, w_keyval, positions, documents):
    f32 = jnp.float32
    scaling = HEAD_DIMENSION ** -0.5
    query_raw = jnp.dot(tokens, w_query, preferred_element_type=f32)
    key_value_rows = jnp.dot(tokens, w_keyval, preferred_element_type=f32).astype(jnp.bfloat16)
    cosine, sine = rotation_tables(positions)
    query_rows = rotate(query_raw.reshape(SEQUENCE_TOKENS, QUERY_HEADS, HEAD_DIMENSION), cosine, sine).astype(jnp.bfloat16)
    key_value_quad = key_value_rows.reshape(SEQUENCE_TOKENS, KEY_VALUE_HEADS, 2, HEAD_DIMENSION)
    key = rotate(key_value_quad[:, :, 0].astype(f32), cosine, sine).astype(jnp.bfloat16)
    value = key_value_quad[:, :, 1]
    doc_of = jnp.take(documents, positions)
    visible = (positions[None, :] <= positions[:, None]) & (doc_of[None, :] == doc_of[:, None])
    group_width = QUERY_HEADS // KEY_VALUE_HEADS
    query_head_groups = query_rows.reshape(SEQUENCE_TOKENS, KEY_VALUE_HEADS, group_width, HEAD_DIMENSION).transpose(1, 0, 2, 3)
    gradient_groups = upstream.reshape(SEQUENCE_TOKENS, KEY_VALUE_HEADS, group_width, HEAD_DIMENSION).transpose(1, 0, 2, 3)
    key_groups = key.transpose(1, 0, 2)
    value_groups = value.transpose(1, 0, 2)

    def one_group(inputs):
        query_g, grad_g, key_g, value_g = inputs
        query_f = query_g.astype(f32)
        grad_f = grad_g.astype(f32)
        key_f = key_g.astype(f32)
        value_f = value_g.astype(f32)
        scores = jnp.einsum('qhd,kd->hqk', query_f, key_f) * scaling
        scores = jnp.where(visible[None], scores, -1e30)
        row_peak = jnp.max(scores, axis=-1, keepdims=True)
        exponent = jnp.exp(scores - row_peak)
        probs = exponent / jnp.sum(exponent, axis=-1, keepdims=True)
        probs_half = probs.astype(jnp.bfloat16).astype(f32)
        output = jnp.einsum('hqk,kd->qhd', probs_half, value_f)
        deltas = jnp.sum(grad_f * output, axis=-1)
        prob_grad = jnp.einsum('qhd,kd->hqk', grad_f, value_f)
        score_grad = (probs * (prob_grad - deltas.T[:, :, None])).astype(jnp.bfloat16).astype(f32)
        dquery = jnp.einsum('hqk,kd->qhd', score_grad, key_f) * scaling
        dkey = jnp.einsum('hqk,qhd->kd', score_grad, query_f) * scaling
        dvalue = jnp.einsum('hqk,qhd->kd', probs_half, grad_f)
        return dquery, dkey, dvalue

    dquery, dkey, dvalue = lax.map(one_group, (query_head_groups, gradient_groups, key_groups, value_groups))
    dquery = dquery.transpose(1, 0, 2, 3).reshape(SEQUENCE_TOKENS, QUERY_HEADS, HEAD_DIMENSION)
    query_back = rotate_back(dquery, cosine, sine).astype(jnp.bfloat16).reshape(SEQUENCE_TOKENS, QUERY_HEADS * HEAD_DIMENSION)
    key_backward = rotate_back(dkey.transpose(1, 0, 2), cosine, sine).astype(jnp.bfloat16)
    value_backward = dvalue.transpose(1, 0, 2).astype(jnp.bfloat16)
    key_value_backward = jnp.stack([key_backward, value_backward], axis=2).reshape(SEQUENCE_TOKENS, 2 * KEY_VALUE_HEADS * HEAD_DIMENSION)
    token_grad = jnp.dot(query_back, w_query.T, preferred_element_type=f32)
    token_grad = token_grad + jnp.dot(key_value_backward, w_keyval.T, preferred_element_type=f32)
    row_grads = jnp.concatenate([query_back, key_value_backward], axis=1)
    token_blocks = tokens.reshape(N_CTX, TOK_CTX, MODEL_DIMENSION)
    grad_blocks = row_grads.reshape(N_CTX, TOK_CTX, row_grads.shape[1])

    def accumulate(running, inputs):
        token_block, grad_block = inputs
        term = jnp.dot(token_block.T, grad_block, preferred_element_type=f32)
        term = lax.optimization_barrier(term.astype(jnp.bfloat16)).astype(f32)
        return running + term, None

    start_value = jnp.zeros((MODEL_DIMENSION, row_grads.shape[1]), f32)
    weight_grad, _ = lax.scan(accumulate, start_value, (token_blocks, grad_blocks))
    return token_grad.astype(jnp.bfloat16), weight_grad[:, :QUERY_HEADS * HEAD_DIMENSION], weight_grad[:, QUERY_HEADS * HEAD_DIMENSION:]
```

```python
import jax
import jax.numpy as jnp
from jax import lax
from jax.experimental import pallas as pl
from jax.experimental.pallas import tpu as pltpu
from jax.sharding import PartitionSpec as P

KEY_VALUE_HEADS = 8
HEAD_DIMENSION = 128


rope_base = 500000.0


def side_by_side(arrays, axis, dim, along):
    both = jnp.concatenate(arrays, axis=along)
    filled, at, gathered = (lax.all_gather(both, axis, axis=dim, tiled=True), 0, [])
    for a in arrays:
        gathered.append(lax.slice_in_dim(filled, at, at + a.shape[along], axis=along))
        at += a.shape[along]
    return tuple(gathered)


def partner_2(block, axis, bit):
    count = lax.axis_size(axis)
    route = []
    for low in range(count):
        high = low | 1 << bit
        if high != low and high < count:
            route += [(low, high), (high, low)]
    return lax.ppermute(block, axis, route)


def copy_for_each(x, axis):
    count = lax.axis_size(axis)
    return lax.all_to_all(jnp.broadcast_to(x[None], (count, *x.shape)), axis, 0, 0, tiled=True)


def laid_out(blocks, dim):
    lengths = list(blocks.shape[1:])
    lengths[dim] *= blocks.shape[0]
    return jnp.moveaxis(blocks, 0, dim).reshape(lengths)


def gathered_copies(x, axis, dim):
    blocks = copy_for_each(x, axis)
    return laid_out(blocks, dim)


def cut_along(x, dim, count):
    lengths = x.shape
    blocks = x.reshape(*lengths[:dim], count, lengths[dim] // count, *lengths[dim + 1 :])
    return jnp.moveaxis(blocks, dim, 0)


def summed_on_arrival(x, axis, dim):
    count = lax.axis_size(axis)
    blocks = lax.all_to_all(cut_along(x, dim, count), axis, 0, 0, tiled=True)
    return jnp.sum(blocks.astype(jnp.float32), axis=0)


def rotation_tables(positions):
    half_width = HEAD_DIMENSION // 2
    frequency = rope_base ** (-(jnp.arange(half_width, dtype=jnp.float32) * 2.0 / HEAD_DIMENSION))
    angles = positions.astype(jnp.float32)[:, None] * frequency[None, :]
    cosine = jnp.concatenate([jnp.cos(angles), jnp.cos(angles)], axis=1)
    sine = jnp.concatenate([jnp.sin(angles), jnp.sin(angles)], axis=1)
    return (cosine, sine)


def rotate(values, cosine, sine):
    half_width = values.shape[-1] // 2
    turned = jnp.concatenate([-values[..., half_width:], values[..., :half_width]], axis=-1)
    return values * cosine[:, None, :] + turned * sine[:, None, :]


def rotate_back(gradient, cosine, sine):
    half_width = gradient.shape[-1] // 2
    scaled = gradient * sine[:, None, :]
    turned = jnp.concatenate([scaled[..., half_width:], -scaled[..., :half_width]], axis=-1)
    return gradient * cosine[:, None, :] + turned


def attend_kernel(pos_ref, doc_ref, q_ref, up_ref, k_ref, v_ref, cos_ref, sin_ref, qb_ref, dkv_ref,
                  score_sc, grad_sc, q2_sc, up2_sc, dq_sc, dk_sc, dv_sc, where_sm):
    f32 = jnp.float32
    bf16 = jnp.bfloat16
    run = 256
    rows = 2 * run
    scaling = HEAD_DIMENSION ** (-0.5)
    log2e = 1.4426950408889634
    nt = (((1,), (1,)), ((), ()))
    tn = (((0,), (0,)), ((), ()))
    nn = (((1,), (0,)), ((), ()))
    ctx = lax.axis_index("ctx")

    for s in range(16):
        where_sm[lax.shift_right_logical(pos_ref[s * run], 8)] = s
    doc = doc_ref[...]
    starts = [jnp.sum(jnp.where(doc < d, 1.0, 0.0)).astype(jnp.int32) for d in (1, 2, 3)]
    dk_sc[...] = jnp.zeros_like(dk_sc)
    dv_sc[...] = jnp.zeros_like(dv_sc)

    def one_run(t, carry):
        base = pos_ref[(ctx * 2 + t) * run]
        mine = pl.ds(pl.multiple_of(t * run, run), run)
        first = jnp.int32(0)
        for start in starts:
            first = jnp.where(start <= base, jnp.maximum(first, start), first)
        low = lax.shift_right_logical(first, 8)
        high = lax.shift_right_logical(base, 8) + 1
        q_pos = base + (lax.broadcasted_iota(jnp.int32, (1, rows), 1) & (run - 1))
        q_low = jnp.zeros_like(q_pos)
        for start in starts:
            q_low = jnp.where(start <= q_pos, jnp.maximum(q_low, start), q_low)
        for h in range(2):
            q2_sc[h * run:(h + 1) * run, :] = q_ref[mine, h * 128:(h + 1) * 128]
            up2_sc[h * run:(h + 1) * run, :] = up_ref[mine, h * 128:(h + 1) * 128]

        def keys_at(j):
            return pl.ds(pl.multiple_of(where_sm[j] * run, run), run)

        def scan_scores(j, peak):
            at = keys_at(j)
            score = lax.dot_general(k_ref[at, :], q2_sc[...], nt, preferred_element_type=f32)
            k_pos = j * run + lax.broadcasted_iota(jnp.int32, (run, 1), 0)
            score = jnp.where((k_pos >= q_low) & (k_pos <= q_pos), score, -1e30)
            score_sc[j - low] = score
            grad_sc[j - low] = lax.dot_general(v_ref[at, :], up2_sc[...], nt, preferred_element_type=f32)
            return jnp.maximum(peak, jnp.max(score, axis=0, keepdims=True))

        peak = lax.fori_loop(low, high, scan_scores, jnp.full((1, rows), -1e30, f32))

        def scan_sums(j, sums):
            total, delta = sums
            exponent = jnp.exp2((score_sc[j - low] - peak) * (scaling * log2e))
            score_sc[j - low] = exponent
            total = total + jnp.sum(exponent, axis=0, keepdims=True)
            delta = delta + jnp.sum(exponent * grad_sc[j - low], axis=0, keepdims=True)
            return total, delta

        zero = jnp.zeros((1, rows), f32)
        total, delta = lax.fori_loop(low, high, scan_sums, (zero, zero))
        inverse = 1.0 / total
        delta = delta * inverse
        dq_sc[...] = jnp.zeros_like(dq_sc)

        def scan_grads(j, c):
            at = keys_at(j)
            probs = score_sc[j - low] * inverse
            score_grad = (probs * (grad_sc[j - low] - delta)).astype(bf16)
            dv_sc[at, :] += lax.dot_general(probs.astype(bf16), up2_sc[...], nn, preferred_element_type=f32)
            dk_sc[at, :] += lax.dot_general(score_grad, q2_sc[...], nn, preferred_element_type=f32)
            dq_sc[...] += lax.dot_general(k_ref[at, :], score_grad, tn, preferred_element_type=f32)
            return c

        lax.fori_loop(low, high, scan_grads, 0)
        cosine, sine = cos_ref[mine, :], sin_ref[mine, :]
        for h in range(2):
            grad = dq_sc[:, h * run:(h + 1) * run].T * scaling
            back = grad * cosine - pltpu.roll(grad, 64, 1) * sine
            qb_ref[mine, h * 128:(h + 1) * 128] = back.astype(bf16)
        return carry

    lax.fori_loop(0, 2, one_run, 0)

    def put_out(i, carry):
        at = pl.ds(pl.multiple_of(i * run, run), run)
        dkv_ref[0, at, :] = (dk_sc[at, :] * scaling).astype(bf16)
        dkv_ref[1, at, :] = dv_sc[at, :].astype(bf16)
        return carry

    lax.fori_loop(0, 16, put_out, 0)


def attend(positions, documents, query, upstream, keys, values, cosine, sine):
    f32 = jnp.float32
    vmem = pl.BlockSpec(memory_space=pltpu.VMEM)
    return pl.pallas_call(
        attend_kernel,
        out_shape=(
            jax.ShapeDtypeStruct((512, 256), jnp.bfloat16),
            jax.ShapeDtypeStruct((2, 4096, 128), jnp.bfloat16),
        ),
        in_specs=[pl.BlockSpec(memory_space=pltpu.SMEM)] + [vmem] * 7,
        out_specs=(vmem, vmem),
        scratch_shapes=[
            pltpu.VMEM((16, 256, 512), f32),
            pltpu.VMEM((16, 256, 512), f32),
            pltpu.VMEM((512, 128), jnp.bfloat16),
            pltpu.VMEM((512, 128), jnp.bfloat16),
            pltpu.VMEM((128, 512), f32),
            pltpu.VMEM((4096, 128), f32),
            pltpu.VMEM((4096, 128), f32),
            pltpu.SMEM((16,), jnp.int32),
        ],
        compiler_params=pltpu.CompilerParams(vmem_limit_bytes=50 * 1024 * 1024),
        name="attend",
    )(positions, documents.reshape(32, 128), query, upstream, keys, values, cosine, sine)


def shards(tokens, upstream, w_query, w_keyval, positions, documents):
    f32 = jnp.float32
    ctx_rank = lax.axis_index("ctx")
    tp_rank = lax.axis_index("tp")
    tensor_split_count = lax.axis_size("tp")
    gathered = lax.all_gather(tokens, "tp", axis=0, tiled=True)
    tok_rows = gathered.shape[0]
    query_cols = w_query.shape[1]
    head_count = query_cols // HEAD_DIMENSION
    pairing_flags = (tensor_split_count // KEY_VALUE_HEADS).bit_length() - 1
    cosine_all, sine_all = rotation_tables(positions)
    row_offset = ctx_rank * tok_rows
    my_cos = lax.dynamic_slice_in_dim(cosine_all, row_offset, tok_rows, 0)
    my_sin = lax.dynamic_slice_in_dim(sine_all, row_offset, tok_rows, 0)
    query_full, keyval_full = side_by_side((w_query, w_keyval), "ctx", 0, 1)
    query_raw = jnp.dot(gathered, query_full, preferred_element_type=f32)
    keyval_raw = jnp.dot(gathered, keyval_full, preferred_element_type=f32)
    query_rot = rotate(
        query_raw.reshape(tok_rows, head_count, HEAD_DIMENSION), my_cos, my_sin
    ).astype(jnp.bfloat16)
    head_kv = keyval_raw.astype(jnp.bfloat16)
    bit_index = 0
    partner = partner_2(head_kv, "tp", bit_index)
    is_lower = tp_rank // (1 << bit_index) % 2 == 0
    head_kv = jnp.where(
        is_lower,
        jnp.concatenate([head_kv, partner], axis=1),
        jnp.concatenate([partner, head_kv], axis=1),
    )
    key_rot = rotate(head_kv[:, None, :HEAD_DIMENSION].astype(f32), my_cos, my_sin)[:, 0].astype(
        jnp.bfloat16
    )
    local_kv = jnp.concatenate([key_rot, head_kv[:, HEAD_DIMENSION:]], axis=1)
    key_value = gathered_copies(local_kv, "ctx", 0)
    sign = jnp.where(jnp.arange(HEAD_DIMENSION) < HEAD_DIMENSION // 2, -1.0, 1.0)
    query_back, key_grads = attend(
        positions,
        documents,
        query_rot.reshape(tok_rows, query_cols),
        upstream,
        key_value[:, :HEAD_DIMENSION],
        key_value[:, HEAD_DIMENSION:],
        my_cos,
        my_sin * sign,
    )
    key_backward = rotate_back(key_grads[0].astype(f32)[:, None, :], cosine_all, sine_all)[:, 0]
    key_terms = jnp.concatenate([key_backward, key_grads[1].astype(f32)], axis=1)
    head_grad = summed_on_arrival(key_terms.astype(jnp.bfloat16), "ctx", 0)
    for bit_index in reversed(range(pairing_flags)):
        half_width = head_grad.shape[1] // 2
        lower_half = head_grad[:, :half_width]
        upper_half = head_grad[:, half_width:]
        is_lower = tp_rank // (1 << bit_index) % 2 == 0
        retained = jnp.where(is_lower, lower_half, upper_half)
        outgoing = jnp.where(is_lower, upper_half, lower_half)
        head_grad = retained + partner_2(outgoing.astype(jnp.bfloat16), "tp", bit_index).astype(
            outgoing.dtype
        )
    key_value_backward = head_grad.astype(jnp.bfloat16)
    row_grads = jnp.concatenate([query_back, key_value_backward], axis=1)
    part_query = lax.dot_general(
        row_grads[:, :query_cols], query_full, (((1,), (1,)), ((), ())), preferred_element_type=f32
    )
    part_keyval = lax.dot_general(
        row_grads[:, query_cols:], keyval_full, (((1,), (1,)), ((), ())), preferred_element_type=f32
    )
    token_grad = lax.psum_scatter(
        (part_query + part_keyval).astype(jnp.bfloat16), "tp", scatter_dimension=0, tiled=True
    )
    weight_grad = summed_on_arrival(
        lax.dot_general(
            gathered, row_grads, (((0,), (0,)), ((), ())), preferred_element_type=f32
        ).astype(jnp.bfloat16),
        "ctx",
        0,
    )
    return (token_grad, weight_grad[:, :query_cols], weight_grad[:, query_cols:])


def solution(mesh):
    return jax.shard_map(
        shards,
        mesh=mesh,
        in_specs=(P(("ctx", "tp"), None), P("ctx", "tp"), P("ctx", "tp"), P("ctx", "tp"), P(), P()),
        out_specs=(P(("ctx", "tp"), None), P("ctx", "tp"), P("ctx", "tp")),
        check_vma=False,
    )
```

```python
import jax
import jax.numpy as jnp
from jax import lax
from jax.experimental import pallas as pl
from jax.experimental.pallas import tpu as pltpu
from jax.sharding import PartitionSpec as P

HEAD_DIMENSION = 128


rope_base = 500000.0


def rotation_tables(positions):
    half_width = HEAD_DIMENSION // 2
    frequency = rope_base ** (-(jnp.arange(half_width, dtype=jnp.float32) * 2.0 / HEAD_DIMENSION))
    angles = positions.astype(jnp.float32)[:, None] * frequency[None, :]
    cosine = jnp.concatenate([jnp.cos(angles), jnp.cos(angles)], axis=1)
    sine = jnp.concatenate([jnp.sin(angles), jnp.sin(angles)], axis=1)
    return (cosine, sine)


def attend_kernel(pos_ref, doc_ref, q_ref, up_ref, kv_ref, cos_ref, sin_ref, qb_ref, dkv_ref,
                  score_sc, grad_sc, q2_sc, up2_sc, dq_sc, dk_sc, dv_sc, where_sm):
    f32 = jnp.float32
    bf16 = jnp.bfloat16
    run = 256
    rows = 2 * run
    scaling = HEAD_DIMENSION ** (-0.5)
    log2e = 1.4426950408889634
    nt = (((1,), (1,)), ((), ()))
    tn = (((0,), (0,)), ((), ()))
    nn = (((1,), (0,)), ((), ()))
    ctx = lax.axis_index("ctx")

    for s in range(16):
        where_sm[lax.shift_right_logical(pos_ref[s * run], 8)] = s
    doc = doc_ref[...]
    starts = [jnp.sum(jnp.where(doc < d, 1.0, 0.0)).astype(jnp.int32) for d in (1, 2, 3)]
    dk_sc[...] = jnp.zeros_like(dk_sc)
    dv_sc[...] = jnp.zeros_like(dv_sc)

    def one_run(t, carry):
        base = pos_ref[(ctx * 2 + t) * run]
        mine = pl.ds(pl.multiple_of(t * run, run), run)
        first = jnp.int32(0)
        for start in starts:
            first = jnp.where(start <= base, jnp.maximum(first, start), first)
        low = lax.shift_right_logical(first, 8)
        high = lax.shift_right_logical(base, 8) + 1
        q_pos = base + (lax.broadcasted_iota(jnp.int32, (1, rows), 1) & (run - 1))
        q_low = jnp.zeros_like(q_pos)
        for start in starts:
            q_low = jnp.where(start <= q_pos, jnp.maximum(q_low, start), q_low)
        for h in range(2):
            q2_sc[h * run:(h + 1) * run, :] = q_ref[mine, h * 128:(h + 1) * 128]
            up2_sc[h * run:(h + 1) * run, :] = up_ref[mine, h * 128:(h + 1) * 128]

        def keys_at(j):
            return pl.ds(pl.multiple_of(where_sm[j] * run, run), run)

        def scan_scores(j, peak):
            at = keys_at(j)
            score = lax.dot_general(kv_ref[0, at, :], q2_sc[...], nt, preferred_element_type=f32)
            k_pos = j * run + lax.broadcasted_iota(jnp.int32, (run, 1), 0)
            score = jnp.where((k_pos >= q_low) & (k_pos <= q_pos), score, -1e30)
            score_sc[j - low] = score
            grad_sc[j - low] = lax.dot_general(kv_ref[1, at, :], up2_sc[...], nt, preferred_element_type=f32)
            return jnp.maximum(peak, jnp.max(score, axis=0, keepdims=True))

        peak = lax.fori_loop(low, high, scan_scores, jnp.full((1, rows), -1e30, f32))

        def scan_sums(j, sums):
            total, delta = sums
            exponent = jnp.exp2((score_sc[j - low] - peak) * (scaling * log2e))
            score_sc[j - low] = exponent
            total = total + jnp.sum(exponent, axis=0, keepdims=True)
            delta = delta + jnp.sum(exponent * grad_sc[j - low], axis=0, keepdims=True)
            return total, delta

        zero = jnp.zeros((1, rows), f32)
        total, delta = lax.fori_loop(low, high, scan_sums, (zero, zero))
        inverse = 1.0 / total
        delta = delta * inverse
        dq_sc[...] = jnp.zeros_like(dq_sc)

        def scan_grads(j, c):
            at = keys_at(j)
            probs = score_sc[j - low] * inverse
            score_grad = (probs * (grad_sc[j - low] - delta)).astype(bf16)
            dv_sc[at, :] += lax.dot_general(probs.astype(bf16), up2_sc[...], nn, preferred_element_type=f32)
            dk_sc[at, :] += lax.dot_general(score_grad, q2_sc[...], nn, preferred_element_type=f32)
            dq_sc[...] += lax.dot_general(kv_ref[0, at, :], score_grad, tn, preferred_element_type=f32)
            return c

        lax.fori_loop(low, high, scan_grads, 0)
        cosine, sine = cos_ref[mine, :], sin_ref[mine, :]
        for h in range(2):
            grad = dq_sc[:, h * run:(h + 1) * run].T * scaling
            back = grad * cosine - pltpu.roll(grad, 64, 1) * sine
            qb_ref[mine, h * 128:(h + 1) * 128] = back.astype(bf16)
        return carry

    lax.fori_loop(0, 2, one_run, 0)

    def put_out(i, carry):
        at = pl.ds(pl.multiple_of(i * run, run), run)
        dkv_ref[0, at, :] = (dk_sc[at, :] * scaling).astype(bf16)
        dkv_ref[1, at, :] = dv_sc[at, :].astype(bf16)
        return carry

    lax.fori_loop(0, 16, put_out, 0)


def attend(positions, documents, query, upstream, key_value, cosine, sine):
    f32 = jnp.float32
    vmem = pl.BlockSpec(memory_space=pltpu.VMEM)
    return pl.pallas_call(
        attend_kernel,
        out_shape=(
            jax.ShapeDtypeStruct((512, 256), jnp.bfloat16),
            jax.ShapeDtypeStruct((2, 4096, 128), jnp.bfloat16),
        ),
        in_specs=[pl.BlockSpec(memory_space=pltpu.SMEM)] + [vmem] * 6,
        out_specs=(vmem, vmem),
        scratch_shapes=[
            pltpu.VMEM((16, 256, 512), f32),
            pltpu.VMEM((16, 256, 512), f32),
            pltpu.VMEM((512, 128), jnp.bfloat16),
            pltpu.VMEM((512, 128), jnp.bfloat16),
            pltpu.VMEM((128, 512), f32),
            pltpu.VMEM((4096, 128), f32),
            pltpu.VMEM((4096, 128), f32),
            pltpu.SMEM((16,), jnp.int32),
        ],
        compiler_params=pltpu.CompilerParams(vmem_limit_bytes=50 * 1024 * 1024),
        name="attend",
    )(positions, documents.reshape(32, 128), query, upstream, key_value.reshape(2, 4096, 128), cosine, sine)


MESH = pl.DeviceIdType.MESH
VMEM_LIMIT = 60 * 1024 * 1024


def places():
    ctx = lax.axis_index("ctx")
    tp = lax.axis_index("tp")
    y, x_lo = ctx // 2, lax.rem(ctx, 2)
    x_hi, z, core = tp // 8, lax.rem(tp // 2, 4), lax.rem(tp, 2)

    def ctx_at(pair, step):
        return lax.rem(y + step + 4, 4) * 2 + (1 - x_lo if pair else x_lo)

    def tp_at(pair, step, other=0):
        side = 1 - x_hi if pair else x_hi
        return side * 8 + lax.rem(z + step + 4, 4) * 2 + (1 - core if other else core)

    ctx_peers = [(ctx_at(1, 0), tp), (ctx_at(0, 1), tp), (ctx_at(0, -1), tp)]
    tp_peers = [(ctx, tp_at(1, 0)), (ctx, tp_at(0, 1)), (ctx, tp_at(0, -1))]
    twin = (ctx, tp_at(0, 0, 1))
    return ctx, tp, core, ctx_at, tp_at, ctx_peers, tp_peers, twin


def meet(peers):
    barrier = pltpu.get_barrier_semaphore()
    for peer in peers:
        pl.semaphore_signal(barrier, inc=1, device_id=peer, device_id_type=MESH)
    pl.semaphore_wait(barrier, len(peers))


def remote(src, dst, send, recv, n, peer):
    return pltpu.make_async_remote_copy(
        src_ref=src, dst_ref=dst, send_sem=send.at[n], recv_sem=recv.at[n],
        device_id=peer, device_id_type=MESH,
    )


class Gather:
    def __init__(self, block, rows, peers, send, recv):
        half = rows // 2

        def part(pair, step, h):
            return block(pair, step).at[pl.ds(h * half, half)]

        pair, after, before = peers
        self.out = [
            (block(0, 0), pair), (block(0, 0), after), (block(0, 0), before),
            (block(1, 0), after), (block(1, 0), before),
            (part(0, -1, 0), after), (part(0, 1, 1), before),
            (part(1, -1, 0), after), (part(1, 1, 1), before),
        ]
        self.into = [
            block(1, 0), block(0, -1), block(0, 1), block(1, -1), block(1, 1),
            part(0, 2, 0), part(0, 2, 1), part(1, 2, 0), part(1, 2, 1),
        ]
        self.sems = (send, recv)

    def start(self, *which):
        for n in which:
            ref, peer = self.out[n]
            remote(ref, ref, *self.sems, n, peer).start()

    def arrived(self, *which):
        for n in which:
            ref = self.into[n]
            remote(ref, ref, *self.sems, n, self.out[n][1]).wait_recv()

    def finish(self):
        for n, (ref, peer) in enumerate(self.out):
            remote(ref, ref, *self.sems, n, peer).wait_send()


class Share:
    order = [(0, 0), (1, 0), (0, -1), (0, 1), (1, -1), (1, 1), (0, 2), (1, 2)]

    def __init__(self, mine, theirs, twin, send, recv):
        self.mine = [mine(*p) for p in self.order]
        self.theirs = [theirs(*p) for p in self.order]
        self.twin = twin
        self.sems = (send, recv)

    def start(self, *which):
        for n in which:
            remote(self.mine[n], self.mine[n], *self.sems, n, self.twin).start()

    def arrived(self):
        for n, ref in enumerate(self.theirs):
            remote(ref, ref, *self.sems, n, self.twin).wait_recv()

    def finish(self):
        for n, ref in enumerate(self.mine):
            remote(ref, ref, *self.sems, n, self.twin).wait_send()


class Reduce:
    def __init__(self, block, rows, peers, halves, wholes, last, send, recv):
        half = rows // 2
        pair, after, before = peers

        def part(p, step, h):
            return block(p, step).at[pl.ds(h * half, half)]

        self.block = block
        self.part = part
        self.halves, self.wholes, self.last = halves, wholes, last
        self.out = [
            (part(1, 2, 0), halves.at[0], after), (part(1, 2, 1), halves.at[1], before),
            (part(0, 2, 0), halves.at[2], after), (part(0, 2, 1), halves.at[3], before),
            (block(1, 1), wholes.at[0], after), (block(1, -1), wholes.at[1], before),
            (block(0, 1), wholes.at[2], after), (block(0, -1), wholes.at[3], before),
            (block(1, 0), last, pair),
        ]
        self.sems = (send, recv)

    def start(self, *which):
        for n in which:
            src, dst, peer = self.out[n]
            remote(src, dst, *self.sems, n, peer).start()

    def arrived(self, *which):
        for n in which:
            src, dst, peer = self.out[n]
            remote(src, dst, *self.sems, n, peer).wait_recv()

    def finish(self):
        for n in range(9):
            src, dst, peer = self.out[n]
            remote(src, dst, *self.sems, n, peer).wait_send()

    def second(self, p):
        n = 0 if p else 2
        for k, (step, h) in enumerate(((1, 0), (-1, 1))):
            self.arrived(n + k)
            add_into(self.part(p, step, h), self.halves.at[n + k])
            self.start(4 + n + k)

    def third(self):
        self.arrived(4, 5)
        add_into(self.block(1, 0), self.wholes.at[0], self.wholes.at[1])
        self.start(8)

    def total(self, at):
        f32 = jnp.float32
        parts = [self.block(0, 0), self.wholes.at[2], self.wholes.at[3], self.last]
        return sum(r[at].astype(f32) for r in parts)


def add_into(dst, *terms):
    rows, cols = dst.shape
    tile = max(16, min(rows, 32768 // cols))

    def one(i, carry):
        at = pl.ds(pl.multiple_of(i * tile, tile), tile)
        total = dst[at, :].astype(jnp.float32)
        for t in terms:
            total = total + t[at, :].astype(jnp.float32)
        dst[at, :] = total.astype(dst.dtype)
        return carry

    lax.fori_loop(0, rows // tile, one, 0)


def chosen(t, values):
    at = values[0]
    for n, v in enumerate(values[1:]):
        at = jnp.where(t == n + 1, v, at)
    return at


def project_kernel(tok_ref, wq_ref, wk_ref, cos_ref, sin_ref, q_ref, kv_ref, tok_out, w_out,
                   tbuf, wbuf, kvbuf, acc, t_send, t_recv, c_send, c_recv, w_send, w_recv,
                   k_send, k_recv, f_send, f_recv, local):
    f32 = jnp.float32
    bf16 = jnp.bfloat16
    ctx, tp, core, ctx_at, tp_at, ctx_peers, tp_peers, twin = places()
    copies = [
        pltpu.make_async_copy(tok_ref, tbuf.at[tp], local.at[0]),
        pltpu.make_async_copy(wq_ref, wbuf.at[ctx, :, pl.ds(0, 256)], local.at[1]),
        pltpu.make_async_copy(wk_ref, wbuf.at[ctx, :, pl.ds(256, 128)], local.at[2]),
    ]
    for c in copies:
        c.start()
    meet(ctx_peers + tp_peers + [twin])
    toks = Gather(lambda p, d: tbuf.at[tp_at(p, d)], 32, tp_peers, t_send, t_recv)
    tshare = Share(lambda p, d: tbuf.at[tp_at(p, d)], lambda p, d: tbuf.at[tp_at(p, d, 1)], twin, c_send, c_recv)
    weights = Gather(lambda p, d: wbuf.at[ctx_at(p, d)], 512, ctx_peers, w_send, w_recv)
    copies[0].wait()
    toks.start(0, 1, 2)
    copies[1].wait()
    copies[2].wait()
    weights.start(0, 1, 2)
    tshare.start(0)

    toks.arrived(1, 2)
    toks.start(5, 6)
    tshare.start(2, 3)
    toks.arrived(0)
    toks.start(3, 4)
    tshare.start(1)
    weights.arrived(0)
    weights.start(3, 4)
    weights.arrived(1, 2)
    weights.start(5, 6)
    toks.arrived(5, 6)
    tshare.start(6)
    toks.arrived(3, 4)
    toks.start(7, 8)
    tshare.start(4, 5)
    toks.arrived(7, 8)
    tshare.start(7)
    weights.arrived(3, 4)
    weights.start(7, 8)
    tshare.arrived()
    out_tok = pltpu.make_async_copy(tbuf, tok_out, local.at[3])
    out_tok.start()

    def multiply(blocks, first):
        def one(i, carry):
            c = chosen(i // 2, blocks)
            m = lax.rem(i, 2)
            cols = pl.ds(pl.multiple_of(c * 512, 512), 512)
            left = tbuf[pl.ds(m * 8, 8), :, cols].reshape(256, 512)
            rows = pl.ds(pl.multiple_of(m * 256, 256), 256)
            acc[rows, :] += jnp.dot(left, wbuf[c], preferred_element_type=f32)
            return carry

        lax.fori_loop(0, 2 * len(blocks), one, 0)

    acc[...] = jnp.zeros_like(acc)
    multiply([ctx_at(0, 0), ctx_at(1, 0), ctx_at(0, -1), ctx_at(0, 1), ctx_at(1, -1), ctx_at(1, 1)], True)
    weights.arrived(5, 6)
    weights.arrived(7, 8)
    out_w = pltpu.make_async_copy(wbuf, w_out, local.at[4])
    out_w.start()
    multiply([ctx_at(0, 2), ctx_at(1, 2)], False)

    cosine, sine = cos_ref[...], sin_ref[...]
    held = acc[:, 256:384].astype(bf16).astype(f32)
    turned = held * cosine + pltpu.roll(held, 64, 1) * sine
    kvbuf[core, ctx] = jnp.where(core == 0, turned, held).astype(bf16)
    keys = Gather(lambda p, d: kvbuf.at[core, ctx_at(p, d)], 512, ctx_peers, k_send, k_recv)
    kshare = Share(lambda p, d: kvbuf.at[core, ctx_at(p, d)], lambda p, d: kvbuf.at[1 - core, ctx_at(p, d)], twin, f_send, f_recv)
    keys.start(0, 1, 2)
    kshare.start(0)
    for h in range(2):
        raw = acc[:, h * 128:(h + 1) * 128]
        q_ref[:, h * 128:(h + 1) * 128] = (raw * cosine + pltpu.roll(raw, 64, 1) * sine).astype(bf16)
    keys.arrived(0)
    keys.start(3, 4)
    kshare.start(1)
    keys.arrived(1, 2)
    keys.start(5, 6)
    kshare.start(2, 3)
    keys.arrived(3, 4)
    keys.start(7, 8)
    kshare.start(4, 5)
    keys.arrived(5, 6)
    kshare.start(6)
    keys.arrived(7, 8)
    kshare.start(7)
    kshare.arrived()
    out_kv = pltpu.make_async_copy(kvbuf, kv_ref, local.at[5])
    out_kv.start()
    toks.finish()
    tshare.finish()
    weights.finish()
    keys.finish()
    kshare.finish()
    out_tok.wait()
    out_w.wait()
    out_kv.wait()


def project(tokens, w_query, w_keyval, cosine, sine):
    bf16 = jnp.bfloat16
    vmem = pl.BlockSpec(memory_space=pltpu.VMEM)
    hbm = pl.BlockSpec(memory_space=pl.ANY)
    dma = pltpu.SemaphoreType.DMA
    return pl.pallas_call(
        project_kernel,
        out_shape=(
            jax.ShapeDtypeStruct((512, 256), bf16),
            jax.ShapeDtypeStruct((2, 8, 512, 128), bf16),
            jax.ShapeDtypeStruct((16, 32, 4096), bf16),
            jax.ShapeDtypeStruct((8, 512, 384), bf16),
        ),
        in_specs=[hbm, hbm, hbm, vmem, vmem],
        out_specs=(vmem, hbm, hbm, hbm),
        scratch_shapes=[
            pltpu.VMEM((16, 32, 4096), bf16),
            pltpu.VMEM((8, 512, 384), bf16),
            pltpu.VMEM((2, 8, 512, 128), bf16),
            pltpu.VMEM((512, 384), jnp.float32),
            dma((9,)), dma((9,)), dma((8,)), dma((8,)), dma((9,)), dma((9,)),
            dma((9,)), dma((9,)), dma((8,)), dma((8,)), dma((6,)),
        ],
        compiler_params=pltpu.CompilerParams(collective_id=0, has_side_effects=True, vmem_limit_bytes=VMEM_LIMIT),
        name="project",
    )(tokens, w_query, w_keyval, cosine, sine)


def reduce_kernel(tok_ref, w_ref, qb_ref, dkv_ref, cos_ref, sin_ref, tg_ref, gq_ref, gk_ref,
                  tbuf, wbuf, kv, kv_in, kv_halves, kv_wholes, kv_last, turned_q, kvg,
                  wg, wg_halves, wg_wholes, wg_last, px, pb, pb_in, tg_halves, tg_wholes, tg_last,
                  k_send, k_recv, w_send, w_recv, t_send, t_recv, e_send, e_recv, local):
    f32 = jnp.float32
    bf16 = jnp.bfloat16
    nt = (((1,), (1,)), ((), ()))
    ctx, tp, core, ctx_at, tp_at, ctx_peers, tp_peers, twin = places()
    copies = [
        pltpu.make_async_copy(dkv_ref.at[core], kv, local.at[0]),
        pltpu.make_async_copy(tok_ref, tbuf, local.at[1]),
        pltpu.make_async_copy(w_ref, wbuf, local.at[2]),
    ]
    for c in copies:
        c.start()
    meet(ctx_peers + tp_peers + [twin])
    swap = remote(dkv_ref.at[1 - core], kv_in, e_send, e_recv, 4, twin)
    swap.start()
    turned_q[...] = qb_ref[...].T
    copies[1].wait()

    def tok_cols(c):
        return tbuf[:, :, pl.ds(pl.multiple_of(c * 512, 512), 512)].reshape(512, 512)

    def query_terms(c, carry):
        wg[c, 0:256, :] = jnp.dot(turned_q[...], tok_cols(c), preferred_element_type=f32).astype(bf16)
        return carry

    keys = Reduce(lambda p, d: kv.at[ctx_at(p, d)], 512, ctx_peers, kv_halves, kv_wholes, kv_last, k_send, k_recv)
    copies[0].wait()
    swap.wait_recv()
    for d in (2, 1, -1, 0):
        for p in (1, 0):
            add_into(kv.at[ctx_at(p, d)], kv_in.at[ctx_at(p, d)])
        if d == 2:
            keys.start(0, 1, 2, 3)
    lax.fori_loop(0, 8, query_terms, 0)
    keys.second(1)
    keys.second(0)
    copies[2].wait()

    def query_part(c, carry):
        px[c] = lax.dot_general(qb_ref[...], wbuf[c, :, 0:256], nt, preferred_element_type=f32)
        return carry

    lax.fori_loop(0, 4, query_part, 0)
    keys.third()
    lax.fori_loop(4, 8, query_part, 0)
    keys.arrived(6, 7, 8)
    total = keys.total(...)
    back = total * cos_ref[...] - pltpu.roll(total, 64, 1) * sin_ref[...]
    total = jnp.where(core == 0, back, total)
    kvg[...] = total.astype(bf16)
    turned_q[0:128, :] = total.T.astype(bf16)

    order = [ctx_at(p, d) for d in (2, 1, -1, 0) for p in (1, 0)]

    def keyval_terms(i, carry):
        c = chosen(i, order)
        wg[c, 256:384, :] = jnp.dot(turned_q[0:128, :], tok_cols(c), preferred_element_type=f32).astype(bf16)
        return carry

    weights = Reduce(lambda p, d: wg.at[ctx_at(p, d)], 384, ctx_peers, wg_halves, wg_wholes, wg_last, w_send, w_recv)
    lax.fori_loop(0, 2, keyval_terms, 0)
    weights.start(0, 1, 2, 3)

    def keyval_part(c, carry):
        part = px[c] + lax.dot_general(kvg[...], wbuf[c, :, 256:384], nt, preferred_element_type=f32)
        part = part.astype(bf16).reshape(2, 4, 2, 32, 512)
        cols = pl.ds(pl.multiple_of(c * 512, 512), 512)
        for side in range(2):
            for level in range(4):
                for k in range(2):
                    pb[k, level, side, :, cols] = part[side, level, k]
        return carry

    lax.fori_loop(0, 8, keyval_part, 0)

    def level(d):
        return tp_at(0, d) // 2 - 4 * (tp // 8)

    steps = (2, 1, -1, 0)
    swaps = [
        remote(pb.at[1 - core, level(d)], pb_in.at[level(d)], e_send, e_recv, n, twin)
        for n, d in enumerate(steps)
    ]
    for s in swaps:
        s.start()
    lax.fori_loop(2, 8, keyval_terms, 0)
    side = tp // 8

    def tg_block(p, d):
        return pb.at[core, level(d), 1 - side if p else side]

    def merged(n):
        swaps[n].wait_recv()
        for p in (1, 0):
            add_into(tg_block(p, steps[n]), pb_in.at[level(steps[n]), 1 - side if p else side])

    toks = Reduce(tg_block, 32, tp_peers, tg_halves, tg_wholes, tg_last, t_send, t_recv)
    merged(0)
    toks.start(0, 1, 2, 3)
    merged(1)
    merged(2)
    merged(3)
    toks.second(1)
    weights.second(1)
    toks.second(0)
    weights.second(0)
    toks.third()
    weights.third()
    toks.arrived(6, 7, 8)
    tg_ref[...] = toks.total(...).astype(bf16)
    weights.arrived(6, 7, 8)
    for n in range(3):
        rows = slice(n * 128, (n + 1) * 128)
        turned = weights.total((rows, slice(None))).T
        if n < 2:
            gq_ref[:, n * 128:(n + 1) * 128] = turned
        else:
            gk_ref[...] = turned
    swap.wait_send()
    for s in swaps:
        s.wait_send()
    keys.finish()
    weights.finish()
    toks.finish()


def reduce(tok_full, w_full, query_back, dkv, cosine, sine):
    bf16 = jnp.bfloat16
    f32 = jnp.float32
    vmem = pl.BlockSpec(memory_space=pltpu.VMEM)
    hbm = pl.BlockSpec(memory_space=pl.ANY)
    dma = pltpu.SemaphoreType.DMA
    return pl.pallas_call(
        reduce_kernel,
        out_shape=(
            jax.ShapeDtypeStruct((32, 4096), bf16),
            jax.ShapeDtypeStruct((512, 256), f32),
            jax.ShapeDtypeStruct((512, 128), f32),
        ),
        in_specs=[hbm, hbm, vmem, hbm, vmem, vmem],
        out_specs=(vmem, vmem, vmem),
        scratch_shapes=[
            pltpu.VMEM((16, 32, 4096), bf16),
            pltpu.VMEM((8, 512, 384), bf16),
            pltpu.VMEM((8, 512, 128), bf16),
            pltpu.VMEM((8, 512, 128), bf16),
            pltpu.VMEM((4, 256, 128), bf16),
            pltpu.VMEM((4, 512, 128), bf16),
            pltpu.VMEM((512, 128), bf16),
            pltpu.VMEM((256, 512), bf16),
            pltpu.VMEM((512, 128), bf16),
            pltpu.VMEM((8, 384, 512), bf16),
            pltpu.VMEM((4, 192, 512), bf16),
            pltpu.VMEM((4, 384, 512), bf16),
            pltpu.VMEM((384, 512), bf16),
            pltpu.VMEM((8, 512, 512), f32),
            pltpu.VMEM((2, 4, 2, 32, 4096), bf16),
            pltpu.VMEM((4, 2, 32, 4096), bf16),
            pltpu.VMEM((4, 16, 4096), bf16),
            pltpu.VMEM((4, 32, 4096), bf16),
            pltpu.VMEM((32, 4096), bf16),
            dma((9,)), dma((9,)), dma((9,)), dma((9,)), dma((9,)), dma((9,)),
            dma((5,)), dma((5,)), dma((3,)),
        ],
        compiler_params=pltpu.CompilerParams(collective_id=1, has_side_effects=True, vmem_limit_bytes=VMEM_LIMIT),
        name="reduce",
    )(tok_full, w_full, query_back, dkv, cosine, sine)


def shards(tokens, upstream, w_query, w_keyval, positions, documents):
    ctx = lax.axis_index("ctx")
    my_pos = lax.dynamic_slice_in_dim(positions, ctx * 512, 512, 0)
    cosine, sine = rotation_tables(my_pos)
    sign = jnp.where(jnp.arange(HEAD_DIMENSION) < HEAD_DIMENSION // 2, -1.0, 1.0)
    sine = sine * sign
    query, key_value, tok_full, w_full = project(tokens, w_query, w_keyval, cosine, sine)
    query_back, dkv = attend(positions, documents, query, upstream, key_value, cosine, sine)
    return reduce(tok_full, w_full, query_back, dkv.reshape(2, 8, 512, 128), cosine, sine)


def solution(mesh):
    return jax.shard_map(
        shards,
        mesh=mesh,
        in_specs=(P(("ctx", "tp"), None), P("ctx", "tp"), P("ctx", "tp"), P("ctx", "tp"), P(), P()),
        out_specs=(P(("ctx", "tp"), None), P("ctx", "tp"), P("ctx", "tp")),
        check_vma=False,
    )
```

```python
import jax
import jax.numpy as jnp
from jax import lax
from jax.experimental import pallas as pl
from jax.experimental.pallas import tpu as pltpu
from jax.sharding import PartitionSpec as P

HEAD_DIMENSION = 128


rope_base = 500000.0


def attend_kernel(pos_ref, doc_ref, q_ref, up_ref, kv_ref, cos_ref, sin_ref, qb_ref, dkv_ref,
                  score_sc, grad_sc, q2_sc, up2_sc, dq_sc, dk_sc, dv_sc, where_sm):
    f32 = jnp.float32
    bf16 = jnp.bfloat16
    run = 256
    rows = 2 * run
    scaling = HEAD_DIMENSION ** (-0.5)
    log2e = 1.4426950408889634
    nt = (((1,), (1,)), ((), ()))
    tn = (((0,), (0,)), ((), ()))
    nn = (((1,), (0,)), ((), ()))
    ctx = lax.axis_index("ctx")

    for s in range(16):
        where_sm[lax.shift_right_logical(pos_ref[s * run], 8)] = s
    doc = doc_ref[...]
    starts = [jnp.sum(jnp.where(doc < d, 1.0, 0.0)).astype(jnp.int32) for d in (1, 2, 3)]
    dk_sc[...] = jnp.zeros_like(dk_sc)
    dv_sc[...] = jnp.zeros_like(dv_sc)

    def one_run(t, carry):
        base = pos_ref[(ctx * 2 + t) * run]
        mine = pl.ds(pl.multiple_of(t * run, run), run)
        first = jnp.int32(0)
        for start in starts:
            first = jnp.where(start <= base, jnp.maximum(first, start), first)
        low = lax.shift_right_logical(first, 8)
        high = lax.shift_right_logical(base, 8) + 1
        q_pos = base + (lax.broadcasted_iota(jnp.int32, (1, rows), 1) & (run - 1))
        q_low = jnp.zeros_like(q_pos)
        for start in starts:
            q_low = jnp.where(start <= q_pos, jnp.maximum(q_low, start), q_low)
        for h in range(2):
            q2_sc[h * run:(h + 1) * run, :] = q_ref[mine, h * 128:(h + 1) * 128]
            up2_sc[h * run:(h + 1) * run, :] = up_ref[mine, h * 128:(h + 1) * 128]

        def keys_at(j):
            return pl.ds(pl.multiple_of(where_sm[j] * run, run), run)

        def scan_scores(j, peak):
            at = keys_at(j)
            score = lax.dot_general(kv_ref[0, at, :], q2_sc[...], nt, preferred_element_type=f32)
            k_pos = j * run + lax.broadcasted_iota(jnp.int32, (run, 1), 0)
            score = jnp.where((k_pos >= q_low) & (k_pos <= q_pos), score, -1e30)
            score_sc[j - low] = score
            grad_sc[j - low] = lax.dot_general(kv_ref[1, at, :], up2_sc[...], nt, preferred_element_type=f32)
            return jnp.maximum(peak, jnp.max(score, axis=0, keepdims=True))

        peak = lax.fori_loop(low, high, scan_scores, jnp.full((1, rows), -1e30, f32))

        def scan_sums(j, sums):
            total, delta = sums
            exponent = jnp.exp2((score_sc[j - low] - peak) * (scaling * log2e))
            score_sc[j - low] = exponent
            total = total + jnp.sum(exponent, axis=0, keepdims=True)
            delta = delta + jnp.sum(exponent * grad_sc[j - low], axis=0, keepdims=True)
            return total, delta

        zero = jnp.zeros((1, rows), f32)
        total, delta = lax.fori_loop(low, high, scan_sums, (zero, zero))
        inverse = 1.0 / total
        delta = delta * inverse
        dq_sc[...] = jnp.zeros_like(dq_sc)

        def scan_grads(j, c):
            at = keys_at(j)
            probs = score_sc[j - low] * inverse
            score_grad = (probs * (grad_sc[j - low] - delta)).astype(bf16)
            dv_sc[at, :] += lax.dot_general(probs.astype(bf16), up2_sc[...], nn, preferred_element_type=f32)
            dk_sc[at, :] += lax.dot_general(score_grad, q2_sc[...], nn, preferred_element_type=f32)
            dq_sc[...] += lax.dot_general(kv_ref[0, at, :], score_grad, tn, preferred_element_type=f32)
            return c

        lax.fori_loop(low, high, scan_grads, 0)
        cosine, sine = cos_ref[mine, :], sin_ref[mine, :]
        for h in range(2):
            grad = dq_sc[:, h * run:(h + 1) * run].T * scaling
            back = grad * cosine - pltpu.roll(grad, 64, 1) * sine
            qb_ref[mine, h * 128:(h + 1) * 128] = back.astype(bf16)
        return carry

    lax.fori_loop(0, 2, one_run, 0)

    def put_out(i, carry):
        at = pl.ds(pl.multiple_of(i * run, run), run)
        dkv_ref[0, at, :] = (dk_sc[at, :] * scaling).astype(bf16)
        dkv_ref[1, at, :] = dv_sc[at, :].astype(bf16)
        return carry

    lax.fori_loop(0, 16, put_out, 0)


def attend(positions, documents, query, upstream, key_value, cosine, sine):
    f32 = jnp.float32
    vmem = pl.BlockSpec(memory_space=pltpu.VMEM)
    return pl.pallas_call(
        attend_kernel,
        out_shape=(
            jax.ShapeDtypeStruct((512, 256), jnp.bfloat16),
            jax.ShapeDtypeStruct((2, 4096, 128), jnp.bfloat16),
        ),
        in_specs=[pl.BlockSpec(memory_space=pltpu.SMEM)] + [vmem] * 6,
        out_specs=(vmem, vmem),
        scratch_shapes=[
            pltpu.VMEM((16, 256, 512), f32),
            pltpu.VMEM((16, 256, 512), f32),
            pltpu.VMEM((512, 128), jnp.bfloat16),
            pltpu.VMEM((512, 128), jnp.bfloat16),
            pltpu.VMEM((128, 512), f32),
            pltpu.VMEM((4096, 128), f32),
            pltpu.VMEM((4096, 128), f32),
            pltpu.SMEM((16,), jnp.int32),
        ],
        compiler_params=pltpu.CompilerParams(vmem_limit_bytes=60 * 1024 * 1024),
        name="attend",
    )(positions, documents.reshape(32, 128), query, upstream, key_value.reshape(2, 4096, 128), cosine, sine)


MESH = pl.DeviceIdType.MESH
VMEM_LIMIT = 60 * 1024 * 1024


def places():
    ctx = lax.axis_index("ctx")
    tp = lax.axis_index("tp")
    y, x_lo = ctx // 2, lax.rem(ctx, 2)
    x_hi, z, core = tp // 8, lax.rem(tp // 2, 4), lax.rem(tp, 2)

    def ctx_at(pair, step):
        return lax.rem(y + step + 4, 4) * 2 + (1 - x_lo if pair else x_lo)

    def tp_at(pair, step, other=0):
        side = 1 - x_hi if pair else x_hi
        return side * 8 + lax.rem(z + step + 4, 4) * 2 + (1 - core if other else core)

    ctx_peers = [(ctx_at(1, 0), tp), (ctx_at(0, 1), tp), (ctx_at(0, -1), tp)]
    tp_peers = [(ctx, tp_at(1, 0)), (ctx, tp_at(0, 1)), (ctx, tp_at(0, -1))]
    twin = (ctx, tp_at(0, 0, 1))
    return ctx, tp, core, ctx_at, tp_at, ctx_peers, tp_peers, twin


def meet(peers):
    barrier = pltpu.get_barrier_semaphore()
    for peer in peers:
        pl.semaphore_signal(barrier, inc=1, device_id=peer, device_id_type=MESH)
    pl.semaphore_wait(barrier, len(peers))


def remote(src, dst, send, recv, n, peer):
    return pltpu.make_async_remote_copy(
        src_ref=src, dst_ref=dst, send_sem=send.at[n], recv_sem=recv.at[n],
        device_id=peer, device_id_type=MESH,
    )


class Gather:
    def __init__(self, block, rows, peers, send, recv):
        half = rows // 2

        def part(pair, step, h):
            return block(pair, step).at[pl.ds(h * half, half)]

        pair, after, before = peers
        self.out = [
            (part(0, 0, 0), pair), (part(0, 0, 1), pair), (block(0, 0), after), (block(0, 0), before),
            (part(1, 0, 0), after), (part(1, 0, 0), before), (part(1, 0, 1), after), (part(1, 0, 1), before),
            (part(0, -1, 0), after), (part(0, 1, 1), before),
            (part(1, -1, 0), after), (part(1, 1, 1), before),
        ]
        self.into = [
            part(1, 0, 0), part(1, 0, 1), block(0, -1), block(0, 1),
            part(1, -1, 0), part(1, 1, 0), part(1, -1, 1), part(1, 1, 1),
            part(0, 2, 0), part(0, 2, 1), part(1, 2, 0), part(1, 2, 1),
        ]
        self.sems = (send, recv)

    def start(self, *which):
        for n in which:
            ref, peer = self.out[n]
            remote(ref, ref, *self.sems, n, peer).start()

    def arrived(self, *which):
        for n in which:
            ref = self.into[n]
            remote(ref, ref, *self.sems, n, self.out[n][1]).wait_recv()

    def finish(self):
        for n, (ref, peer) in enumerate(self.out):
            remote(ref, ref, *self.sems, n, peer).wait_send()


class RingGather:
    def __init__(self, block, rows, peers, send, recv):
        half = rows // 2

        def part(pair, step, h):
            return block(pair, step).at[pl.ds(h * half, half)]

        pair, after, before = peers
        self.out = [
            (block(0, 0), after), (block(0, 0), before), (part(0, -1, 0), after), (part(0, 1, 1), before),
            (block(0, 0), pair), (block(0, -1), pair), (block(0, 1), pair), (part(0, 2, 0), pair), (part(0, 2, 1), pair),
        ]
        self.into = [
            block(0, -1), block(0, 1), part(0, 2, 0), part(0, 2, 1),
            block(1, 0), block(1, -1), block(1, 1), part(1, 2, 0), part(1, 2, 1),
        ]
        self.sems = (send, recv)

    start = Gather.start
    arrived = Gather.arrived
    finish = Gather.finish


class Share:
    order = [(0, 0), (1, 0), (0, -1), (0, 1), (1, -1), (1, 1), (0, 2), (1, 2)]

    def __init__(self, mine, theirs, twin, send, recv):
        self.mine = [mine(*p) for p in self.order]
        self.theirs = [theirs(*p) for p in self.order]
        self.twin = twin
        self.sems = (send, recv)

    def start(self, *which):
        for n in which:
            remote(self.mine[n], self.mine[n], *self.sems, n, self.twin).start()

    def arrived(self):
        for n, ref in enumerate(self.theirs):
            remote(ref, ref, *self.sems, n, self.twin).wait_recv()

    def finish(self):
        for n, ref in enumerate(self.mine):
            remote(ref, ref, *self.sems, n, self.twin).wait_send()


class Reduce:
    def __init__(self, block, rows, peers, halves, wholes, last, send, recv):
        half = rows // 2
        pair, after, before = peers

        def part(p, step, h):
            return block(p, step).at[pl.ds(h * half, half)]

        self.block = block
        self.part = part
        self.halves, self.wholes, self.last = halves, wholes, last
        self.out = [
            (part(1, 2, 0), halves.at[0], after), (part(1, 2, 1), halves.at[1], before),
            (part(0, 2, 0), halves.at[2], after), (part(0, 2, 1), halves.at[3], before),
            (block(1, 1), wholes.at[0], after), (block(1, -1), wholes.at[1], before),
            (block(0, 1), wholes.at[2], after), (block(0, -1), wholes.at[3], before),
            (block(1, 0), last, pair),
        ]
        self.sems = (send, recv)

    def start(self, *which):
        for n in which:
            src, dst, peer = self.out[n]
            remote(src, dst, *self.sems, n, peer).start()

    def arrived(self, *which):
        for n in which:
            src, dst, peer = self.out[n]
            remote(src, dst, *self.sems, n, peer).wait_recv()

    def finish(self):
        for n in range(9):
            src, dst, peer = self.out[n]
            remote(src, dst, *self.sems, n, peer).wait_send()

    def second(self, p):
        n = 0 if p else 2
        for k, (step, h) in enumerate(((1, 0), (-1, 1))):
            self.arrived(n + k)
            add_into(self.part(p, step, h), self.halves.at[n + k])
            self.start(4 + n + k)

    def third(self):
        self.arrived(4, 5)
        add_into(self.block(1, 0), self.wholes.at[0], self.wholes.at[1])
        self.start(8)

    def total(self, at):
        f32 = jnp.float32
        parts = [self.block(0, 0), self.wholes.at[2], self.wholes.at[3], self.last]
        return sum(r[at].astype(f32) for r in parts)


class PairReduce:
    steps = (2, 1, -1, 0)

    def __init__(self, block, rows, peers, pairs, halves, wholes, send, recv):
        half = rows // 2
        pair, after, before = peers

        def part(p, step, h):
            return block(p, step).at[pl.ds(h * half, half)]

        self.block = block
        self.part = part
        self.pairs, self.halves, self.wholes = pairs, halves, wholes
        self.out = [(block(1, d), pairs.at[n], pair) for n, d in enumerate(self.steps)] + [
            (part(0, 2, 0), halves.at[0], after), (part(0, 2, 1), halves.at[1], before),
            (block(0, 1), wholes.at[0], after), (block(0, -1), wholes.at[1], before),
        ]
        self.sems = (send, recv)

    start = Reduce.start
    arrived = Reduce.arrived

    def finish(self):
        for n, (src, dst, peer) in enumerate(self.out):
            remote(src, dst, *self.sems, n, peer).wait_send()

    def paired(self, *which):
        for n in which:
            self.arrived(n)
            add_into(self.block(0, self.steps[n]), self.pairs.at[n])

    def second(self):
        for k, (step, h) in enumerate(((1, 0), (-1, 1))):
            self.arrived(4 + k)
            add_into(self.part(0, step, h), self.halves.at[k])
            self.start(6 + k)

    def total(self, at):
        f32 = jnp.float32
        self.arrived(3, 6, 7)
        parts = [self.block(0, 0), self.pairs.at[3], self.wholes.at[0], self.wholes.at[1]]
        return sum(r[at].astype(f32) for r in parts)


def add_into(dst, *terms):
    rows, cols = dst.shape
    tile = max(16, min(rows, 32768 // cols))

    def one(i, carry):
        at = pl.ds(pl.multiple_of(i * tile, tile), tile)
        total = dst[at, :].astype(jnp.float32)
        for t in terms:
            total = total + t[at, :].astype(jnp.float32)
        dst[at, :] = total.astype(dst.dtype)
        return carry

    lax.fori_loop(0, rows // tile, one, 0)


def chosen(t, values):
    at = values[0]
    for n, v in enumerate(values[1:]):
        at = jnp.where(t == n + 1, v, at)
    return at


def project_kernel(pos_ref, freq_ref, tok_ref, wq_ref, wk_ref, q_ref, cos_ref, sin_ref, kv_ref, tok_out, wq_out, wk_out,
                   tbuf, wqbuf, wkbuf, kvbuf, acc, acc_kv, t_send, t_recv, c_send, c_recv, wq_send, wq_recv, wk_send, wk_recv,
                   k_send, k_recv, r_send, r_recv, f_send, f_recv, local):
    f32 = jnp.float32
    bf16 = jnp.bfloat16
    ctx, tp, core, ctx_at, tp_at, ctx_peers, tp_peers, twin = places()
    copies = [
        pltpu.make_async_copy(wk_ref, wkbuf.at[ctx], local.at[0]),
        pltpu.make_async_copy(tok_ref, tbuf.at[tp], local.at[1]),
        pltpu.make_async_copy(wq_ref, wqbuf.at[ctx], local.at[2]),
    ]
    for c in copies:
        c.start()
    meet(ctx_peers + tp_peers + [twin])
    toks = Gather(lambda p, d: tbuf.at[tp_at(p, d)], 32, tp_peers, t_send, t_recv)
    tshare = Share(lambda p, d: tbuf.at[tp_at(p, d)], lambda p, d: tbuf.at[tp_at(p, d, 1)], twin, c_send, c_recv)
    wq = Gather(lambda p, d: wqbuf.at[ctx_at(p, d)], 512, ctx_peers, wq_send, wq_recv)
    wk = Gather(lambda p, d: wkbuf.at[ctx_at(p, d)], 512, ctx_peers, wk_send, wk_recv)
    for c in copies:
        c.wait()
    wk.start(0, 1)
    toks.start(0, 1)
    wk.start(2, 3)
    toks.start(2, 3)
    wq.start(2, 3, 0, 1)
    tshare.start(0)

    row = lax.broadcasted_iota(jnp.int32, (512, 128), 0)
    place = jnp.where(row < 256, pos_ref[ctx * 512], pos_ref[ctx * 512 + 256]) + (row & 255)
    angle = place.astype(f32) * freq_ref[...]
    cos_ref[...] = jnp.cos(angle)
    sine = jnp.sin(angle)
    sin_ref[...] = jnp.where(lax.broadcasted_iota(jnp.int32, (512, 128), 1) < 64, -sine, sine)
    acc[...] = jnp.zeros_like(acc)
    acc_kv[...] = jnp.zeros_like(acc_kv)

    wk.arrived(0, 1)
    wk.start(4, 5, 6, 7)
    wk.arrived(2, 3)
    wk.start(8, 9)
    toks.arrived(2, 3)
    toks.start(8, 9)
    tshare.start(2, 3)
    toks.arrived(0)
    toks.start(4, 5)
    toks.arrived(1)
    toks.start(6, 7)
    tshare.start(1)
    wq.arrived(2, 3)
    wq.start(8, 9)
    toks.arrived(8, 9)
    tshare.start(6)
    wk.arrived(4)
    wk.start(10)
    wk.arrived(7)
    wk.start(11)
    toks.arrived(4)
    toks.start(10)
    wq.arrived(0)
    wq.start(4, 5)
    toks.arrived(7)
    toks.start(11)
    toks.arrived(5, 6)
    tshare.start(4, 5)
    wq.arrived(1)
    wq.start(6, 7)
    wk.arrived(5, 6, 8, 9, 10, 11)
    out_wk = pltpu.make_async_copy(wkbuf, wk_out, local.at[3])
    out_wk.start()
    toks.arrived(10, 11)
    tshare.start(7)
    tshare.arrived()
    out_tok = pltpu.make_async_copy(tbuf, tok_out, local.at[4])
    out_tok.start()

    def multiply(total, wbuf, blocks):
        def one(i, carry):
            c = chosen(i // 2, blocks)
            m = lax.rem(i, 2)
            cols = pl.ds(pl.multiple_of(c * 512, 512), 512)
            left = tbuf[pl.ds(m * 8, 8), :, cols].reshape(256, 512)
            rows = pl.ds(pl.multiple_of(m * 256, 256), 256)
            total[rows, :] += jnp.dot(left, wbuf[c], preferred_element_type=f32)
            return carry

        lax.fori_loop(0, 2 * len(blocks), one, 0)

    multiply(acc_kv, wkbuf, list(range(8)))
    cosine, sine = cos_ref[...], sin_ref[...]
    held = acc_kv[...].astype(bf16).astype(f32)
    turned = held * cosine + pltpu.roll(held, 64, 1) * sine
    kvbuf[core, ctx] = jnp.where(core == 0, turned, held).astype(bf16)
    keys = Gather(lambda p, d: kvbuf.at[core, ctx_at(p, d), pl.ds(0, 256)], 256, ctx_peers, k_send, k_recv)
    round_keys = RingGather(lambda p, d: kvbuf.at[core, ctx_at(p, d), pl.ds(256, 256)], 256, ctx_peers, r_send, r_recv)
    kshare = Share(lambda p, d: kvbuf.at[core, ctx_at(p, d)], lambda p, d: kvbuf.at[1 - core, ctx_at(p, d)], twin, f_send, f_recv)
    keys.start(0, 1)
    round_keys.start(0, 1)
    keys.start(2, 3)
    round_keys.start(4)
    kshare.start(0)
    wq.arrived(4)
    wq.start(10)
    wq.arrived(7)
    wq.start(11)
    multiply(acc, wqbuf, [ctx_at(0, 0), ctx_at(1, 0), ctx_at(0, -1), ctx_at(0, 1)])
    round_keys.arrived(0, 1)
    round_keys.start(2, 3, 5, 6)
    keys.arrived(0, 1)
    keys.start(4, 5, 6, 7)
    keys.arrived(2, 3)
    keys.start(8, 9)
    kshare.start(2, 3)
    round_keys.arrived(4)
    kshare.start(1)
    wq.arrived(5, 6)
    multiply(acc, wqbuf, [ctx_at(1, -1), ctx_at(1, 1)])
    round_keys.arrived(2, 3)
    round_keys.start(7, 8)
    keys.arrived(4)
    keys.start(10)
    keys.arrived(7)
    keys.start(11)
    wq.arrived(8, 9, 10, 11)
    out_wq = pltpu.make_async_copy(wqbuf, wq_out, local.at[5])
    out_wq.start()
    multiply(acc, wqbuf, [ctx_at(0, 2), ctx_at(1, 2)])
    for h in range(2):
        raw = acc[:, h * 128:(h + 1) * 128]
        q_ref[:, h * 128:(h + 1) * 128] = (raw * cosine + pltpu.roll(raw, 64, 1) * sine).astype(bf16)
    keys.arrived(5, 6)
    round_keys.arrived(5, 6)
    kshare.start(4, 5)
    keys.arrived(8, 9)
    kshare.start(6)
    keys.arrived(10, 11)
    round_keys.arrived(7, 8)
    kshare.start(7)
    kshare.arrived()
    out_kv = pltpu.make_async_copy(kvbuf, kv_ref, local.at[6])
    out_kv.start()
    toks.finish()
    tshare.finish()
    wq.finish()
    wk.finish()
    keys.finish()
    round_keys.finish()
    kshare.finish()
    out_tok.wait()
    out_wq.wait()
    out_wk.wait()
    out_kv.wait()


def project(positions, frequency, tokens, w_query, w_keyval):
    bf16 = jnp.bfloat16
    f32 = jnp.float32
    vmem = pl.BlockSpec(memory_space=pltpu.VMEM)
    hbm = pl.BlockSpec(memory_space=pltpu.HBM)
    dma = pltpu.SemaphoreType.DMA
    return pl.pallas_call(
        project_kernel,
        out_shape=(
            jax.ShapeDtypeStruct((512, 256), bf16),
            jax.ShapeDtypeStruct((512, 128), f32),
            jax.ShapeDtypeStruct((512, 128), f32),
            jax.ShapeDtypeStruct((2, 8, 512, 128), bf16),
            jax.ShapeDtypeStruct((16, 32, 4096), bf16),
            jax.ShapeDtypeStruct((8, 512, 256), bf16),
            jax.ShapeDtypeStruct((8, 512, 128), bf16),
        ),
        in_specs=[pl.BlockSpec(memory_space=pltpu.SMEM), vmem, hbm, hbm, hbm],
        out_specs=(vmem, vmem, vmem, hbm, hbm, hbm, hbm),
        scratch_shapes=[
            pltpu.VMEM((16, 32, 4096), bf16),
            pltpu.VMEM((8, 512, 256), bf16),
            pltpu.VMEM((8, 512, 128), bf16),
            pltpu.VMEM((2, 8, 512, 128), bf16),
            pltpu.VMEM((512, 256), f32),
            pltpu.VMEM((512, 128), f32),
            dma((12,)), dma((12,)), dma((8,)), dma((8,)), dma((12,)), dma((12,)), dma((12,)), dma((12,)),
            dma((12,)), dma((12,)), dma((9,)), dma((9,)), dma((8,)), dma((8,)), dma((7,)),
        ],
        compiler_params=pltpu.CompilerParams(collective_id=0, has_side_effects=True, vmem_limit_bytes=VMEM_LIMIT),
        name="project",
    )(positions, frequency, tokens, w_query, w_keyval)


def reduce_kernel(tok_ref, wq_ref, wk_ref, qb_ref, dkv_ref, cos_ref, sin_ref, tg_ref, sum_ref,
                  tbuf, wqbuf, wkbuf, kv, kv_in, kv_halves, kv_wholes, kv_last, kp_pairs, kp_halves, kp_wholes, turned_q, kvg,
                  wq, wq_halves, wq_wholes, wq_last, wp_pairs, wp_halves, wp_wholes, wk, wk_halves, wk_wholes, wk_last,
                  px, pb, pb_in, pp, pp_in, tg_halves, tg_wholes, tg_last, tp_pairs, tp_halves, tp_wholes,
                  k_send, k_recv, kp_send, kp_recv, tp_send, tp_recv, wp_send, wp_recv, wq_send, wq_recv, wk_send, wk_recv, t_send, t_recv, e_send, e_recv, local):
    f32 = jnp.float32
    bf16 = jnp.bfloat16
    nt = (((1,), (1,)), ((), ()))
    ctx, tp, core, ctx_at, tp_at, ctx_peers, tp_peers, twin = places()
    copies = [
        pltpu.make_async_copy(dkv_ref.at[core], kv, local.at[0]),
        pltpu.make_async_copy(tok_ref, tbuf, local.at[1]),
        pltpu.make_async_copy(wq_ref, wqbuf, local.at[2]),
        pltpu.make_async_copy(wk_ref, wkbuf, local.at[3]),
    ]
    for c in copies:
        c.start()
    meet(ctx_peers + tp_peers + [twin])
    side = tp // 8
    steps = (2, 1, -1, 0)

    def ring_of(d):
        return lax.rem(ctx // 2 + d + 4, 4)

    def pair_of(d):
        return pl.ds(pl.multiple_of(ring_of(d) * 2, 2), 2)

    swap = [
        remote(dkv_ref.at[1 - core, pair_of(d)], kv_in.at[pair_of(d)], e_send, e_recv, 8 + n, twin)
        for n, d in enumerate(steps)
    ]
    for s in swap:
        s.start()
    turned_q[...] = qb_ref[...].T
    order = [ctx_at(p, d) for d in steps for p in (1, 0)]

    def tok_cols(c):
        return tbuf[:, :, pl.ds(pl.multiple_of(c * 512, 512), 512)].reshape(512, 512)

    def query_terms(i, carry):
        c = chosen(i, order)
        wq[c] = jnp.dot(turned_q[...], tok_cols(c), preferred_element_type=f32).astype(bf16)
        return carry

    keys = Reduce(
        lambda p, d: kv.at[ctx_at(p, d), pl.ds(0, 256)], 256, ctx_peers, kv_halves, kv_wholes, kv_last, k_send, k_recv
    )
    pair_keys = PairReduce(
        lambda p, d: kv.at[ctx_at(p, d), pl.ds(256, 256)], 256, ctx_peers, kp_pairs, kp_halves, kp_wholes, kp_send, kp_recv
    )
    wq_sum = Reduce(
        lambda p, d: wq.at[ctx_at(p, d), pl.ds(0, 128)], 128, ctx_peers, wq_halves, wq_wholes, wq_last, wq_send, wq_recv
    )
    wp_sum = PairReduce(
        lambda p, d: wq.at[ctx_at(p, d), pl.ds(128, 128)], 128, ctx_peers, wp_pairs, wp_halves, wp_wholes, wp_send, wp_recv
    )
    wk_sum = Reduce(lambda p, d: wk.at[ctx_at(p, d)], 128, ctx_peers, wk_halves, wk_wholes, wk_last, wk_send, wk_recv)
    copies[1].wait()
    lax.fori_loop(0, 1, query_terms, 0)
    wq_sum.start(0, 1)
    wp_sum.start(0)
    copies[0].wait()
    for n, d in enumerate(steps):
        swap[n].wait_recv()
        for p in (1, 0):
            add_into(kv.at[ctx_at(p, d)], kv_in.at[ctx_at(p, d)])
        pair_keys.start(n)
        if d == 2:
            keys.start(0, 1, 2, 3)
    lax.fori_loop(1, 2, query_terms, 0)
    wq_sum.start(2, 3)
    lax.fori_loop(2, 4, query_terms, 0)
    wp_sum.start(1)
    keys.second(1)
    keys.second(0)
    pair_keys.paired(0)
    pair_keys.start(4, 5)
    lax.fori_loop(4, 6, query_terms, 0)
    pair_keys.paired(1, 2)
    pair_keys.second()
    wq_sum.second(1)
    keys.third()
    lax.fori_loop(6, 8, query_terms, 0)
    wp_sum.start(2, 3)
    copies[2].wait()

    def query_part(c, carry):
        px[c] = lax.dot_general(qb_ref[...], wqbuf[c], nt, preferred_element_type=f32)
        return carry

    lax.fori_loop(0, 8, query_part, 0)
    wq_sum.second(0)
    copies[3].wait()
    keys.arrived(6, 7, 8)
    total = jnp.concatenate([keys.total(...), pair_keys.total(...)], axis=0)
    back = total * cos_ref[...] - pltpu.roll(total, 64, 1) * sin_ref[...]
    total = jnp.where(core == 0, back, total)
    kvg[...] = total.astype(bf16)

    def level_of(d):
        return lax.rem(tp // 2 + d + 4, 4)

    out_parts, in_parts = (pb, pp), (pb_in, pp_in)
    swaps = [
        [
            remote(out_parts[h].at[1 - core, level_of(d)], in_parts[h].at[level_of(d)], e_send, e_recv, 4 * h + n, twin)
            for n, d in enumerate(steps)
        ]
        for h in range(2)
    ]

    def tg_block(h):
        return lambda p, d: out_parts[h].at[core, level_of(d), 1 - side if p else side]

    ring_toks = Reduce(tg_block(0), 32, tp_peers, tg_halves, tg_wholes, tg_last, t_send, t_recv)
    pair_toks = PairReduce(tg_block(1), 32, tp_peers, tp_pairs, tp_halves, tp_wholes, tp_send, tp_recv)

    def merged(h, n):
        swaps[h][n].wait_recv()
        for p in (1, 0):
            add_into(tg_block(h)(p, steps[n]), in_parts[h].at[level_of(steps[n]), 1 - side if p else side])

    def keyval_part(h, first):
        def one(c, carry):
            part = px[c] + lax.dot_general(kvg[...], wkbuf[c], nt, preferred_element_type=f32)
            part = part.astype(bf16).reshape(2, 4, 2, 32, 512)
            cols = pl.ds(pl.multiple_of((c - first) * 512, 512), 512)
            for s in range(2):
                for level in range(4):
                    for k in range(2):
                        out_parts[h][k, level, s, :, cols] = part[s, level, k]
            return carry

        return one

    def keyval_terms(i, carry):
        c = chosen(i, order)
        wk[c] = jnp.dot(turned_q[0:128, :], tok_cols(c), preferred_element_type=f32).astype(bf16)
        return carry

    lax.fori_loop(0, 6, keyval_part(0, 0), 0)
    for s in swaps[0]:
        s.start()
    turned_q[0:128, :] = total.T.astype(bf16)
    lax.fori_loop(0, 2, keyval_terms, 0)
    wk_sum.start(0, 1, 2, 3)
    lax.fori_loop(6, 8, keyval_part(1, 6), 0)
    for s in swaps[1]:
        s.start()
    merged(0, 0)
    ring_toks.start(0, 1, 2, 3)
    wp_sum.paired(0)
    wp_sum.start(4, 5)
    for n in range(4):
        merged(1, n)
        pair_toks.start(n)
    wp_sum.paired(1, 2)
    wp_sum.second()
    lax.fori_loop(2, 8, keyval_terms, 0)
    for n in (1, 2, 3):
        merged(0, n)
    ring_toks.second(1)
    ring_toks.second(0)
    wq_sum.third()
    pair_toks.paired(0)
    pair_toks.start(4, 5)
    pair_toks.paired(1, 2)
    pair_toks.second()
    wk_sum.second(1)
    wk_sum.second(0)
    ring_toks.third()
    wk_sum.third()
    wq_sum.arrived(6, 7, 8)
    sum_ref[0:128, :] = wq_sum.total(...)
    sum_ref[128:256, :] = wp_sum.total(...)
    tg_ref[:, 3072:4096] = pair_toks.total(...).astype(bf16)
    ring_toks.arrived(6, 7, 8)
    tg_ref[:, 0:3072] = ring_toks.total(...).astype(bf16)
    wk_sum.arrived(6, 7, 8)
    sum_ref[256:384, :] = wk_sum.total(...)
    for s in swap + swaps[0] + swaps[1]:
        s.wait_send()
    for r in (keys, pair_keys, wq_sum, wp_sum, wk_sum, ring_toks, pair_toks):
        r.finish()


def reduce(tok_full, wq_full, wk_full, query_back, dkv, cosine, sine):
    bf16 = jnp.bfloat16
    f32 = jnp.float32
    vmem = pl.BlockSpec(memory_space=pltpu.VMEM)
    hbm = pl.BlockSpec(memory_space=pltpu.HBM)
    dma = pltpu.SemaphoreType.DMA
    return pl.pallas_call(
        reduce_kernel,
        out_shape=(
            jax.ShapeDtypeStruct((32, 4096), bf16),
            jax.ShapeDtypeStruct((384, 512), f32),
        ),
        in_specs=[hbm, hbm, hbm, vmem, hbm, vmem, vmem],
        out_specs=(vmem, vmem),
        scratch_shapes=[
            pltpu.VMEM((16, 32, 4096), bf16),
            pltpu.VMEM((8, 512, 256), bf16),
            pltpu.VMEM((8, 512, 128), bf16),
            pltpu.VMEM((8, 512, 128), bf16),
            pltpu.VMEM((8, 512, 128), bf16),
            pltpu.VMEM((4, 128, 128), bf16),
            pltpu.VMEM((4, 256, 128), bf16),
            pltpu.VMEM((256, 128), bf16),
            pltpu.VMEM((4, 256, 128), bf16),
            pltpu.VMEM((2, 128, 128), bf16),
            pltpu.VMEM((2, 256, 128), bf16),
            pltpu.VMEM((256, 512), bf16),
            pltpu.VMEM((512, 128), bf16),
            pltpu.VMEM((8, 256, 512), bf16),
            pltpu.VMEM((4, 64, 512), bf16),
            pltpu.VMEM((4, 128, 512), bf16),
            pltpu.VMEM((128, 512), bf16),
            pltpu.VMEM((4, 128, 512), bf16),
            pltpu.VMEM((2, 64, 512), bf16),
            pltpu.VMEM((2, 128, 512), bf16),
            pltpu.VMEM((8, 128, 512), bf16),
            pltpu.VMEM((4, 64, 512), bf16),
            pltpu.VMEM((4, 128, 512), bf16),
            pltpu.VMEM((128, 512), bf16),
            pltpu.VMEM((8, 512, 512), f32),
            pltpu.VMEM((2, 4, 2, 32, 3072), bf16),
            pltpu.VMEM((4, 2, 32, 3072), bf16),
            pltpu.VMEM((2, 4, 2, 32, 1024), bf16),
            pltpu.VMEM((4, 2, 32, 1024), bf16),
            pltpu.VMEM((4, 16, 3072), bf16),
            pltpu.VMEM((4, 32, 3072), bf16),
            pltpu.VMEM((32, 3072), bf16),
            pltpu.VMEM((4, 32, 1024), bf16),
            pltpu.VMEM((2, 16, 1024), bf16),
            pltpu.VMEM((2, 32, 1024), bf16),
            dma((9,)), dma((9,)), dma((8,)), dma((8,)), dma((8,)), dma((8,)), dma((8,)), dma((8,)),
            dma((9,)), dma((9,)), dma((9,)), dma((9,)), dma((9,)), dma((9,)),
            dma((12,)), dma((12,)), dma((4,)),
        ],
        compiler_params=pltpu.CompilerParams(collective_id=1, has_side_effects=True, vmem_limit_bytes=VMEM_LIMIT),
        name="reduce",
    )(tok_full, wq_full, wk_full, query_back, dkv, cosine, sine)


def finish_kernel(tg_ref, sum_ref, token_ref, gq_ref, gk_ref):
    token_ref[...] = tg_ref[...]
    gq_ref[...] = sum_ref[0:256, :].T
    gk_ref[...] = sum_ref[256:384, :].T


def finish(token_grad, weight_grad):
    vmem = pl.BlockSpec(memory_space=pltpu.VMEM)
    return pl.pallas_call(
        finish_kernel,
        out_shape=(
            jax.ShapeDtypeStruct((32, 4096), jnp.bfloat16),
            jax.ShapeDtypeStruct((512, 256), jnp.float32),
            jax.ShapeDtypeStruct((512, 128), jnp.float32),
        ),
        in_specs=[vmem, vmem],
        out_specs=(vmem, vmem, vmem),
        name="finish",
    )(token_grad, weight_grad)


def shards(tokens, upstream, w_query, w_keyval, positions, documents):
    half_width = HEAD_DIMENSION // 2
    frequency = rope_base ** (-(jnp.arange(half_width, dtype=jnp.float32) * 2.0 / HEAD_DIMENSION))
    frequency = jnp.concatenate([frequency, frequency])[None, :]
    query, cosine, sine, key_value, tok_full, wq_full, wk_full = project(positions, frequency, tokens, w_query, w_keyval)
    query_back, dkv = attend(positions, documents, query, upstream, key_value, cosine, sine)
    return finish(*reduce(tok_full, wq_full, wk_full, query_back, dkv.reshape(2, 8, 512, 128), cosine, sine))


def solution(mesh):
    return jax.shard_map(
        shards,
        mesh=mesh,
        in_specs=(P(("ctx", "tp"), None), P("ctx", "tp"), P("ctx", "tp"), P("ctx", "tp"), P(), P()),
        out_specs=(P(("ctx", "tp"), None), P("ctx", "tp"), P("ctx", "tp")),
        check_vma=False,
    )
```

```python
import jax
import jax.numpy as jnp
import numpy as np
from jax import lax
from jax.experimental import pallas as pl
from jax.experimental.pallas import tpu as pltpu
from jax.sharding import PartitionSpec as P

HEAD_DIMENSION = 128


rope_base = 500000.0


def attend_kernel(pos_ref, doc_ref, q_ref, up_ref, kv_ref, cos_ref, sin_ref, qb_ref, dkv_ref,
                  score_sc, grad_sc, q2_sc, up2_sc, dq_sc, dk_sc, dv_sc, where_sm):
    f32 = jnp.float32
    bf16 = jnp.bfloat16
    run = 256
    rows = 2 * run
    scaling = HEAD_DIMENSION ** (-0.5)
    log2e = 1.4426950408889634
    nt = (((1,), (1,)), ((), ()))
    tn = (((0,), (0,)), ((), ()))
    nn = (((1,), (0,)), ((), ()))
    ctx = lax.axis_index("ctx")

    for s in range(16):
        where_sm[lax.shift_right_logical(pos_ref[s * run], 8)] = s
    doc = doc_ref[...]
    starts = [jnp.sum(jnp.where(doc < d, 1.0, 0.0)).astype(jnp.int32) for d in (1, 2, 3)]
    dk_sc[...] = jnp.zeros_like(dk_sc)
    dv_sc[...] = jnp.zeros_like(dv_sc)

    def one_run(t, carry):
        base = pos_ref[(ctx * 2 + t) * run]
        mine = pl.ds(pl.multiple_of(t * run, run), run)
        first = jnp.int32(0)
        for start in starts:
            first = jnp.where(start <= base, jnp.maximum(first, start), first)
        low = lax.shift_right_logical(first, 8)
        high = lax.shift_right_logical(base, 8) + 1
        q_pos = base + (lax.broadcasted_iota(jnp.int32, (1, rows), 1) & (run - 1))
        q_low = jnp.zeros_like(q_pos)
        for start in starts:
            q_low = jnp.where(start <= q_pos, jnp.maximum(q_low, start), q_low)
        for h in range(2):
            q2_sc[h * run:(h + 1) * run, :] = q_ref[mine, h * 128:(h + 1) * 128]
            up2_sc[h * run:(h + 1) * run, :] = up_ref[mine, h * 128:(h + 1) * 128]

        def keys_at(j):
            return pl.ds(pl.multiple_of(where_sm[j] * run, run), run)

        def in_pairs(one, carry):
            at = low
            for size in (4, 2, 1):
                count = (high - at) // size
                carry = lax.fori_loop(
                    0, count, lambda i, c, at=at, size=size: one([at + size * i + n for n in range(size)], c), carry
                )
                at = at + count * size
            return carry

        def scan_scores(js, peak):
            for j in js:
                at = keys_at(j)
                score = lax.dot_general(kv_ref[0, at, :], q2_sc[...], nt, preferred_element_type=f32)
                k_pos = j * run + lax.broadcasted_iota(jnp.int32, (run, 1), 0)
                score = jnp.where((k_pos >= q_low) & (k_pos <= q_pos), score, -1e30)
                score_sc[j - low] = score
                grad_sc[j - low] = lax.dot_general(kv_ref[1, at, :], up2_sc[...], nt, preferred_element_type=f32)
                peak = jnp.maximum(peak, jnp.max(score, axis=0, keepdims=True))
            return peak

        peak = in_pairs(scan_scores, jnp.full((1, rows), -1e30, f32))

        def scan_sums(js, sums):
            total, delta = sums
            for j in js:
                exponent = jnp.exp2((score_sc[j - low] - peak) * (scaling * log2e))
                score_sc[j - low] = exponent
                total = total + jnp.sum(exponent, axis=0, keepdims=True)
                delta = delta + jnp.sum(exponent * grad_sc[j - low], axis=0, keepdims=True)
            return total, delta

        zero = jnp.zeros((1, rows), f32)
        total, delta = in_pairs(scan_sums, (zero, zero))
        inverse = 1.0 / total
        delta = delta * inverse
        dq_sc[...] = jnp.zeros_like(dq_sc)

        def scan_grads(js, c):
            ats = [keys_at(j) for j in js]
            dvs = [dv_sc[at, :] for at in ats]
            dks = [dk_sc[at, :] for at in ats]
            dq = dq_sc[...]
            for n, j in enumerate(js):
                probs = score_sc[j - low] * inverse
                score_grad = (probs * (grad_sc[j - low] - delta)).astype(bf16)
                dvs[n] += lax.dot_general(probs.astype(bf16), up2_sc[...], nn, preferred_element_type=f32)
                dks[n] += lax.dot_general(score_grad, q2_sc[...], nn, preferred_element_type=f32)
                dq += lax.dot_general(kv_ref[0, ats[n], :], score_grad, tn, preferred_element_type=f32)
            dq_sc[...] = dq
            for n, at in enumerate(ats):
                dv_sc[at, :] = dvs[n]
                dk_sc[at, :] = dks[n]
            return c

        in_pairs(scan_grads, 0)
        cosine, sine = cos_ref[mine, :], sin_ref[mine, :]
        for h in range(2):
            grad = dq_sc[:, h * run:(h + 1) * run].T * scaling
            back = grad * cosine - pltpu.roll(grad, 64, 1) * sine
            qb_ref[mine, h * 128:(h + 1) * 128] = back.astype(bf16)
        return carry

    lax.fori_loop(0, 2, one_run, 0)

    def put_out(i, carry):
        at = pl.ds(pl.multiple_of(i * run, run), run)
        dkv_ref[0, at, :] = (dk_sc[at, :] * scaling).astype(bf16)
        dkv_ref[1, at, :] = dv_sc[at, :].astype(bf16)
        return carry

    lax.fori_loop(0, 16, put_out, 0)


def attend(positions, documents, query, upstream, key_value, cosine, sine):
    f32 = jnp.float32
    vmem = pl.BlockSpec(memory_space=pltpu.VMEM)
    return pl.pallas_call(
        attend_kernel,
        out_shape=(
            jax.ShapeDtypeStruct((512, 256), jnp.bfloat16),
            jax.ShapeDtypeStruct((2, 4096, 128), jnp.bfloat16),
        ),
        in_specs=[pl.BlockSpec(memory_space=pltpu.SMEM)] + [vmem] * 6,
        out_specs=(vmem, vmem),
        scratch_shapes=[
            pltpu.VMEM((16, 256, 512), f32),
            pltpu.VMEM((16, 256, 512), f32),
            pltpu.VMEM((512, 128), jnp.bfloat16),
            pltpu.VMEM((512, 128), jnp.bfloat16),
            pltpu.VMEM((128, 512), f32),
            pltpu.VMEM((4096, 128), f32),
            pltpu.VMEM((4096, 128), f32),
            pltpu.SMEM((16,), jnp.int32),
        ],
        compiler_params=pltpu.CompilerParams(vmem_limit_bytes=60 * 1024 * 1024),
        name="attend",
    )(positions, documents.reshape(32, 128), query, upstream, key_value.reshape(2, 4096, 128), cosine, sine)


MESH = pl.DeviceIdType.MESH
VMEM_LIMIT = 60 * 1024 * 1024


def places():
    ctx = lax.axis_index("ctx")
    tp = lax.axis_index("tp")
    y, x_lo = ctx // 2, lax.rem(ctx, 2)
    x_hi, z, core = tp // 8, lax.rem(tp // 2, 4), lax.rem(tp, 2)

    def ctx_at(pair, step):
        return lax.rem(y + step + 4, 4) * 2 + (1 - x_lo if pair else x_lo)

    def tp_at(pair, step, other=0):
        side = 1 - x_hi if pair else x_hi
        return side * 8 + lax.rem(z + step + 4, 4) * 2 + (1 - core if other else core)

    ctx_peers = [(ctx_at(1, 0), tp), (ctx_at(0, 1), tp), (ctx_at(0, -1), tp)]
    tp_peers = [(ctx, tp_at(1, 0)), (ctx, tp_at(0, 1)), (ctx, tp_at(0, -1))]
    twin = (ctx, tp_at(0, 0, 1))
    return ctx, tp, core, ctx_at, tp_at, ctx_peers, tp_peers, twin


def meet(peers):
    barrier = pltpu.get_barrier_semaphore()
    for peer in peers:
        pl.semaphore_signal(barrier, inc=1, device_id=peer, device_id_type=MESH)
    pl.semaphore_wait(barrier, len(peers))


def remote(src, dst, send, recv, n, peer):
    return pltpu.make_async_remote_copy(
        src_ref=src, dst_ref=dst, send_sem=send.at[n], recv_sem=recv.at[n],
        device_id=peer, device_id_type=MESH,
    )


class Gather:
    def __init__(self, block, rows, peers, send, recv):
        half = rows // 2

        def part(pair, step, h):
            return block(pair, step).at[pl.ds(h * half, half)]

        pair, after, before = peers
        self.out = [
            (part(0, 0, 0), pair), (part(0, 0, 1), pair), (block(0, 0), after), (block(0, 0), before),
            (part(1, 0, 0), after), (part(1, 0, 0), before), (part(1, 0, 1), after), (part(1, 0, 1), before),
            (part(0, -1, 0), after), (part(0, 1, 1), before),
            (part(1, -1, 0), after), (part(1, 1, 1), before),
        ]
        self.into = [
            part(1, 0, 0), part(1, 0, 1), block(0, -1), block(0, 1),
            part(1, -1, 0), part(1, 1, 0), part(1, -1, 1), part(1, 1, 1),
            part(0, 2, 0), part(0, 2, 1), part(1, 2, 0), part(1, 2, 1),
        ]
        self.sems = (send, recv)

    def start(self, *which):
        for n in which:
            ref, peer = self.out[n]
            remote(ref, ref, *self.sems, n, peer).start()

    def arrived(self, *which):
        for n in which:
            ref = self.into[n]
            remote(ref, ref, *self.sems, n, self.out[n][1]).wait_recv()

    def finish(self):
        for n, (ref, peer) in enumerate(self.out):
            remote(ref, ref, *self.sems, n, peer).wait_send()


class RingGather:
    def __init__(self, block, rows, peers, send, recv):
        half = rows // 2

        def part(pair, step, h):
            return block(pair, step).at[pl.ds(h * half, half)]

        pair, after, before = peers
        self.out = [
            (block(0, 0), after), (block(0, 0), before), (part(0, -1, 0), after), (part(0, 1, 1), before),
            (block(0, 0), pair), (block(0, -1), pair), (block(0, 1), pair), (part(0, 2, 0), pair), (part(0, 2, 1), pair),
        ]
        self.into = [
            block(0, -1), block(0, 1), part(0, 2, 0), part(0, 2, 1),
            block(1, 0), block(1, -1), block(1, 1), part(1, 2, 0), part(1, 2, 1),
        ]
        self.sems = (send, recv)

    start = Gather.start
    arrived = Gather.arrived
    finish = Gather.finish


class Share:
    order = [(0, 0), (1, 0), (0, -1), (0, 1), (1, -1), (1, 1), (0, 2), (1, 2)]

    def __init__(self, mine, theirs, twin, send, recv):
        self.mine = [mine(*p) for p in self.order]
        self.theirs = [theirs(*p) for p in self.order]
        self.twin = twin
        self.sems = (send, recv)

    def start(self, *which):
        for n in which:
            remote(self.mine[n], self.mine[n], *self.sems, n, self.twin).start()

    def arrived(self):
        for n, ref in enumerate(self.theirs):
            remote(ref, ref, *self.sems, n, self.twin).wait_recv()

    def finish(self):
        for n, ref in enumerate(self.mine):
            remote(ref, ref, *self.sems, n, self.twin).wait_send()


class Reduce:
    def __init__(self, block, rows, peers, halves, wholes, last, send, recv):
        half = rows // 2
        pair, after, before = peers

        def part(p, step, h):
            return block(p, step).at[pl.ds(h * half, half)]

        self.block = block
        self.part = part
        self.halves, self.wholes, self.last = halves, wholes, last
        self.out = [
            (part(1, 2, 0), halves.at[0], after), (part(1, 2, 1), halves.at[1], before),
            (part(0, 2, 0), halves.at[2], after), (part(0, 2, 1), halves.at[3], before),
            (block(1, 1), wholes.at[0], after), (block(1, -1), wholes.at[1], before),
            (block(0, 1), wholes.at[2], after), (block(0, -1), wholes.at[3], before),
            (block(1, 0), last, pair),
        ]
        self.sems = (send, recv)

    def start(self, *which):
        for n in which:
            src, dst, peer = self.out[n]
            remote(src, dst, *self.sems, n, peer).start()

    def arrived(self, *which):
        for n in which:
            src, dst, peer = self.out[n]
            remote(src, dst, *self.sems, n, peer).wait_recv()

    def finish(self):
        for n in range(9):
            src, dst, peer = self.out[n]
            remote(src, dst, *self.sems, n, peer).wait_send()

    def second(self, p):
        n = 0 if p else 2
        for k, (step, h) in enumerate(((1, 0), (-1, 1))):
            self.arrived(n + k)
            add_into(self.part(p, step, h), self.halves.at[n + k])
            self.start(4 + n + k)

    def third(self):
        self.arrived(4, 5)
        add_into(self.block(1, 0), self.wholes.at[0], self.wholes.at[1])
        self.start(8)

    def total(self, at):
        f32 = jnp.float32
        parts = [self.block(0, 0), self.wholes.at[2], self.wholes.at[3], self.last]
        return sum(r[at].astype(f32) for r in parts)


class PairReduce:
    steps = (2, 1, -1, 0)

    def __init__(self, block, rows, peers, pairs, halves, wholes, send, recv):
        half = rows // 2
        pair, after, before = peers

        def part(p, step, h):
            return block(p, step).at[pl.ds(h * half, half)]

        self.block = block
        self.part = part
        self.pairs, self.halves, self.wholes = pairs, halves, wholes
        self.out = [(block(1, d), pairs.at[n], pair) for n, d in enumerate(self.steps)] + [
            (part(0, 2, 0), halves.at[0], after), (part(0, 2, 1), halves.at[1], before),
            (block(0, 1), wholes.at[0], after), (block(0, -1), wholes.at[1], before),
        ]
        self.sems = (send, recv)

    start = Reduce.start
    arrived = Reduce.arrived

    def finish(self):
        for n, (src, dst, peer) in enumerate(self.out):
            remote(src, dst, *self.sems, n, peer).wait_send()

    def paired(self, *which):
        for n in which:
            self.arrived(n)
            add_into(self.block(0, self.steps[n]), self.pairs.at[n])

    def second(self):
        for k, (step, h) in enumerate(((1, 0), (-1, 1))):
            self.arrived(4 + k)
            add_into(self.part(0, step, h), self.halves.at[k])
            self.start(6 + k)

    def total(self, at):
        f32 = jnp.float32
        self.arrived(3, 6, 7)
        parts = [self.block(0, 0), self.pairs.at[3], self.wholes.at[0], self.wholes.at[1]]
        return sum(r[at].astype(f32) for r in parts)


def add_into(dst, *terms):
    rows, cols = dst.shape
    tile = max(16, min(rows, 32768 // cols))

    def one(i, carry):
        at = pl.ds(pl.multiple_of(i * tile, tile), tile)
        total = dst[at, :].astype(jnp.float32)
        for t in terms:
            total = total + t[at, :].astype(jnp.float32)
        dst[at, :] = total.astype(dst.dtype)
        return carry

    lax.fori_loop(0, rows // tile, one, 0)


def chosen(t, values):
    at = values[0]
    for n, v in enumerate(values[1:]):
        at = jnp.where(t == n + 1, v, at)
    return at


def project_kernel(pos_ref, freq_ref, tok_ref, wq_ref, wk_ref, q_ref, cos_ref, sin_ref, kv_ref, tok_out, wq_out, wk_out,
                   tbuf, wqbuf, wkbuf, kvbuf, acc, acc_kv, t_send, t_recv, c_send, c_recv, wa_send, wa_recv, wb_send, wb_recv, wk_send, wk_recv,
                   k_send, k_recv, r_send, r_recv, f_send, f_recv, local):
    f32 = jnp.float32
    bf16 = jnp.bfloat16
    ctx, tp, core, ctx_at, tp_at, ctx_peers, tp_peers, twin = places()
    copies = [
        pltpu.make_async_copy(wk_ref, wkbuf.at[ctx], local.at[0]),
        pltpu.make_async_copy(tok_ref, tbuf.at[tp], local.at[1]),
        pltpu.make_async_copy(wq_ref, wqbuf.at[ctx], local.at[2]),
    ]
    for c in copies:
        c.start()
    meet(ctx_peers + tp_peers + [twin])
    toks = Gather(lambda p, d: tbuf.at[tp_at(p, d)], 32, tp_peers, t_send, t_recv)
    tshare = Share(lambda p, d: tbuf.at[tp_at(p, d)], lambda p, d: tbuf.at[tp_at(p, d, 1)], twin, c_send, c_recv)
    wqa = Gather(lambda p, d: wqbuf.at[ctx_at(p, d), pl.ds(0, 320)], 320, ctx_peers, wa_send, wa_recv)
    wqb = RingGather(lambda p, d: wqbuf.at[ctx_at(p, d), pl.ds(320, 192)], 192, ctx_peers, wb_send, wb_recv)
    wk = Gather(lambda p, d: wkbuf.at[ctx_at(p, d)], 512, ctx_peers, wk_send, wk_recv)
    for c in copies:
        c.wait()
    toks.start(0, 1)
    wk.start(2, 3)
    toks.start(2, 3)
    wk.start(0, 1)
    wqb.start(0, 1)
    wqa.start(2, 3, 0, 1)
    wqb.start(4)
    tshare.start(0)

    row = lax.broadcasted_iota(jnp.int32, (512, 128), 0)
    place = jnp.where(row < 256, pos_ref[ctx * 512], pos_ref[ctx * 512 + 256]) + (row & 255)
    angle = place.astype(f32) * freq_ref[...]
    cos_ref[...] = jnp.cos(angle)
    sine = jnp.sin(angle)
    sin_ref[...] = jnp.where(lax.broadcasted_iota(jnp.int32, (512, 128), 1) < 64, -sine, sine)
    acc[...] = jnp.zeros_like(acc)

    wk.arrived(2, 3)
    wk.start(8, 9)
    toks.arrived(0)
    toks.start(4, 5)
    wqb.arrived(0, 1)
    wqb.start(5, 6)
    toks.arrived(2, 3)
    tshare.start(2, 3)
    toks.arrived(1)
    toks.start(6, 7)
    toks.start(8, 9)
    tshare.start(1)
    wk.arrived(0, 1)
    wk.start(4, 5, 6, 7)
    wqb.start(2, 3)
    toks.arrived(4)
    toks.start(10)
    wqa.arrived(2, 3)
    wqa.start(8, 9)
    toks.arrived(7)
    toks.start(11)
    toks.arrived(5, 6)
    tshare.start(4, 5)
    wqa.arrived(0, 1)
    wqa.start(4, 5, 6, 7)
    wk.arrived(4)
    wk.start(10)
    wk.arrived(7)
    wk.start(11)
    wqb.arrived(2, 3)
    wqb.start(7, 8)
    toks.arrived(8, 9)
    tshare.start(6)
    wk.arrived(5, 6, 8, 9, 10, 11)
    out_wk = pltpu.make_async_copy(wkbuf, wk_out, local.at[3])
    out_wk.start()
    toks.arrived(10, 11)
    tshare.start(7)
    wqa.arrived(4)
    wqa.start(10)
    wqa.arrived(7)
    wqa.start(11)
    tshare.arrived()
    out_tok = pltpu.make_async_copy(tbuf, tok_out, local.at[4])
    out_tok.start()

    def multiply(total, wbuf, blocks):
        def one(i, carry):
            c = chosen(i // 2, blocks)
            m = lax.rem(i, 2)
            cols = pl.ds(pl.multiple_of(c * 512, 512), 512)
            left = tbuf[pl.ds(m * 8, 8), :, cols].reshape(256, 512)
            rows = pl.ds(pl.multiple_of(m * 256, 256), 256)
            total[rows, :] += jnp.dot(left, wbuf[c], preferred_element_type=f32)
            return carry

        lax.fori_loop(0, 2 * len(blocks), one, 0)

    def keyval(m, carry):
        left = tbuf[pl.ds(m * 8, 8)].reshape(256, 4096)
        rows = pl.ds(pl.multiple_of(m * 256, 256), 256)
        acc_kv[rows, :] = jnp.dot(left, wkbuf[...].reshape(4096, 128), preferred_element_type=f32)
        return carry

    lax.fori_loop(0, 2, keyval, 0)
    cosine, sine = cos_ref[...], sin_ref[...]
    held = acc_kv[...].astype(bf16).astype(f32)
    turned = held * cosine + pltpu.roll(held, 64, 1) * sine
    kvbuf[core, ctx] = jnp.where(core == 0, turned, held).astype(bf16)
    keys = Gather(lambda p, d: kvbuf.at[core, ctx_at(p, d), pl.ds(0, 256)], 256, ctx_peers, k_send, k_recv)
    round_keys = RingGather(lambda p, d: kvbuf.at[core, ctx_at(p, d), pl.ds(256, 256)], 256, ctx_peers, r_send, r_recv)
    kshare = Share(lambda p, d: kvbuf.at[core, ctx_at(p, d)], lambda p, d: kvbuf.at[1 - core, ctx_at(p, d)], twin, f_send, f_recv)
    keys.start(0, 1)
    round_keys.start(0, 1)
    keys.start(2, 3)
    round_keys.start(4)
    kshare.start(0)
    wqa.arrived(8, 9)
    multiply(acc, wqbuf, [ctx_at(0, 0), ctx_at(0, -1), ctx_at(0, 1), ctx_at(0, 2)])
    round_keys.arrived(0, 1)
    round_keys.start(2, 3, 5, 6)
    keys.arrived(0, 1)
    keys.start(4, 5, 6, 7)
    keys.arrived(2, 3)
    keys.start(8, 9)
    kshare.start(2, 3)
    round_keys.arrived(4)
    kshare.start(1)
    wqa.arrived(5, 6)
    wqb.arrived(4, 5, 6)
    multiply(acc, wqbuf, [ctx_at(1, 0), ctx_at(1, -1), ctx_at(1, 1)])
    round_keys.arrived(2, 3)
    round_keys.start(7, 8)
    keys.arrived(4)
    keys.start(10)
    keys.arrived(7)
    keys.start(11)
    wqa.arrived(10, 11)
    wqb.arrived(7, 8)
    out_wq = pltpu.make_async_copy(wqbuf, wq_out, local.at[5])
    out_wq.start()
    multiply(acc, wqbuf, [ctx_at(1, 2)])
    for h in range(2):
        raw = acc[:, h * 128:(h + 1) * 128]
        q_ref[:, h * 128:(h + 1) * 128] = (raw * cosine + pltpu.roll(raw, 64, 1) * sine).astype(bf16)
    keys.arrived(5, 6)
    round_keys.arrived(5, 6)
    kshare.start(4, 5)
    keys.arrived(8, 9)
    kshare.start(6)
    keys.arrived(10, 11)
    round_keys.arrived(7, 8)
    kshare.start(7)
    kshare.arrived()
    out_kv = pltpu.make_async_copy(kvbuf, kv_ref, local.at[6])
    out_kv.start()
    toks.finish()
    tshare.finish()
    wqa.finish()
    wqb.finish()
    wk.finish()
    keys.finish()
    round_keys.finish()
    kshare.finish()
    out_tok.wait()
    out_wq.wait()
    out_wk.wait()
    out_kv.wait()


def project(positions, frequency, tokens, w_query, w_keyval):
    bf16 = jnp.bfloat16
    f32 = jnp.float32
    vmem = pl.BlockSpec(memory_space=pltpu.VMEM)
    hbm = pl.BlockSpec(memory_space=pltpu.HBM)
    dma = pltpu.SemaphoreType.DMA
    return pl.pallas_call(
        project_kernel,
        out_shape=(
            jax.ShapeDtypeStruct((512, 256), bf16),
            jax.ShapeDtypeStruct((512, 128), f32),
            jax.ShapeDtypeStruct((512, 128), f32),
            jax.ShapeDtypeStruct((2, 8, 512, 128), bf16),
            jax.ShapeDtypeStruct((16, 32, 4096), bf16),
            jax.ShapeDtypeStruct((8, 512, 256), bf16),
            jax.ShapeDtypeStruct((8, 512, 128), bf16),
        ),
        in_specs=[pl.BlockSpec(memory_space=pltpu.SMEM), vmem, hbm, hbm, hbm],
        out_specs=(vmem, vmem, vmem, hbm, hbm, hbm, hbm),
        scratch_shapes=[
            pltpu.VMEM((16, 32, 4096), bf16),
            pltpu.VMEM((8, 512, 256), bf16),
            pltpu.VMEM((8, 512, 128), bf16),
            pltpu.VMEM((2, 8, 512, 128), bf16),
            pltpu.VMEM((512, 256), f32),
            pltpu.VMEM((512, 128), f32),
            dma((12,)), dma((12,)), dma((8,)), dma((8,)), dma((12,)), dma((12,)), dma((9,)), dma((9,)), dma((12,)), dma((12,)),
            dma((12,)), dma((12,)), dma((9,)), dma((9,)), dma((8,)), dma((8,)), dma((7,)),
        ],
        compiler_params=pltpu.CompilerParams(collective_id=0, has_side_effects=True, vmem_limit_bytes=VMEM_LIMIT),
        name="project",
    )(positions, frequency, tokens, w_query, w_keyval)


def reduce_kernel(tok_ref, wq_ref, wk_ref, qb_ref, dkv_ref, cos_ref, sin_ref, tg_ref, sum_ref,
                  tbuf, wqbuf, wkbuf, kv, kv_in, kv_halves, kv_wholes, kv_last, kp_pairs, kp_halves, kp_wholes, turned_q, kvg,
                  wq, wq_halves, wq_wholes, wq_last, wp_pairs, wp_halves, wp_wholes, wk, wk_halves, wk_wholes, wk_last,
                  px, pb, pb_in, pp, pp_in, tg_halves, tg_wholes, tg_last, tp_halves, tp_wholes, tp_last,
                  k_send, k_recv, kp_send, kp_recv, tp_send, tp_recv, wp_send, wp_recv, wq_send, wq_recv, wk_send, wk_recv, t_send, t_recv, e_send, e_recv, local):
    f32 = jnp.float32
    bf16 = jnp.bfloat16
    nt = (((1,), (1,)), ((), ()))
    ctx, tp, core, ctx_at, tp_at, ctx_peers, tp_peers, twin = places()
    copies = [
        pltpu.make_async_copy(dkv_ref.at[core], kv, local.at[0]),
        pltpu.make_async_copy(tok_ref, tbuf, local.at[1]),
        pltpu.make_async_copy(wq_ref, wqbuf, local.at[2]),
        pltpu.make_async_copy(wk_ref, wkbuf, local.at[3]),
    ]
    for c in copies:
        c.start()
    meet(ctx_peers + tp_peers + [twin])
    side = tp // 8
    steps = (2, 1, -1, 0)

    def ring_of(d):
        return lax.rem(ctx // 2 + d + 4, 4)

    def pair_of(d):
        return pl.ds(pl.multiple_of(ring_of(d) * 2, 2), 2)

    swap = [
        remote(dkv_ref.at[1 - core, pair_of(d)], kv_in.at[pair_of(d)], e_send, e_recv, 8 + n, twin)
        for n, d in enumerate(steps)
    ]
    for s in swap:
        s.start()
    turned_q[...] = qb_ref[...].T
    order = [ctx_at(p, d) for d in steps for p in (1, 0)]

    def tok_cols(c):
        return tbuf[:, :, pl.ds(pl.multiple_of(c * 512, 512), 512)].reshape(512, 512)

    def query_terms(i, carry):
        c = chosen(i, order)
        wq[c] = jnp.dot(turned_q[...], tok_cols(c), preferred_element_type=f32).astype(bf16)
        return carry

    keys = Reduce(
        lambda p, d: kv.at[ctx_at(p, d), pl.ds(0, 256)], 256, ctx_peers, kv_halves, kv_wholes, kv_last, k_send, k_recv
    )
    pair_keys = PairReduce(
        lambda p, d: kv.at[ctx_at(p, d), pl.ds(256, 256)], 256, ctx_peers, kp_pairs, kp_halves, kp_wholes, kp_send, kp_recv
    )
    wq_sum = Reduce(
        lambda p, d: wq.at[ctx_at(p, d), pl.ds(0, 128)], 128, ctx_peers, wq_halves, wq_wholes, wq_last, wq_send, wq_recv
    )
    wp_sum = PairReduce(
        lambda p, d: wq.at[ctx_at(p, d), pl.ds(128, 128)], 128, ctx_peers, wp_pairs, wp_halves, wp_wholes, wp_send, wp_recv
    )
    wk_sum = Reduce(lambda p, d: wk.at[ctx_at(p, d)], 128, ctx_peers, wk_halves, wk_wholes, wk_last, wk_send, wk_recv)
    copies[1].wait()
    lax.fori_loop(0, 1, query_terms, 0)
    wq_sum.start(0, 1)
    wp_sum.start(0)
    copies[0].wait()
    for n, d in enumerate(steps):
        swap[n].wait_recv()
        for p in (1, 0):
            add_into(kv.at[ctx_at(p, d)], kv_in.at[ctx_at(p, d)])
        pair_keys.start(n)
        if d == 2:
            keys.start(0, 1, 2, 3)
    lax.fori_loop(1, 2, query_terms, 0)
    wq_sum.start(2, 3)
    lax.fori_loop(2, 4, query_terms, 0)
    wp_sum.start(1)
    keys.second(1)
    keys.second(0)
    pair_keys.paired(0)
    pair_keys.start(4, 5)
    lax.fori_loop(4, 6, query_terms, 0)
    pair_keys.paired(1, 2)
    pair_keys.second()
    wq_sum.second(1)
    keys.third()
    lax.fori_loop(6, 8, query_terms, 0)
    wp_sum.start(2, 3)
    copies[2].wait()

    def query_part(c, carry):
        px[c] = lax.dot_general(qb_ref[...], wqbuf[c], nt, preferred_element_type=f32)
        return carry

    lax.fori_loop(0, 8, query_part, 0)
    wq_sum.second(0)
    copies[3].wait()
    keys.arrived(6, 7, 8)
    total = jnp.concatenate([keys.total(...), pair_keys.total(...)], axis=0)
    back = total * cos_ref[...] - pltpu.roll(total, 64, 1) * sin_ref[...]
    total = jnp.where(core == 0, back, total)
    kvg[...] = total.astype(bf16)

    def level_of(d):
        return lax.rem(tp // 2 + d + 4, 4)

    out_parts, in_parts = (pb, pp), (pb_in, pp_in)
    swaps = [
        [
            remote(out_parts[h].at[1 - core, level_of(d)], in_parts[h].at[level_of(d)], e_send, e_recv, 4 * h + n, twin)
            for n, d in enumerate(steps)
        ]
        for h in range(2)
    ]

    def tg_block(h):
        return lambda p, d: out_parts[h].at[core, level_of(d), 1 - side if p else side]

    ring_toks = Reduce(tg_block(0), 32, tp_peers, tg_halves, tg_wholes, tg_last, t_send, t_recv)
    late_toks = Reduce(tg_block(1), 32, tp_peers, tp_halves, tp_wholes, tp_last, tp_send, tp_recv)

    def merged(h, n):
        swaps[h][n].wait_recv()
        for p in (1, 0):
            add_into(tg_block(h)(p, steps[n]), in_parts[h].at[level_of(steps[n]), 1 - side if p else side])

    def keyval_part(h, first):
        def one(c, carry):
            part = px[c] + lax.dot_general(kvg[...], wkbuf[c], nt, preferred_element_type=f32)
            part = part.astype(bf16).reshape(2, 4, 2, 32, 512)
            cols = pl.ds(pl.multiple_of((c - first) * 512, 512), 512)
            for s in range(2):
                for level in range(4):
                    for k in range(2):
                        out_parts[h][k, level, s, :, cols] = part[s, level, k]
            return carry

        return one

    def keyval_terms(i, carry):
        c = chosen(i, order)
        wk[c] = jnp.dot(turned_q[0:128, :], tok_cols(c), preferred_element_type=f32).astype(bf16)
        return carry

    lax.fori_loop(0, 6, keyval_part(0, 0), 0)
    for s in swaps[0]:
        s.start()
    turned_q[0:128, :] = total.T.astype(bf16)
    lax.fori_loop(0, 2, keyval_terms, 0)
    wk_sum.start(0, 1, 2, 3)
    lax.fori_loop(6, 8, keyval_part(1, 6), 0)
    for s in swaps[1]:
        s.start()
    merged(0, 0)
    ring_toks.start(0, 1, 2, 3)
    wp_sum.paired(0)
    wp_sum.start(4, 5)
    merged(1, 0)
    late_toks.start(0, 1, 2, 3)
    wp_sum.paired(1, 2)
    wp_sum.second()
    lax.fori_loop(2, 8, keyval_terms, 0)
    for n in (1, 2, 3):
        merged(0, n)
        merged(1, n)
    ring_toks.second(1)
    ring_toks.second(0)
    wq_sum.third()
    late_toks.second(1)
    late_toks.second(0)
    wk_sum.second(1)
    wk_sum.second(0)
    ring_toks.third()
    late_toks.third()
    wk_sum.third()
    wq_sum.arrived(6, 7, 8)
    sum_ref[0:128, :] = wq_sum.total(...)
    sum_ref[128:256, :] = wp_sum.total(...)
    ring_toks.arrived(6, 7, 8)
    tg_ref[:, 0:3072] = ring_toks.total(...).astype(bf16)
    late_toks.arrived(6, 7, 8)
    tg_ref[:, 3072:4096] = late_toks.total(...).astype(bf16)
    wk_sum.arrived(6, 7, 8)
    sum_ref[256:384, :] = wk_sum.total(...)
    for s in swap + swaps[0] + swaps[1]:
        s.wait_send()
    for r in (keys, pair_keys, wq_sum, wp_sum, wk_sum, ring_toks, late_toks):
        r.finish()


def reduce(tok_full, wq_full, wk_full, query_back, dkv, cosine, sine):
    bf16 = jnp.bfloat16
    f32 = jnp.float32
    vmem = pl.BlockSpec(memory_space=pltpu.VMEM)
    hbm = pl.BlockSpec(memory_space=pltpu.HBM)
    dma = pltpu.SemaphoreType.DMA
    return pl.pallas_call(
        reduce_kernel,
        out_shape=(
            jax.ShapeDtypeStruct((32, 4096), bf16),
            jax.ShapeDtypeStruct((384, 512), f32),
        ),
        in_specs=[hbm, hbm, hbm, vmem, hbm, vmem, vmem],
        out_specs=(vmem, vmem),
        scratch_shapes=[
            pltpu.VMEM((16, 32, 4096), bf16),
            pltpu.VMEM((8, 512, 256), bf16),
            pltpu.VMEM((8, 512, 128), bf16),
            pltpu.VMEM((8, 512, 128), bf16),
            pltpu.VMEM((8, 512, 128), bf16),
            pltpu.VMEM((4, 128, 128), bf16),
            pltpu.VMEM((4, 256, 128), bf16),
            pltpu.VMEM((256, 128), bf16),
            pltpu.VMEM((4, 256, 128), bf16),
            pltpu.VMEM((2, 128, 128), bf16),
            pltpu.VMEM((2, 256, 128), bf16),
            pltpu.VMEM((256, 512), bf16),
            pltpu.VMEM((512, 128), bf16),
            pltpu.VMEM((8, 256, 512), bf16),
            pltpu.VMEM((4, 64, 512), bf16),
            pltpu.VMEM((4, 128, 512), bf16),
            pltpu.VMEM((128, 512), bf16),
            pltpu.VMEM((4, 128, 512), bf16),
            pltpu.VMEM((2, 64, 512), bf16),
            pltpu.VMEM((2, 128, 512), bf16),
            pltpu.VMEM((8, 128, 512), bf16),
            pltpu.VMEM((4, 64, 512), bf16),
            pltpu.VMEM((4, 128, 512), bf16),
            pltpu.VMEM((128, 512), bf16),
            pltpu.VMEM((8, 512, 512), f32),
            pltpu.VMEM((2, 4, 2, 32, 3072), bf16),
            pltpu.VMEM((4, 2, 32, 3072), bf16),
            pltpu.VMEM((2, 4, 2, 32, 1024), bf16),
            pltpu.VMEM((4, 2, 32, 1024), bf16),
            pltpu.VMEM((4, 16, 3072), bf16),
            pltpu.VMEM((4, 32, 3072), bf16),
            pltpu.VMEM((32, 3072), bf16),
            pltpu.VMEM((4, 16, 1024), bf16),
            pltpu.VMEM((4, 32, 1024), bf16),
            pltpu.VMEM((32, 1024), bf16),
            dma((9,)), dma((9,)), dma((8,)), dma((8,)), dma((9,)), dma((9,)), dma((8,)), dma((8,)),
            dma((9,)), dma((9,)), dma((9,)), dma((9,)), dma((9,)), dma((9,)),
            dma((12,)), dma((12,)), dma((4,)),
        ],
        compiler_params=pltpu.CompilerParams(collective_id=1, has_side_effects=True, vmem_limit_bytes=VMEM_LIMIT),
        name="reduce",
    )(tok_full, wq_full, wk_full, query_back, dkv, cosine, sine)


def finish_kernel(tg_ref, sum_ref, token_ref, gq_ref, gk_ref):
    token_ref[...] = tg_ref[...]
    gq_ref[...] = sum_ref[0:256, :].T
    gk_ref[...] = sum_ref[256:384, :].T


def finish(token_grad, weight_grad):
    return pl.pallas_call(
        finish_kernel,
        grid=(2,),
        out_shape=(
            jax.ShapeDtypeStruct((32, 4096), jnp.bfloat16),
            jax.ShapeDtypeStruct((512, 256), jnp.float32),
            jax.ShapeDtypeStruct((512, 128), jnp.float32),
        ),
        in_specs=[pl.BlockSpec((32, 2048), lambda i: (0, i)), pl.BlockSpec((384, 256), lambda i: (0, i))],
        out_specs=(
            pl.BlockSpec((32, 2048), lambda i: (0, i)),
            pl.BlockSpec((256, 256), lambda i: (i, 0)),
            pl.BlockSpec((256, 128), lambda i: (i, 0)),
        ),
        name="finish",
    )(token_grad, weight_grad)


def shards(tokens, upstream, w_query, w_keyval, positions, documents):
    powers = np.arange(HEAD_DIMENSION // 2, dtype=np.float32) * np.float32(2.0 / HEAD_DIMENSION)
    frequency = np.power(np.float32(rope_base), -powers).astype(np.float32)
    frequency = jnp.asarray(np.concatenate([frequency, frequency])[None, :])
    query, cosine, sine, key_value, tok_full, wq_full, wk_full = project(positions, frequency, tokens, w_query, w_keyval)
    query_back, dkv = attend(positions, documents, query, upstream, key_value, cosine, sine)
    return finish(*reduce(tok_full, wq_full, wk_full, query_back, dkv.reshape(2, 8, 512, 128), cosine, sine))


def solution(mesh):
    return jax.shard_map(
        shards,
        mesh=mesh,
        in_specs=(P(("ctx", "tp"), None), P("ctx", "tp"), P("ctx", "tp"), P("ctx", "tp"), P(), P()),
        out_specs=(P(("ctx", "tp"), None), P("ctx", "tp"), P("ctx", "tp")),
        check_vma=False,
    )
```

```python
import jax
import jax.numpy as jnp
import numpy as np
from jax import lax
from jax.experimental import pallas as pl
from jax.experimental.pallas import tpu as pltpu
from jax.sharding import PartitionSpec as P

HEAD_DIMENSION = 128


rope_base = 500000.0


def attend_kernel(pos_ref, doc_ref, q_ref, up_ref, kv_ref, cos_ref, sin_ref, qb_ref, dkv_ref,
                  score_sc, grad_sc, q2_sc, up2_sc, dq_sc, dk_sc, dv_sc, where_sm):
    f32 = jnp.float32
    bf16 = jnp.bfloat16
    run = 256
    rows = 2 * run
    scaling = HEAD_DIMENSION ** (-0.5)
    log2e = 1.4426950408889634
    nt = (((1,), (1,)), ((), ()))
    tn = (((0,), (0,)), ((), ()))
    nn = (((1,), (0,)), ((), ()))
    ctx = lax.axis_index("ctx")

    for s in range(16):
        where_sm[lax.shift_right_logical(pos_ref[s * run], 8)] = s
    doc = doc_ref[...]
    starts = [jnp.sum(jnp.where(doc < d, 1.0, 0.0)).astype(jnp.int32) for d in (1, 2, 3)]
    dk_sc[...] = jnp.zeros_like(dk_sc)
    dv_sc[...] = jnp.zeros_like(dv_sc)

    def one_run(t, carry):
        base = pos_ref[(ctx * 2 + t) * run]
        mine = pl.ds(pl.multiple_of(t * run, run), run)
        first = jnp.int32(0)
        for start in starts:
            first = jnp.where(start <= base, jnp.maximum(first, start), first)
        low = lax.shift_right_logical(first, 8)
        high = lax.shift_right_logical(base, 8) + 1
        q_pos = base + (lax.broadcasted_iota(jnp.int32, (1, rows), 1) & (run - 1))
        q_low = jnp.zeros_like(q_pos)
        for start in starts:
            q_low = jnp.where(start <= q_pos, jnp.maximum(q_low, start), q_low)
        for h in range(2):
            q2_sc[h * run:(h + 1) * run, :] = q_ref[mine, h * 128:(h + 1) * 128]
            up2_sc[h * run:(h + 1) * run, :] = up_ref[mine, h * 128:(h + 1) * 128]

        def keys_at(j):
            return pl.ds(pl.multiple_of(where_sm[j] * run, run), run)

        def in_pairs(one, carry):
            at = low
            for size in (4, 2, 1):
                count = (high - at) // size
                carry = lax.fori_loop(
                    0, count, lambda i, c, at=at, size=size: one([at + size * i + n for n in range(size)], c), carry
                )
                at = at + count * size
            return carry

        def scan_scores(js, peak):
            for j in js:
                at = keys_at(j)
                score = lax.dot_general(kv_ref[0, at, :], q2_sc[...], nt, preferred_element_type=f32)
                k_pos = j * run + lax.broadcasted_iota(jnp.int32, (run, 1), 0)
                score = jnp.where((k_pos >= q_low) & (k_pos <= q_pos), score, -1e30)
                score_sc[j - low] = score
                grad_sc[j - low] = lax.dot_general(kv_ref[1, at, :], up2_sc[...], nt, preferred_element_type=f32)
                peak = jnp.maximum(peak, jnp.max(score, axis=0, keepdims=True))
            return peak

        peak = in_pairs(scan_scores, jnp.full((1, rows), -1e30, f32))

        def scan_sums(js, sums):
            total, delta = sums
            for j in js:
                exponent = jnp.exp2((score_sc[j - low] - peak) * (scaling * log2e))
                score_sc[j - low] = exponent
                total = total + jnp.sum(exponent, axis=0, keepdims=True)
                delta = delta + jnp.sum(exponent * grad_sc[j - low], axis=0, keepdims=True)
            return total, delta

        zero = jnp.zeros((1, rows), f32)
        total, delta = in_pairs(scan_sums, (zero, zero))
        inverse = 1.0 / total
        delta = delta * inverse
        dq_sc[...] = jnp.zeros_like(dq_sc)

        def scan_grads(js, c):
            ats = [keys_at(j) for j in js]
            dvs = [dv_sc[at, :] for at in ats]
            dks = [dk_sc[at, :] for at in ats]
            dq = dq_sc[...]
            for n, j in enumerate(js):
                probs = score_sc[j - low] * inverse
                score_grad = (probs * (grad_sc[j - low] - delta)).astype(bf16)
                dvs[n] += lax.dot_general(probs.astype(bf16), up2_sc[...], nn, preferred_element_type=f32)
                dks[n] += lax.dot_general(score_grad, q2_sc[...], nn, preferred_element_type=f32)
                dq += lax.dot_general(kv_ref[0, ats[n], :], score_grad, tn, preferred_element_type=f32)
            dq_sc[...] = dq
            for n, at in enumerate(ats):
                dv_sc[at, :] = dvs[n]
                dk_sc[at, :] = dks[n]
            return c

        in_pairs(scan_grads, 0)
        cosine, sine = cos_ref[mine, :], sin_ref[mine, :]
        for h in range(2):
            grad = dq_sc[:, h * run:(h + 1) * run].T * scaling
            back = grad * cosine - pltpu.roll(grad, 64, 1) * sine
            qb_ref[mine, h * 128:(h + 1) * 128] = back.astype(bf16)
        return carry

    lax.fori_loop(0, 2, one_run, 0)

    def put_out(i, carry):
        at = pl.ds(pl.multiple_of(i * run, run), run)
        dkv_ref[0, at, :] = (dk_sc[at, :] * scaling).astype(bf16)
        dkv_ref[1, at, :] = dv_sc[at, :].astype(bf16)
        return carry

    lax.fori_loop(0, 16, put_out, 0)


def attend(positions, documents, query, upstream, key_value, cosine, sine):
    f32 = jnp.float32
    vmem = pl.BlockSpec(memory_space=pltpu.VMEM)
    return pl.pallas_call(
        attend_kernel,
        out_shape=(
            jax.ShapeDtypeStruct((512, 256), jnp.bfloat16),
            jax.ShapeDtypeStruct((2, 4096, 128), jnp.bfloat16),
        ),
        in_specs=[pl.BlockSpec(memory_space=pltpu.SMEM)] + [vmem] * 6,
        out_specs=(vmem, vmem),
        scratch_shapes=[
            pltpu.VMEM((16, 256, 512), f32),
            pltpu.VMEM((16, 256, 512), f32),
            pltpu.VMEM((512, 128), jnp.bfloat16),
            pltpu.VMEM((512, 128), jnp.bfloat16),
            pltpu.VMEM((128, 512), f32),
            pltpu.VMEM((4096, 128), f32),
            pltpu.VMEM((4096, 128), f32),
            pltpu.SMEM((16,), jnp.int32),
        ],
        compiler_params=pltpu.CompilerParams(vmem_limit_bytes=60 * 1024 * 1024),
        name="attend",
    )(positions, documents.reshape(32, 128), query, upstream, key_value.reshape(2, 4096, 128), cosine, sine)


MESH = pl.DeviceIdType.MESH
VMEM_LIMIT = 60 * 1024 * 1024


def places():
    ctx = lax.axis_index("ctx")
    tp = lax.axis_index("tp")
    y, x_lo = ctx // 2, lax.rem(ctx, 2)
    x_hi, z, core = tp // 8, lax.rem(tp // 2, 4), lax.rem(tp, 2)

    def ctx_at(pair, step):
        return lax.rem(y + step + 4, 4) * 2 + (1 - x_lo if pair else x_lo)

    def tp_at(pair, step, other=0):
        side = 1 - x_hi if pair else x_hi
        return side * 8 + lax.rem(z + step + 4, 4) * 2 + (1 - core if other else core)

    ctx_peers = [(ctx_at(1, 0), tp), (ctx_at(0, 1), tp), (ctx_at(0, -1), tp)]
    tp_peers = [(ctx, tp_at(1, 0)), (ctx, tp_at(0, 1)), (ctx, tp_at(0, -1))]
    twin = (ctx, tp_at(0, 0, 1))
    return ctx, tp, core, ctx_at, tp_at, ctx_peers, tp_peers, twin


def greet(peers):
    barrier = pltpu.get_barrier_semaphore()
    for peer in peers:
        pl.semaphore_signal(barrier, inc=1, device_id=peer, device_id_type=MESH)


def met(peers):
    pl.semaphore_wait(pltpu.get_barrier_semaphore(), len(peers))


def remote(src, dst, send, recv, n, peer):
    return pltpu.make_async_remote_copy(
        src_ref=src, dst_ref=dst, send_sem=send.at[n], recv_sem=recv.at[n],
        device_id=peer, device_id_type=MESH,
    )


class Gather:
    def __init__(self, block, rows, peers, send, recv):
        half = rows // 2

        def part(pair, step, h):
            return block(pair, step).at[pl.ds(h * half, half)]

        pair, after, before = peers
        self.out = [
            (part(0, 0, 0), pair), (part(0, 0, 1), pair), (block(0, 0), after), (block(0, 0), before),
            (part(1, 0, 0), after), (part(1, 0, 0), before), (part(1, 0, 1), after), (part(1, 0, 1), before),
            (part(0, -1, 0), after), (part(0, 1, 1), before),
            (part(1, -1, 0), after), (part(1, 1, 1), before),
        ]
        self.into = [
            part(1, 0, 0), part(1, 0, 1), block(0, -1), block(0, 1),
            part(1, -1, 0), part(1, 1, 0), part(1, -1, 1), part(1, 1, 1),
            part(0, 2, 0), part(0, 2, 1), part(1, 2, 0), part(1, 2, 1),
        ]
        self.sems = (send, recv)

    def start(self, *which):
        for n in which:
            ref, peer = self.out[n]
            remote(ref, ref, *self.sems, n, peer).start()

    def arrived(self, *which):
        for n in which:
            ref = self.into[n]
            remote(ref, ref, *self.sems, n, self.out[n][1]).wait_recv()

    def finish(self):
        for n, (ref, peer) in enumerate(self.out):
            remote(ref, ref, *self.sems, n, peer).wait_send()


class RingGather:
    def __init__(self, block, rows, peers, send, recv):
        half = rows // 2

        def part(pair, step, h):
            return block(pair, step).at[pl.ds(h * half, half)]

        pair, after, before = peers
        self.out = [
            (block(0, 0), after), (block(0, 0), before), (part(0, -1, 0), after), (part(0, 1, 1), before),
            (block(0, 0), pair), (block(0, -1), pair), (block(0, 1), pair), (part(0, 2, 0), pair), (part(0, 2, 1), pair),
        ]
        self.into = [
            block(0, -1), block(0, 1), part(0, 2, 0), part(0, 2, 1),
            block(1, 0), block(1, -1), block(1, 1), part(1, 2, 0), part(1, 2, 1),
        ]
        self.sems = (send, recv)

    start = Gather.start
    arrived = Gather.arrived
    finish = Gather.finish


class Share:
    order = [(0, 0), (1, 0), (0, -1), (0, 1), (1, -1), (1, 1), (0, 2), (1, 2)]

    def __init__(self, mine, theirs, twin, send, recv):
        self.mine = [mine(*p) for p in self.order]
        self.theirs = [theirs(*p) for p in self.order]
        self.twin = twin
        self.sems = (send, recv)

    def start(self, *which):
        for n in which:
            remote(self.mine[n], self.mine[n], *self.sems, n, self.twin).start()

    def arrived(self, *which):
        for n in which or range(8):
            remote(self.theirs[n], self.theirs[n], *self.sems, n, self.twin).wait_recv()

    def finish(self):
        for n, ref in enumerate(self.mine):
            remote(ref, ref, *self.sems, n, self.twin).wait_send()


class Reduce:
    def __init__(self, block, rows, peers, halves, wholes, last, send, recv):
        half = rows // 2
        pair, after, before = peers

        def part(p, step, h):
            return block(p, step).at[pl.ds(h * half, half)]

        self.block = block
        self.part = part
        self.halves, self.wholes, self.last = halves, wholes, last
        self.out = [
            (part(1, 2, 0), halves.at[0], after), (part(1, 2, 1), halves.at[1], before),
            (part(0, 2, 0), halves.at[2], after), (part(0, 2, 1), halves.at[3], before),
            (block(1, 1), wholes.at[0], after), (block(1, -1), wholes.at[1], before),
            (block(0, 1), wholes.at[2], after), (block(0, -1), wholes.at[3], before),
            (block(1, 0), last, pair),
        ]
        self.sems = (send, recv)

    def start(self, *which):
        for n in which:
            src, dst, peer = self.out[n]
            remote(src, dst, *self.sems, n, peer).start()

    def arrived(self, *which):
        for n in which:
            src, dst, peer = self.out[n]
            remote(src, dst, *self.sems, n, peer).wait_recv()

    def finish(self):
        for n in range(9):
            src, dst, peer = self.out[n]
            remote(src, dst, *self.sems, n, peer).wait_send()

    def second(self, p):
        n = 0 if p else 2
        for k, (step, h) in enumerate(((1, 0), (-1, 1))):
            self.arrived(n + k)
            add_into(self.part(p, step, h), self.halves.at[n + k])
            self.start(4 + n + k)

    def third(self):
        self.arrived(4, 5)
        add_into(self.block(1, 0), self.wholes.at[0], self.wholes.at[1])
        self.start(8)

    def total(self, at):
        f32 = jnp.float32
        parts = [self.block(0, 0), self.wholes.at[2], self.wholes.at[3], self.last]
        return sum(r[at].astype(f32) for r in parts)


class PairReduce:
    steps = (2, 1, -1, 0)

    def __init__(self, block, rows, peers, pairs, halves, wholes, send, recv):
        half = rows // 2
        pair, after, before = peers

        def part(p, step, h):
            return block(p, step).at[pl.ds(h * half, half)]

        self.block = block
        self.part = part
        self.pairs, self.halves, self.wholes = pairs, halves, wholes
        self.out = [(block(1, d), pairs.at[n], pair) for n, d in enumerate(self.steps)] + [
            (part(0, 2, 0), halves.at[0], after), (part(0, 2, 1), halves.at[1], before),
            (block(0, 1), wholes.at[0], after), (block(0, -1), wholes.at[1], before),
        ]
        self.sems = (send, recv)

    start = Reduce.start
    arrived = Reduce.arrived

    def finish(self):
        for n, (src, dst, peer) in enumerate(self.out):
            remote(src, dst, *self.sems, n, peer).wait_send()

    def paired(self, *which):
        for n in which:
            self.arrived(n)
            add_into(self.block(0, self.steps[n]), self.pairs.at[n])

    def second(self):
        for k, (step, h) in enumerate(((1, 0), (-1, 1))):
            self.arrived(4 + k)
            add_into(self.part(0, step, h), self.halves.at[k])
            self.start(6 + k)

    def total(self, at):
        f32 = jnp.float32
        self.arrived(3, 6, 7)
        parts = [self.block(0, 0), self.pairs.at[3], self.wholes.at[0], self.wholes.at[1]]
        return sum(r[at].astype(f32) for r in parts)


def add_into(dst, *terms):
    rows, cols = dst.shape
    tile = next(t for t in (256, 128, 64, 32, 16) if rows % t == 0 and (t * cols <= 32768 or t == 16))

    def one(i, carry):
        at = pl.ds(pl.multiple_of(i * tile, tile), tile)
        total = dst[at, :].astype(jnp.float32)
        for t in terms:
            total = total + t[at, :].astype(jnp.float32)
        dst[at, :] = total.astype(dst.dtype)
        return carry

    lax.fori_loop(0, rows // tile, one, 0)


def chosen(t, values):
    at = values[0]
    for n, v in enumerate(values[1:]):
        at = jnp.where(t == n + 1, v, at)
    return at


def project_kernel(pos_ref, freq_ref, tok_ref, wq_ref, wk_ref, q_ref, cos_ref, sin_ref, kv_ref, tok_out, wq_out, wk_out,
                   tbuf, wqbuf, wkbuf, kvbuf, acc, acc_kv, pos_sc, freq_sc, cos_sc, sin_sc, t_send, t_recv, u_send, u_recv, c_send, c_recv, wa_send, wa_recv, wb_send, wb_recv, wk_send, wk_recv,
                   k_send, k_recv, r_send, r_recv, f_send, f_recv, local, outs):
    f32 = jnp.float32
    bf16 = jnp.bfloat16
    ctx, tp, core, ctx_at, tp_at, ctx_peers, tp_peers, twin = places()
    copies = [
        pltpu.make_async_copy(wk_ref, wkbuf.at[ctx], local.at[0]),
        pltpu.make_async_copy(tok_ref, tbuf.at[tp], local.at[1]),
        pltpu.make_async_copy(wq_ref, wqbuf.at[ctx], local.at[2]),
    ]
    small = [pltpu.make_async_copy(pos_ref, pos_sc, local.at[6]), pltpu.make_async_copy(freq_ref, freq_sc, local.at[7])]
    greet(ctx_peers + tp_peers + [twin])
    for c in copies + small:
        c.start()
    met(ctx_peers + tp_peers + [twin])
    toks = Gather(lambda p, d: tbuf.at[tp_at(p, d), :, pl.ds(0, 3072)], 32, tp_peers, t_send, t_recv)
    round_toks = RingGather(lambda p, d: tbuf.at[tp_at(p, d), :, pl.ds(3072, 1024)], 32, tp_peers, u_send, u_recv)
    tshare = Share(lambda p, d: tbuf.at[tp_at(p, d)], lambda p, d: tbuf.at[tp_at(p, d, 1)], twin, c_send, c_recv)
    wqa = Gather(lambda p, d: wqbuf.at[ctx_at(p, d), pl.ds(0, 416)], 416, ctx_peers, wa_send, wa_recv)
    wqb = RingGather(lambda p, d: wqbuf.at[ctx_at(p, d), pl.ds(416, 96)], 96, ctx_peers, wb_send, wb_recv)
    wk = Gather(lambda p, d: wkbuf.at[ctx_at(p, d)], 512, ctx_peers, wk_send, wk_recv)
    for c in copies:
        c.wait()
    toks.start(0, 1)
    wk.start(2, 3)
    round_toks.start(0, 1)
    toks.start(2, 3)
    round_toks.start(4)
    wk.start(0, 1)
    wqb.start(0, 1)
    wqa.start(2, 3)
    tshare.start(0)

    row = lax.broadcasted_iota(jnp.int32, (512, 128), 0)
    for c in small:
        c.wait()
    begin = [pos_sc[pl.ds(ctx * 4 + 2 * t, 1), :][:, 0:1] for t in range(2)]
    place = jnp.where(row < 256, begin[0], begin[1]) + (row & 255)
    angle = place.astype(f32) * freq_sc[...]
    cos_sc[...] = jnp.cos(angle)
    sine = jnp.sin(angle)
    sin_sc[...] = jnp.where(lax.broadcasted_iota(jnp.int32, (512, 128), 1) < 64, -sine, sine)
    acc[...] = jnp.zeros_like(acc)

    round_toks.arrived(0, 1)
    round_toks.start(2, 3, 5, 6)
    wk.arrived(2, 3)
    wk.start(8, 9)
    toks.arrived(0)
    toks.start(4, 5)
    toks.arrived(1)
    toks.start(6, 7)
    toks.arrived(2, 3)
    toks.start(8, 9)
    tshare.start(2, 3)
    round_toks.arrived(4)
    tshare.start(1)
    wqa.arrived(2, 3)
    round_toks.arrived(2, 3)
    round_toks.start(7, 8)
    wqa.start(0, 1)
    wqa.start(8, 9)
    wqb.start(4)
    wk.arrived(0, 1)
    wk.start(4, 5, 6, 7)
    wqb.arrived(0, 1)
    wqb.start(2, 3, 5, 6)
    toks.arrived(4)
    toks.start(10)
    toks.arrived(7)
    toks.start(11)
    toks.arrived(5, 6)
    round_toks.arrived(5, 6)
    tshare.start(4, 5)
    toks.arrived(8, 9)
    tshare.start(6)
    wk.arrived(4)
    wk.start(10)
    wk.arrived(7)
    wk.start(11)
    wqb.arrived(2, 3)
    wqb.start(7, 8)
    toks.arrived(10, 11)
    round_toks.arrived(7, 8)
    tshare.start(7)
    wk.arrived(5, 6, 8, 9, 10, 11)
    out_wk = pltpu.make_async_copy(wkbuf, wk_out, local.at[3])
    out_wk.start()
    out_cos = pltpu.make_async_copy(cos_sc, cos_ref, local.at[6])
    out_sin = pltpu.make_async_copy(sin_sc, sin_ref, local.at[7])
    out_cos.start()
    out_sin.start()
    tshare.arrived()
    out_tok = pltpu.make_async_copy(tbuf, tok_out, local.at[4])
    out_tok.start()

    def multiply(total, wbuf, blocks):
        def one(i, carry):
            c = chosen(i // 2, blocks)
            m = lax.rem(i, 2)
            cols = pl.ds(pl.multiple_of(c * 512, 512), 512)
            left = tbuf[pl.ds(m * 8, 8), :, cols].reshape(256, 512)
            rows = pl.ds(pl.multiple_of(m * 256, 256), 256)
            total[rows, :] += jnp.dot(left, wbuf[c], preferred_element_type=f32)
            return carry

        lax.fori_loop(0, 2 * len(blocks), one, 0)

    def keyval(m, carry):
        left = tbuf[pl.ds(m * 8, 8)].reshape(256, 4096)
        rows = pl.ds(pl.multiple_of(m * 256, 256), 256)
        acc_kv[rows, :] = jnp.dot(left, wkbuf[...].reshape(4096, 128), preferred_element_type=f32)
        return carry

    lax.fori_loop(0, 2, keyval, 0)
    cosine, sine = cos_sc[...], sin_sc[...]
    held = acc_kv[...].astype(bf16).astype(f32)
    turned = held * cosine + pltpu.roll(held, 64, 1) * sine
    kvbuf[core, ctx] = jnp.where(core == 0, turned, held).astype(bf16)
    keys = Gather(lambda p, d: kvbuf.at[core, ctx_at(p, d), pl.ds(0, 256)], 256, ctx_peers, k_send, k_recv)
    round_keys = RingGather(lambda p, d: kvbuf.at[core, ctx_at(p, d), pl.ds(256, 256)], 256, ctx_peers, r_send, r_recv)
    kshare = Share(lambda p, d: kvbuf.at[core, ctx_at(p, d)], lambda p, d: kvbuf.at[1 - core, ctx_at(p, d)], twin, f_send, f_recv)
    keys.start(0, 1)
    round_keys.start(0, 1)
    keys.start(2, 3)
    round_keys.start(4)
    kshare.start(0)
    wqa.arrived(0, 1)
    wqa.start(4, 5, 6, 7)
    wqa.arrived(8, 9)
    multiply(acc, wqbuf, [ctx_at(0, 0), ctx_at(0, -1), ctx_at(0, 1), ctx_at(0, 2)])
    round_keys.arrived(0, 1)
    round_keys.start(2, 3, 5, 6)
    keys.arrived(0, 1)
    keys.start(4, 5, 6, 7)
    keys.arrived(2, 3)
    keys.start(8, 9)
    kshare.start(2, 3)
    round_keys.arrived(4)
    kshare.start(1)
    wqa.arrived(4)
    wqa.start(10)
    wqa.arrived(7)
    wqa.start(11)
    wqa.arrived(5, 6)
    wqb.arrived(4, 5, 6)
    multiply(acc, wqbuf, [ctx_at(1, 0), ctx_at(1, -1), ctx_at(1, 1)])
    round_keys.arrived(2, 3)
    round_keys.start(7, 8)
    keys.arrived(4)
    keys.start(10)
    keys.arrived(7)
    keys.start(11)
    wqa.arrived(10, 11)
    wqb.arrived(7, 8)
    out_wq = pltpu.make_async_copy(wqbuf, wq_out, local.at[5])
    out_wq.start()
    multiply(acc, wqbuf, [ctx_at(1, 2)])
    for h in range(2):
        raw = acc[:, h * 128:(h + 1) * 128]
        q_ref[:, h * 128:(h + 1) * 128] = (raw * cosine + pltpu.roll(raw, 64, 1) * sine).astype(bf16)
    def block_out(mine, n):
        p, d = Share.order[n]
        plane = core if mine else 1 - core
        at = ctx_at(p, d)
        return pltpu.make_async_copy(kvbuf.at[plane, at], kv_ref.at[plane, at], outs.at[8 * mine + n])

    for n in range(4):
        block_out(1, n).start()
    keys.arrived(5, 6)
    round_keys.arrived(5, 6)
    kshare.start(4, 5)
    keys.arrived(8, 9)
    kshare.start(6)
    for n in (4, 5, 6):
        block_out(1, n).start()
    keys.arrived(10, 11)
    round_keys.arrived(7, 8)
    kshare.start(7)
    block_out(1, 7).start()
    for n in range(8):
        kshare.arrived(n)
        block_out(0, n).start()
    toks.finish()
    round_toks.finish()
    tshare.finish()
    wqa.finish()
    wqb.finish()
    wk.finish()
    keys.finish()
    round_keys.finish()
    kshare.finish()
    out_tok.wait()
    out_wq.wait()
    out_wk.wait()
    out_cos.wait()
    out_sin.wait()
    for n in range(8):
        block_out(0, n).wait()
        block_out(1, n).wait()


def project(positions, frequency, tokens, w_query, w_keyval):
    bf16 = jnp.bfloat16
    f32 = jnp.float32
    vmem = pl.BlockSpec(memory_space=pltpu.VMEM)
    hbm = pl.BlockSpec(memory_space=pltpu.HBM)
    dma = pltpu.SemaphoreType.DMA
    return pl.pallas_call(
        project_kernel,
        out_shape=(
            jax.ShapeDtypeStruct((512, 256), bf16),
            jax.ShapeDtypeStruct((512, 128), f32),
            jax.ShapeDtypeStruct((512, 128), f32),
            jax.ShapeDtypeStruct((2, 8, 512, 128), bf16),
            jax.ShapeDtypeStruct((16, 32, 4096), bf16),
            jax.ShapeDtypeStruct((8, 512, 256), bf16),
            jax.ShapeDtypeStruct((8, 512, 128), bf16),
        ),
        in_specs=[hbm] * 5,
        out_specs=(vmem, hbm, hbm, hbm, hbm, hbm, hbm),
        scratch_shapes=[
            pltpu.VMEM((16, 32, 4096), bf16),
            pltpu.VMEM((8, 512, 256), bf16),
            pltpu.VMEM((8, 512, 128), bf16),
            pltpu.VMEM((2, 8, 512, 128), bf16),
            pltpu.VMEM((512, 256), f32),
            pltpu.VMEM((512, 128), f32),
            pltpu.VMEM((32, 128), jnp.int32),
            pltpu.VMEM((1, 128), f32),
            pltpu.VMEM((512, 128), f32),
            pltpu.VMEM((512, 128), f32),
            dma((12,)), dma((12,)), dma((9,)), dma((9,)), dma((8,)), dma((8,)),
            dma((12,)), dma((12,)), dma((9,)), dma((9,)), dma((12,)), dma((12,)),
            dma((12,)), dma((12,)), dma((9,)), dma((9,)), dma((8,)), dma((8,)), dma((8,)), dma((16,)),
        ],
        compiler_params=pltpu.CompilerParams(collective_id=0, has_side_effects=True, vmem_limit_bytes=VMEM_LIMIT),
        name="project",
    )(positions.reshape(32, 128), frequency, tokens, w_query, w_keyval)


TOKEN_PARTS = ((0, 3), (3, 3), (6, 2))


def reduce_kernel(tok_ref, wq_ref, wk_ref, qb_ref, dkv_ref, cos_ref, sin_ref, tg_ref, sum_ref,
                  tbuf, wqbuf, wkbuf, kv, kv_in, kv_halves, kv_wholes, kv_last, kp_pairs, kp_halves, kp_wholes, turned_q, kvg,
                  wq, wq_halves, wq_wholes, wq_last, wp_pairs, wp_halves, wp_wholes, wk, wk_halves, wk_wholes, wk_last,
                  qb, cos_sc, sin_sc, px, parts_out, parts_in, parts_halves, parts_wholes, parts_last,
                  k_send, k_recv, kp_send, kp_recv, wp_send, wp_recv, wq_send, wq_recv, wk_send, wk_recv,
                  t_send, t_recv, e_send, e_recv, local):
    f32 = jnp.float32
    bf16 = jnp.bfloat16
    nt = (((1,), (1,)), ((), ()))
    ctx, tp, core, ctx_at, tp_at, ctx_peers, tp_peers, twin = places()
    copies = [
        pltpu.make_async_copy(dkv_ref.at[core], kv, local.at[0]),
        pltpu.make_async_copy(tok_ref, tbuf, local.at[1]),
        pltpu.make_async_copy(wq_ref, wqbuf, local.at[2]),
        pltpu.make_async_copy(wk_ref, wkbuf, local.at[3]),
        pltpu.make_async_copy(cos_ref, cos_sc, local.at[4]),
        pltpu.make_async_copy(sin_ref, sin_sc, local.at[5]),
    ]
    first = pltpu.make_async_copy(qb_ref, qb, local.at[6])
    greet(ctx_peers + tp_peers + [twin])
    first.start()
    for c in copies:
        c.start()
    met(ctx_peers + tp_peers + [twin])
    side = tp // 8
    steps = (2, 1, -1, 0)

    def ring_of(d):
        return lax.rem(ctx // 2 + d + 4, 4)

    def pair_of(d):
        return pl.ds(pl.multiple_of(ring_of(d) * 2, 2), 2)

    swap = [
        remote(dkv_ref.at[1 - core, pair_of(d)], kv_in.at[pair_of(d)], e_send, e_recv, 12 + n, twin)
        for n, d in enumerate(steps)
    ]
    for s in swap:
        s.start()
    first.wait()
    turned_q[...] = qb[...].T
    order = [ctx_at(p, d) for d in steps for p in (1, 0)]

    def tok_cols(c):
        return tbuf[:, :, pl.ds(pl.multiple_of(c * 512, 512), 512)].reshape(512, 512)

    def query_terms(i, carry):
        c = chosen(i, order)
        wq[c] = jnp.dot(turned_q[...], tok_cols(c), preferred_element_type=f32).astype(bf16)
        return carry

    keys = Reduce(
        lambda p, d: kv.at[ctx_at(p, d), pl.ds(0, 256)], 256, ctx_peers, kv_halves, kv_wholes, kv_last, k_send, k_recv
    )
    pair_keys = PairReduce(
        lambda p, d: kv.at[ctx_at(p, d), pl.ds(256, 256)], 256, ctx_peers, kp_pairs, kp_halves, kp_wholes, kp_send, kp_recv
    )
    wq_sum = Reduce(
        lambda p, d: wq.at[ctx_at(p, d), pl.ds(0, 128)], 128, ctx_peers, wq_halves, wq_wholes, wq_last, wq_send, wq_recv
    )
    wp_sum = PairReduce(
        lambda p, d: wq.at[ctx_at(p, d), pl.ds(128, 128)], 128, ctx_peers, wp_pairs, wp_halves, wp_wholes, wp_send, wp_recv
    )
    wk_sum = Reduce(lambda p, d: wk.at[ctx_at(p, d)], 128, ctx_peers, wk_halves, wk_wholes, wk_last, wk_send, wk_recv)
    copies[1].wait()
    lax.fori_loop(0, 1, query_terms, 0)
    wq_sum.start(0, 1)
    wp_sum.start(0)
    copies[0].wait()
    for n, d in enumerate(steps):
        swap[n].wait_recv()
        for p in (1, 0):
            add_into(kv.at[ctx_at(p, d)], kv_in.at[ctx_at(p, d)])
        pair_keys.start(n)
        if d == 2:
            keys.start(0, 1, 2, 3)
    lax.fori_loop(1, 2, query_terms, 0)
    wq_sum.start(2, 3)
    lax.fori_loop(2, 4, query_terms, 0)
    wp_sum.start(1)
    keys.second(1)
    keys.second(0)
    pair_keys.paired(0)
    pair_keys.start(4, 5)
    lax.fori_loop(4, 6, query_terms, 0)
    pair_keys.paired(1, 2)
    pair_keys.second()
    wq_sum.second(1)
    keys.third()
    lax.fori_loop(6, 8, query_terms, 0)
    wp_sum.start(2, 3)
    copies[2].wait()

    def query_part(c, carry):
        px[c] = lax.dot_general(qb[...], wqbuf[c], nt, preferred_element_type=f32)
        return carry

    lax.fori_loop(0, 8, query_part, 0)
    wq_sum.second(0)
    copies[3].wait()
    keys.arrived(6, 7, 8)
    total = jnp.concatenate([keys.total(...), pair_keys.total(...)], axis=0)
    copies[4].wait()
    copies[5].wait()
    back = total * cos_sc[...] - pltpu.roll(total, 64, 1) * sin_sc[...]
    total = jnp.where(core == 0, back, total)
    kvg[...] = total.astype(bf16)

    def level_of(d):
        return lax.rem(tp // 2 + d + 4, 4)

    count = len(TOKEN_PARTS)
    swaps = [
        [
            remote(parts_out[h].at[1 - core, level_of(d)], parts_in[h].at[level_of(d)], e_send, e_recv, 4 * h + n, twin)
            for n, d in enumerate(steps)
        ]
        for h in range(count)
    ]

    def tg_block(h):
        return lambda p, d: parts_out[h].at[core, level_of(d), 1 - side if p else side]

    toks = [
        Reduce(
            tg_block(h), 32, tp_peers, parts_halves[h], parts_wholes[h], parts_last[h], t_send.at[h], t_recv.at[h]
        )
        for h in range(count)
    ]

    def merged(h, *which):
        for n in which:
            swaps[h][n].wait_recv()
            for p in (1, 0):
                add_into(tg_block(h)(p, steps[n]), parts_in[h].at[level_of(steps[n]), 1 - side if p else side])

    def keyval_part(h):
        first, tiles = TOKEN_PARTS[h]

        def one(c, carry):
            part = px[c] + lax.dot_general(kvg[...], wkbuf[c], nt, preferred_element_type=f32)
            part = part.astype(bf16).reshape(2, 4, 2, 32, 512)
            cols = pl.ds(pl.multiple_of((c - first) * 512, 512), 512)
            for s in range(2):
                for level in range(4):
                    for k in range(2):
                        parts_out[h][k, level, s, :, cols] = part[s, level, k]
            return carry

        lax.fori_loop(first, first + tiles, one, 0)
        for s in swaps[h]:
            s.start()

    def keyval_terms(i, carry):
        c = chosen(i, order)
        wk[c] = jnp.dot(turned_q[0:128, :], tok_cols(c), preferred_element_type=f32).astype(bf16)
        return carry

    keyval_part(0)
    turned_q[0:128, :] = total.T.astype(bf16)
    lax.fori_loop(0, 2, keyval_terms, 0)
    wk_sum.start(0, 1, 2, 3)
    keyval_part(1)
    merged(0, 0)
    toks[0].start(0, 1, 2, 3)
    keyval_part(2)
    wq_sum.third()
    merged(1, 0)
    toks[1].start(0, 1, 2, 3)
    wp_sum.paired(0)
    wp_sum.start(4, 5)
    merged(2, 0)
    toks[2].start(0, 1, 2, 3)
    merged(0, 1, 2, 3)
    toks[0].second(1)
    toks[0].second(0)
    wp_sum.paired(1, 2)
    wp_sum.second()
    lax.fori_loop(2, 8, keyval_terms, 0)
    merged(1, 1, 2, 3)
    toks[1].second(1)
    toks[1].second(0)
    wk_sum.second(1)
    wk_sum.second(0)
    merged(2, 1, 2, 3)
    toks[2].second(1)
    toks[2].second(0)
    for h in range(count):
        toks[h].third()
    wk_sum.third()
    wq_sum.arrived(6, 7, 8)
    sum_ref[0:128, :] = wq_sum.total(...)
    sum_ref[128:256, :] = wp_sum.total(...)
    for h in range(count):
        first, tiles = TOKEN_PARTS[h]
        toks[h].arrived(6, 7, 8)
        tg_ref[:, first * 512:(first + tiles) * 512] = toks[h].total(...).astype(bf16)
    wk_sum.arrived(6, 7, 8)
    sum_ref[256:384, :] = wk_sum.total(...)
    for s in swap + sum(swaps, []):
        s.wait_send()
    for r in [keys, pair_keys, wq_sum, wp_sum, wk_sum] + toks:
        r.finish()


def reduce(tok_full, wq_full, wk_full, query_back, dkv, cosine, sine):
    bf16 = jnp.bfloat16
    f32 = jnp.float32
    vmem = pl.BlockSpec(memory_space=pltpu.VMEM)
    hbm = pl.BlockSpec(memory_space=pltpu.HBM)
    dma = pltpu.SemaphoreType.DMA
    return pl.pallas_call(
        reduce_kernel,
        out_shape=(
            jax.ShapeDtypeStruct((32, 4096), bf16),
            jax.ShapeDtypeStruct((384, 512), f32),
        ),
        in_specs=[hbm] * 7,
        out_specs=(vmem, vmem),
        scratch_shapes=[
            pltpu.VMEM((16, 32, 4096), bf16),
            pltpu.VMEM((8, 512, 256), bf16),
            pltpu.VMEM((8, 512, 128), bf16),
            pltpu.VMEM((8, 512, 128), bf16),
            pltpu.VMEM((8, 512, 128), bf16),
            pltpu.VMEM((4, 128, 128), bf16),
            pltpu.VMEM((4, 256, 128), bf16),
            pltpu.VMEM((256, 128), bf16),
            pltpu.VMEM((4, 256, 128), bf16),
            pltpu.VMEM((2, 128, 128), bf16),
            pltpu.VMEM((2, 256, 128), bf16),
            pltpu.VMEM((256, 512), bf16),
            pltpu.VMEM((512, 128), bf16),
            pltpu.VMEM((8, 256, 512), bf16),
            pltpu.VMEM((4, 64, 512), bf16),
            pltpu.VMEM((4, 128, 512), bf16),
            pltpu.VMEM((128, 512), bf16),
            pltpu.VMEM((4, 128, 512), bf16),
            pltpu.VMEM((2, 64, 512), bf16),
            pltpu.VMEM((2, 128, 512), bf16),
            pltpu.VMEM((8, 128, 512), bf16),
            pltpu.VMEM((4, 64, 512), bf16),
            pltpu.VMEM((4, 128, 512), bf16),
            pltpu.VMEM((128, 512), bf16),
            pltpu.VMEM((512, 256), bf16),
            pltpu.VMEM((512, 128), f32),
            pltpu.VMEM((512, 128), f32),
            pltpu.VMEM((8, 512, 512), f32),
            [pltpu.VMEM((2, 4, 2, 32, 512 * n), bf16) for _, n in TOKEN_PARTS],
            [pltpu.VMEM((4, 2, 32, 512 * n), bf16) for _, n in TOKEN_PARTS],
            [pltpu.VMEM((4, 16, 512 * n), bf16) for _, n in TOKEN_PARTS],
            [pltpu.VMEM((4, 32, 512 * n), bf16) for _, n in TOKEN_PARTS],
            [pltpu.VMEM((32, 512 * n), bf16) for _, n in TOKEN_PARTS],
            dma((9,)), dma((9,)), dma((8,)), dma((8,)), dma((8,)), dma((8,)),
            dma((9,)), dma((9,)), dma((9,)), dma((9,)), dma((3, 9)), dma((3, 9)),
            dma((16,)), dma((16,)), dma((7,)),
        ],
        compiler_params=pltpu.CompilerParams(collective_id=1, has_side_effects=True, vmem_limit_bytes=VMEM_LIMIT),
        name="reduce",
    )(tok_full, wq_full, wk_full, query_back, dkv, cosine, sine)


def finish_kernel(tg_ref, sum_ref, token_ref, gq_ref, gk_ref):
    token_ref[...] = tg_ref[...]
    gq_ref[...] = sum_ref[0:256, :].T
    gk_ref[...] = sum_ref[256:384, :].T


def finish(token_grad, weight_grad):
    return pl.pallas_call(
        finish_kernel,
        grid=(2,),
        out_shape=(
            jax.ShapeDtypeStruct((32, 4096), jnp.bfloat16),
            jax.ShapeDtypeStruct((512, 256), jnp.float32),
            jax.ShapeDtypeStruct((512, 128), jnp.float32),
        ),
        in_specs=[pl.BlockSpec((32, 2048), lambda i: (0, i)), pl.BlockSpec((384, 256), lambda i: (0, i))],
        out_specs=(
            pl.BlockSpec((32, 2048), lambda i: (0, i)),
            pl.BlockSpec((256, 256), lambda i: (i, 0)),
            pl.BlockSpec((256, 128), lambda i: (i, 0)),
        ),
        name="finish",
    )(token_grad, weight_grad)


def shards(tokens, upstream, w_query, w_keyval, positions, documents):
    powers = np.arange(HEAD_DIMENSION // 2, dtype=np.float32) * np.float32(2.0 / HEAD_DIMENSION)
    frequency = np.power(np.float32(rope_base), -powers).astype(np.float32)
    frequency = jnp.asarray(np.concatenate([frequency, frequency])[None, :])
    query, cosine, sine, key_value, tok_full, wq_full, wk_full = project(positions, frequency, tokens, w_query, w_keyval)
    query_back, dkv = attend(positions, documents, query, upstream, key_value, cosine, sine)
    return finish(*reduce(tok_full, wq_full, wk_full, query_back, dkv.reshape(2, 8, 512, 128), cosine, sine))


def solution(mesh):
    return jax.shard_map(
        shards,
        mesh=mesh,
        in_specs=(P(("ctx", "tp"), None), P("ctx", "tp"), P("ctx", "tp"), P("ctx", "tp"), P(), P()),
        out_specs=(P(("ctx", "tp"), None), P("ctx", "tp"), P("ctx", "tp")),
        check_vma=False,
    )
```

```python
import jax
import jax.numpy as jnp
import numpy as np
from jax import lax
from jax.experimental import pallas as pl
from jax.experimental.pallas import tpu as pltpu
from jax.sharding import PartitionSpec as P

HEAD_DIMENSION = 128


rope_base = 500000.0


def attend_kernel(pos_ref, doc_ref, q_ref, up_ref, kv_ref, cos_ref, sin_ref, qb_ref, dkv_ref,
                  score_sc, grad_sc, q2_sc, up2_sc, dq_sc, dk_sc, dv_sc, where_sm):
    f32 = jnp.float32
    bf16 = jnp.bfloat16
    run = 256
    rows = 2 * run
    scaling = HEAD_DIMENSION ** (-0.5)
    log2e = 1.4426950408889634
    nt = (((1,), (1,)), ((), ()))
    tn = (((0,), (0,)), ((), ()))
    nn = (((1,), (0,)), ((), ()))
    ctx = lax.axis_index("ctx")

    for s in range(16):
        where_sm[lax.shift_right_logical(pos_ref[s * run], 8)] = s
    doc = doc_ref[...]
    starts = [jnp.sum(jnp.where(doc < d, 1.0, 0.0)).astype(jnp.int32) for d in (1, 2, 3)]
    dk_sc[...] = jnp.zeros_like(dk_sc)
    dv_sc[...] = jnp.zeros_like(dv_sc)

    def one_run(t, carry):
        base = pos_ref[(ctx * 2 + t) * run]
        mine = pl.ds(pl.multiple_of(t * run, run), run)
        first = jnp.int32(0)
        for start in starts:
            first = jnp.where(start <= base, jnp.maximum(first, start), first)
        low = lax.shift_right_logical(first, 8)
        high = lax.shift_right_logical(base, 8) + 1
        q_pos = base + (lax.broadcasted_iota(jnp.int32, (1, rows), 1) & (run - 1))
        q_low = jnp.zeros_like(q_pos)
        for start in starts:
            q_low = jnp.where(start <= q_pos, jnp.maximum(q_low, start), q_low)
        for h in range(2):
            q2_sc[h * run:(h + 1) * run, :] = q_ref[mine, h * 128:(h + 1) * 128]
            up2_sc[h * run:(h + 1) * run, :] = up_ref[mine, h * 128:(h + 1) * 128]

        def keys_at(j):
            return pl.ds(pl.multiple_of(where_sm[j] * run, run), run)

        def in_pairs(one, carry):
            at = low
            for size in (4, 2, 1):
                count = (high - at) // size
                carry = lax.fori_loop(
                    0, count, lambda i, c, at=at, size=size: one([at + size * i + n for n in range(size)], c), carry
                )
                at = at + count * size
            return carry

        def scan_scores(js, peak):
            for j in js:
                at = keys_at(j)
                score = lax.dot_general(kv_ref[0, at, :], q2_sc[...], nt, preferred_element_type=f32)
                k_pos = j * run + lax.broadcasted_iota(jnp.int32, (run, 1), 0)
                score = jnp.where((k_pos >= q_low) & (k_pos <= q_pos), score, -1e30)
                score_sc[j - low] = score
                grad_sc[j - low] = lax.dot_general(kv_ref[1, at, :], up2_sc[...], nt, preferred_element_type=f32)
                peak = jnp.maximum(peak, jnp.max(score, axis=0, keepdims=True))
            return peak

        peak = in_pairs(scan_scores, jnp.full((1, rows), -1e30, f32))

        def scan_sums(js, sums):
            total, delta = sums
            for j in js:
                exponent = jnp.exp2((score_sc[j - low] - peak) * (scaling * log2e))
                score_sc[j - low] = exponent
                total = total + jnp.sum(exponent, axis=0, keepdims=True)
                delta = delta + jnp.sum(exponent * grad_sc[j - low], axis=0, keepdims=True)
            return total, delta

        zero = jnp.zeros((1, rows), f32)
        total, delta = in_pairs(scan_sums, (zero, zero))
        inverse = 1.0 / total
        delta = delta * inverse
        dq_sc[...] = jnp.zeros_like(dq_sc)

        def scan_grads(js, c):
            ats = [keys_at(j) for j in js]
            dvs = [dv_sc[at, :] for at in ats]
            dks = [dk_sc[at, :] for at in ats]
            dq = dq_sc[...]
            for n, j in enumerate(js):
                probs = score_sc[j - low] * inverse
                score_grad = (probs * (grad_sc[j - low] - delta)).astype(bf16)
                dvs[n] += lax.dot_general(probs.astype(bf16), up2_sc[...], nn, preferred_element_type=f32)
                dks[n] += lax.dot_general(score_grad, q2_sc[...], nn, preferred_element_type=f32)
                dq += lax.dot_general(kv_ref[0, ats[n], :], score_grad, tn, preferred_element_type=f32)
            dq_sc[...] = dq
            for n, at in enumerate(ats):
                dv_sc[at, :] = dvs[n]
                dk_sc[at, :] = dks[n]
            return c

        in_pairs(scan_grads, 0)
        cosine, sine = cos_ref[mine, :], sin_ref[mine, :]
        for h in range(2):
            grad = dq_sc[:, h * run:(h + 1) * run].T * scaling
            back = grad * cosine - pltpu.roll(grad, 64, 1) * sine
            qb_ref[mine, h * 128:(h + 1) * 128] = back.astype(bf16)
        return carry

    lax.fori_loop(0, 2, one_run, 0)

    def put_out(i, carry):
        at = pl.ds(pl.multiple_of(i * run, run), run)
        dkv_ref[0, at, :] = (dk_sc[at, :] * scaling).astype(bf16)
        dkv_ref[1, at, :] = dv_sc[at, :].astype(bf16)
        return carry

    lax.fori_loop(0, 16, put_out, 0)


def attend(positions, documents, query, upstream, key_value, cosine, sine):
    f32 = jnp.float32
    vmem = pl.BlockSpec(memory_space=pltpu.VMEM)
    return pl.pallas_call(
        attend_kernel,
        out_shape=(
            jax.ShapeDtypeStruct((512, 256), jnp.bfloat16),
            jax.ShapeDtypeStruct((2, 4096, 128), jnp.bfloat16),
        ),
        in_specs=[pl.BlockSpec(memory_space=pltpu.SMEM)] + [vmem] * 6,
        out_specs=(vmem, vmem),
        scratch_shapes=[
            pltpu.VMEM((16, 256, 512), f32),
            pltpu.VMEM((16, 256, 512), f32),
            pltpu.VMEM((512, 128), jnp.bfloat16),
            pltpu.VMEM((512, 128), jnp.bfloat16),
            pltpu.VMEM((128, 512), f32),
            pltpu.VMEM((4096, 128), f32),
            pltpu.VMEM((4096, 128), f32),
            pltpu.SMEM((16,), jnp.int32),
        ],
        compiler_params=pltpu.CompilerParams(vmem_limit_bytes=60 * 1024 * 1024),
        name="attend",
    )(positions, documents.reshape(32, 128), query, upstream, key_value.reshape(2, 4096, 128), cosine, sine)


MESH = pl.DeviceIdType.MESH
VMEM_LIMIT = 60 * 1024 * 1024


def places():
    ctx = lax.axis_index("ctx")
    tp = lax.axis_index("tp")
    y, x_lo = ctx // 2, lax.rem(ctx, 2)
    x_hi, z, core = tp // 8, lax.rem(tp // 2, 4), lax.rem(tp, 2)

    def ctx_at(pair, step):
        return lax.rem(y + step + 4, 4) * 2 + (1 - x_lo if pair else x_lo)

    def tp_at(pair, step, other=0):
        side = 1 - x_hi if pair else x_hi
        return side * 8 + lax.rem(z + step + 4, 4) * 2 + (1 - core if other else core)

    ctx_peers = [(ctx_at(1, 0), tp), (ctx_at(0, 1), tp), (ctx_at(0, -1), tp)]
    tp_peers = [(ctx, tp_at(1, 0)), (ctx, tp_at(0, 1)), (ctx, tp_at(0, -1))]
    twin = (ctx, tp_at(0, 0, 1))
    return ctx, tp, core, ctx_at, tp_at, ctx_peers, tp_peers, twin


def greet(peers):
    barrier = pltpu.get_barrier_semaphore()
    for peer in peers:
        pl.semaphore_signal(barrier, inc=1, device_id=peer, device_id_type=MESH)


def met(peers):
    pl.semaphore_wait(pltpu.get_barrier_semaphore(), len(peers))


def remote(src, dst, send, recv, n, peer):
    return pltpu.make_async_remote_copy(
        src_ref=src, dst_ref=dst, send_sem=send.at[n], recv_sem=recv.at[n],
        device_id=peer, device_id_type=MESH,
    )


class Gather:
    def __init__(self, block, rows, peers, send, recv):
        half = rows // 2

        def part(pair, step, h):
            return block(pair, step).at[pl.ds(h * half, half)]

        pair, after, before = peers
        self.out = [
            (part(0, 0, 0), pair), (part(0, 0, 1), pair), (block(0, 0), after), (block(0, 0), before),
            (part(1, 0, 0), after), (part(1, 0, 0), before), (part(1, 0, 1), after), (part(1, 0, 1), before),
            (part(0, -1, 0), after), (part(0, 1, 1), before),
            (part(1, -1, 0), after), (part(1, 1, 1), before),
        ]
        self.into = [
            part(1, 0, 0), part(1, 0, 1), block(0, -1), block(0, 1),
            part(1, -1, 0), part(1, 1, 0), part(1, -1, 1), part(1, 1, 1),
            part(0, 2, 0), part(0, 2, 1), part(1, 2, 0), part(1, 2, 1),
        ]
        self.sems = (send, recv)

    def start(self, *which):
        for n in which:
            ref, peer = self.out[n]
            remote(ref, ref, *self.sems, n, peer).start()

    def arrived(self, *which):
        for n in which:
            ref = self.into[n]
            remote(ref, ref, *self.sems, n, self.out[n][1]).wait_recv()

    def finish(self):
        for n, (ref, peer) in enumerate(self.out):
            remote(ref, ref, *self.sems, n, peer).wait_send()


class RingGather:
    def __init__(self, block, rows, peers, send, recv):
        half = rows // 2

        def part(pair, step, h):
            return block(pair, step).at[pl.ds(h * half, half)]

        pair, after, before = peers
        self.out = [
            (block(0, 0), after), (block(0, 0), before), (part(0, -1, 0), after), (part(0, 1, 1), before),
            (block(0, 0), pair), (block(0, -1), pair), (block(0, 1), pair), (part(0, 2, 0), pair), (part(0, 2, 1), pair),
        ]
        self.into = [
            block(0, -1), block(0, 1), part(0, 2, 0), part(0, 2, 1),
            block(1, 0), block(1, -1), block(1, 1), part(1, 2, 0), part(1, 2, 1),
        ]
        self.sems = (send, recv)

    start = Gather.start
    arrived = Gather.arrived
    finish = Gather.finish


class Share:
    order = [(0, 0), (1, 0), (0, -1), (0, 1), (1, -1), (1, 1), (0, 2), (1, 2)]

    def __init__(self, mine, theirs, twin, send, recv):
        self.mine = [mine(*p) for p in self.order]
        self.theirs = [theirs(*p) for p in self.order]
        self.twin = twin
        self.sems = (send, recv)

    def start(self, *which):
        for n in which:
            remote(self.mine[n], self.mine[n], *self.sems, n, self.twin).start()

    def arrived(self, *which):
        for n in which or range(8):
            remote(self.theirs[n], self.theirs[n], *self.sems, n, self.twin).wait_recv()

    def finish(self):
        for n, ref in enumerate(self.mine):
            remote(ref, ref, *self.sems, n, self.twin).wait_send()


class Reduce:
    def __init__(self, block, rows, peers, halves, wholes, last, send, recv):
        half = rows // 2
        pair, after, before = peers

        def part(p, step, h):
            return block(p, step).at[pl.ds(h * half, half)]

        self.block = block
        self.part = part
        self.halves, self.wholes, self.last = halves, wholes, last
        self.out = [
            (part(1, 2, 0), halves.at[0], after), (part(1, 2, 1), halves.at[1], before),
            (part(0, 2, 0), halves.at[2], after), (part(0, 2, 1), halves.at[3], before),
            (block(1, 1), wholes.at[0], after), (block(1, -1), wholes.at[1], before),
            (block(0, 1), wholes.at[2], after), (block(0, -1), wholes.at[3], before),
            (block(1, 0), last, pair),
        ]
        self.sems = (send, recv)

    def start(self, *which):
        for n in which:
            src, dst, peer = self.out[n]
            remote(src, dst, *self.sems, n, peer).start()

    def arrived(self, *which):
        for n in which:
            src, dst, peer = self.out[n]
            remote(src, dst, *self.sems, n, peer).wait_recv()

    def finish(self):
        for n in range(9):
            src, dst, peer = self.out[n]
            remote(src, dst, *self.sems, n, peer).wait_send()

    def second(self, p):
        n = 0 if p else 2
        for k, (step, h) in enumerate(((1, 0), (-1, 1))):
            self.arrived(n + k)
            add_into(self.part(p, step, h), self.halves.at[n + k])
            self.start(4 + n + k)

    def third(self):
        self.arrived(4, 5)
        add_into(self.block(1, 0), self.wholes.at[0], self.wholes.at[1])
        self.start(8)

    def total(self, at):
        f32 = jnp.float32
        parts = [self.block(0, 0), self.wholes.at[2], self.wholes.at[3], self.last]
        return sum(r[at].astype(f32) for r in parts)


class PairReduce:
    steps = (2, 1, -1, 0)

    def __init__(self, block, rows, peers, pairs, halves, wholes, send, recv):
        half = rows // 2
        pair, after, before = peers

        def part(p, step, h):
            return block(p, step).at[pl.ds(h * half, half)]

        self.block = block
        self.part = part
        self.pairs, self.halves, self.wholes = pairs, halves, wholes
        self.out = [(block(1, d), pairs.at[n], pair) for n, d in enumerate(self.steps)] + [
            (part(0, 2, 0), halves.at[0], after), (part(0, 2, 1), halves.at[1], before),
            (block(0, 1), wholes.at[0], after), (block(0, -1), wholes.at[1], before),
        ]
        self.sems = (send, recv)

    start = Reduce.start
    arrived = Reduce.arrived

    def finish(self):
        for n, (src, dst, peer) in enumerate(self.out):
            remote(src, dst, *self.sems, n, peer).wait_send()

    def paired(self, *which):
        for n in which:
            self.arrived(n)
            add_into(self.block(0, self.steps[n]), self.pairs.at[n])

    def second(self):
        for k, (step, h) in enumerate(((1, 0), (-1, 1))):
            self.arrived(4 + k)
            add_into(self.part(0, step, h), self.halves.at[k])
            self.start(6 + k)

    def total(self, at):
        f32 = jnp.float32
        self.arrived(3, 6, 7)
        parts = [self.block(0, 0), self.pairs.at[3], self.wholes.at[0], self.wholes.at[1]]
        return sum(r[at].astype(f32) for r in parts)


def add_into(dst, *terms):
    rows, cols = dst.shape
    tile = next(t for t in (256, 128, 64, 32, 16) if rows % t == 0 and (t * cols <= 32768 or t == 16))

    def one(i, carry):
        at = pl.ds(pl.multiple_of(i * tile, tile), tile)
        total = dst[at, :].astype(jnp.float32)
        for t in terms:
            total = total + t[at, :].astype(jnp.float32)
        dst[at, :] = total.astype(dst.dtype)
        return carry

    lax.fori_loop(0, rows // tile, one, 0)


def chosen(t, values):
    at = values[0]
    for n, v in enumerate(values[1:]):
        at = jnp.where(t == n + 1, v, at)
    return at


def project_kernel(pos_ref, freq_ref, tok_ref, wq_ref, wk_ref, q_ref, cos_ref, sin_ref, kv_ref, tok_out, wq_out, wk_out,
                   tbuf, wqbuf, wkbuf, kvbuf, acc, acc_kv, pos_sc, freq_sc, cos_sc, sin_sc, t_send, t_recv, u_send, u_recv, c_send, c_recv, wa_send, wa_recv, wb_send, wb_recv, wk_send, wk_recv,
                   k_send, k_recv, r_send, r_recv, f_send, f_recv, local, outs):
    f32 = jnp.float32
    bf16 = jnp.bfloat16
    ctx, tp, core, ctx_at, tp_at, ctx_peers, tp_peers, twin = places()
    copies = [
        pltpu.make_async_copy(wk_ref, wkbuf.at[ctx], local.at[0]),
        pltpu.make_async_copy(tok_ref, tbuf.at[tp], local.at[1]),
        pltpu.make_async_copy(wq_ref, wqbuf.at[ctx], local.at[2]),
    ]
    small = [pltpu.make_async_copy(pos_ref, pos_sc, local.at[6]), pltpu.make_async_copy(freq_ref, freq_sc, local.at[7])]
    greet(ctx_peers + tp_peers + [twin])
    for c in copies + small:
        c.start()
    met(ctx_peers + tp_peers + [twin])
    toks = Gather(lambda p, d: tbuf.at[tp_at(p, d), :, pl.ds(0, 3072)], 32, tp_peers, t_send, t_recv)
    round_toks = RingGather(lambda p, d: tbuf.at[tp_at(p, d), :, pl.ds(3072, 1024)], 32, tp_peers, u_send, u_recv)
    tshare = Share(lambda p, d: tbuf.at[tp_at(p, d)], lambda p, d: tbuf.at[tp_at(p, d, 1)], twin, c_send, c_recv)
    wqa = Gather(lambda p, d: wqbuf.at[ctx_at(p, d), pl.ds(0, 416)], 416, ctx_peers, wa_send, wa_recv)
    wqb = RingGather(lambda p, d: wqbuf.at[ctx_at(p, d), pl.ds(416, 96)], 96, ctx_peers, wb_send, wb_recv)
    wk = Gather(lambda p, d: wkbuf.at[ctx_at(p, d)], 512, ctx_peers, wk_send, wk_recv)
    for c in copies:
        c.wait()
    toks.start(0, 1)
    wk.start(2, 3)
    round_toks.start(0, 1)
    toks.start(2, 3)
    round_toks.start(4)
    wk.start(0, 1)
    wqb.start(0, 1)
    wqa.start(2, 3)
    tshare.start(0)

    row = lax.broadcasted_iota(jnp.int32, (512, 128), 0)
    for c in small:
        c.wait()
    begin = [pos_sc[pl.ds(ctx * 4 + 2 * t, 1), :][:, 0:1] for t in range(2)]
    place = jnp.where(row < 256, begin[0], begin[1]) + (row & 255)
    angle = place.astype(f32) * freq_sc[...]
    cos_sc[...] = jnp.cos(angle)
    sine = jnp.sin(angle)
    sin_sc[...] = jnp.where(lax.broadcasted_iota(jnp.int32, (512, 128), 1) < 64, -sine, sine)
    acc[...] = jnp.zeros_like(acc)

    round_toks.arrived(0, 1)
    round_toks.start(2, 3, 5, 6)
    wk.arrived(2, 3)
    wk.start(8, 9)
    toks.arrived(0)
    toks.start(4, 5)
    toks.arrived(1)
    toks.start(6, 7)
    toks.arrived(2, 3)
    toks.start(8, 9)
    tshare.start(2, 3)
    round_toks.arrived(4)
    tshare.start(1)
    wqa.arrived(2, 3)
    round_toks.arrived(2, 3)
    round_toks.start(7, 8)
    wqa.start(0, 1)
    wqa.start(8, 9)
    wqb.start(4)
    wk.arrived(0, 1)
    wk.start(4, 5, 6, 7)
    wqb.arrived(0, 1)
    wqb.start(2, 3, 5, 6)
    toks.arrived(4)
    toks.start(10)
    toks.arrived(7)
    toks.start(11)
    toks.arrived(5, 6)
    round_toks.arrived(5, 6)
    tshare.start(4, 5)
    toks.arrived(8, 9)
    tshare.start(6)
    wk.arrived(4)
    wk.start(10)
    wk.arrived(7)
    wk.start(11)
    wqb.arrived(2, 3)
    wqb.start(7, 8)
    toks.arrived(10, 11)
    round_toks.arrived(7, 8)
    tshare.start(7)
    wk.arrived(5, 6, 8, 9, 10, 11)
    out_wk = pltpu.make_async_copy(wkbuf, wk_out, local.at[3])
    out_wk.start()
    out_cos = pltpu.make_async_copy(cos_sc, cos_ref, local.at[6])
    out_sin = pltpu.make_async_copy(sin_sc, sin_ref, local.at[7])
    out_cos.start()
    out_sin.start()
    tshare.arrived()
    out_tok = pltpu.make_async_copy(tbuf, tok_out, local.at[4])
    out_tok.start()

    def multiply(total, wbuf, blocks):
        def one(i, carry):
            c = chosen(i // 2, blocks)
            m = lax.rem(i, 2)
            cols = pl.ds(pl.multiple_of(c * 512, 512), 512)
            left = tbuf[pl.ds(m * 8, 8), :, cols].reshape(256, 512)
            rows = pl.ds(pl.multiple_of(m * 256, 256), 256)
            total[rows, :] += jnp.dot(left, wbuf[c], preferred_element_type=f32)
            return carry

        lax.fori_loop(0, 2 * len(blocks), one, 0)

    def keyval(m, carry):
        left = tbuf[pl.ds(m * 8, 8)].reshape(256, 4096)
        rows = pl.ds(pl.multiple_of(m * 256, 256), 256)
        acc_kv[rows, :] = jnp.dot(left, wkbuf[...].reshape(4096, 128), preferred_element_type=f32)
        return carry

    lax.fori_loop(0, 2, keyval, 0)
    cosine, sine = cos_sc[...], sin_sc[...]
    held = acc_kv[...].astype(bf16).astype(f32)
    turned = held * cosine + pltpu.roll(held, 64, 1) * sine
    kvbuf[core, ctx] = jnp.where(core == 0, turned, held).astype(bf16)
    keys = Gather(lambda p, d: kvbuf.at[core, ctx_at(p, d), pl.ds(0, 256)], 256, ctx_peers, k_send, k_recv)
    round_keys = RingGather(lambda p, d: kvbuf.at[core, ctx_at(p, d), pl.ds(256, 256)], 256, ctx_peers, r_send, r_recv)
    kshare = Share(lambda p, d: kvbuf.at[core, ctx_at(p, d)], lambda p, d: kvbuf.at[1 - core, ctx_at(p, d)], twin, f_send, f_recv)
    keys.start(0, 1)
    round_keys.start(0, 1)
    keys.start(2, 3)
    round_keys.start(4)
    kshare.start(0)
    wqa.arrived(0, 1)
    wqa.start(4, 5, 6, 7)
    wqa.arrived(8, 9)
    multiply(acc, wqbuf, [ctx_at(0, 0), ctx_at(0, -1), ctx_at(0, 1), ctx_at(0, 2)])
    round_keys.arrived(0, 1)
    round_keys.start(2, 3, 5, 6)
    keys.arrived(0, 1)
    keys.start(4, 5, 6, 7)
    keys.arrived(2, 3)
    keys.start(8, 9)
    kshare.start(2, 3)
    round_keys.arrived(4)
    kshare.start(1)
    wqa.arrived(4)
    wqa.start(10)
    wqa.arrived(7)
    wqa.start(11)
    wqa.arrived(5, 6)
    wqb.arrived(4, 5, 6)
    multiply(acc, wqbuf, [ctx_at(1, 0), ctx_at(1, -1), ctx_at(1, 1)])
    round_keys.arrived(2, 3)
    round_keys.start(7, 8)
    keys.arrived(4)
    keys.start(10)
    keys.arrived(7)
    keys.start(11)
    wqa.arrived(10, 11)
    wqb.arrived(7, 8)
    out_wq = pltpu.make_async_copy(wqbuf, wq_out, local.at[5])
    out_wq.start()
    multiply(acc, wqbuf, [ctx_at(1, 2)])
    for h in range(2):
        raw = acc[:, h * 128:(h + 1) * 128]
        q_ref[:, h * 128:(h + 1) * 128] = (raw * cosine + pltpu.roll(raw, 64, 1) * sine).astype(bf16)
    def block_out(mine, n):
        p, d = Share.order[n]
        plane = core if mine else 1 - core
        at = ctx_at(p, d)
        return pltpu.make_async_copy(kvbuf.at[plane, at], kv_ref.at[plane, at], outs.at[8 * mine + n])

    for n in range(4):
        block_out(1, n).start()
    keys.arrived(5, 6)
    round_keys.arrived(5, 6)
    kshare.start(4, 5)
    keys.arrived(8, 9)
    kshare.start(6)
    for n in (4, 5, 6):
        block_out(1, n).start()
    keys.arrived(10, 11)
    round_keys.arrived(7, 8)
    kshare.start(7)
    block_out(1, 7).start()
    for n in range(8):
        kshare.arrived(n)
        block_out(0, n).start()
    toks.finish()
    round_toks.finish()
    tshare.finish()
    wqa.finish()
    wqb.finish()
    wk.finish()
    keys.finish()
    round_keys.finish()
    kshare.finish()
    out_tok.wait()
    out_wq.wait()
    out_wk.wait()
    out_cos.wait()
    out_sin.wait()
    for n in range(8):
        block_out(0, n).wait()
        block_out(1, n).wait()


def project(positions, frequency, tokens, w_query, w_keyval):
    bf16 = jnp.bfloat16
    f32 = jnp.float32
    vmem = pl.BlockSpec(memory_space=pltpu.VMEM)
    hbm = pl.BlockSpec(memory_space=pltpu.HBM)
    dma = pltpu.SemaphoreType.DMA
    return pl.pallas_call(
        project_kernel,
        out_shape=(
            jax.ShapeDtypeStruct((512, 256), bf16),
            jax.ShapeDtypeStruct((512, 128), f32),
            jax.ShapeDtypeStruct((512, 128), f32),
            jax.ShapeDtypeStruct((2, 8, 512, 128), bf16),
            jax.ShapeDtypeStruct((16, 32, 4096), bf16),
            jax.ShapeDtypeStruct((8, 512, 256), bf16),
            jax.ShapeDtypeStruct((8, 512, 128), bf16),
        ),
        in_specs=[hbm] * 5,
        out_specs=(vmem, hbm, hbm, hbm, hbm, hbm, hbm),
        scratch_shapes=[
            pltpu.VMEM((16, 32, 4096), bf16),
            pltpu.VMEM((8, 512, 256), bf16),
            pltpu.VMEM((8, 512, 128), bf16),
            pltpu.VMEM((2, 8, 512, 128), bf16),
            pltpu.VMEM((512, 256), f32),
            pltpu.VMEM((512, 128), f32),
            pltpu.VMEM((32, 128), jnp.int32),
            pltpu.VMEM((1, 128), f32),
            pltpu.VMEM((512, 128), f32),
            pltpu.VMEM((512, 128), f32),
            dma((12,)), dma((12,)), dma((9,)), dma((9,)), dma((8,)), dma((8,)),
            dma((12,)), dma((12,)), dma((9,)), dma((9,)), dma((12,)), dma((12,)),
            dma((12,)), dma((12,)), dma((9,)), dma((9,)), dma((8,)), dma((8,)), dma((8,)), dma((16,)),
        ],
        compiler_params=pltpu.CompilerParams(collective_id=0, has_side_effects=True, vmem_limit_bytes=VMEM_LIMIT),
        name="project",
    )(positions.reshape(32, 128), frequency, tokens, w_query, w_keyval)


TOKEN_PARTS = ((0, 2), (2, 3), (5, 3))


def reduce_kernel(tok_ref, wq_ref, wk_ref, qb_ref, dkv_ref, cos_ref, sin_ref, tg_ref, sum_ref,
                  tbuf, wqbuf, wkbuf, kv, kv_in, kv_halves, kv_wholes, kv_last, kp_pairs, kp_halves, kp_wholes, turned_q, kvg,
                  wq, wq_halves, wq_wholes, wq_last, wp_pairs, wp_halves, wp_wholes, wk, wk_halves, wk_wholes, wk_last,
                  qb, cos_sc, sin_sc, px, parts_out, parts_in, parts_halves, parts_wholes, parts_last, pair_parts,
                  k_send, k_recv, kp_send, kp_recv, wp_send, wp_recv, wq_send, wq_recv, wk_send, wk_recv,
                  t_send, t_recv, e_send, e_recv, local):
    f32 = jnp.float32
    bf16 = jnp.bfloat16
    nt = (((1,), (1,)), ((), ()))
    ctx, tp, core, ctx_at, tp_at, ctx_peers, tp_peers, twin = places()
    copies = [
        pltpu.make_async_copy(dkv_ref.at[core], kv, local.at[0]),
        pltpu.make_async_copy(tok_ref, tbuf, local.at[1]),
        pltpu.make_async_copy(wq_ref, wqbuf, local.at[2]),
        pltpu.make_async_copy(wk_ref, wkbuf, local.at[3]),
        pltpu.make_async_copy(cos_ref, cos_sc, local.at[4]),
        pltpu.make_async_copy(sin_ref, sin_sc, local.at[5]),
    ]
    first = pltpu.make_async_copy(qb_ref, qb, local.at[6])
    greet(ctx_peers + tp_peers + [twin])
    first.start()
    for c in copies:
        c.start()
    met(ctx_peers + tp_peers + [twin])
    side = tp // 8
    steps = (2, 1, -1, 0)

    def ring_of(d):
        return lax.rem(ctx // 2 + d + 4, 4)

    def pair_of(d):
        return pl.ds(pl.multiple_of(ring_of(d) * 2, 2), 2)

    swap = [
        remote(dkv_ref.at[1 - core, pair_of(d)], kv_in.at[pair_of(d)], e_send, e_recv, 12 + n, twin)
        for n, d in enumerate(steps)
    ]
    for s in swap:
        s.start()
    first.wait()
    turned_q[...] = qb[...].T
    order = [ctx_at(p, d) for d in steps for p in (1, 0)]

    def tok_cols(c):
        return tbuf[:, :, pl.ds(pl.multiple_of(c * 512, 512), 512)].reshape(512, 512)

    def query_terms(i, carry):
        c = chosen(i, order)
        wq[c] = jnp.dot(turned_q[...], tok_cols(c), preferred_element_type=f32).astype(bf16)
        return carry

    keys = Reduce(
        lambda p, d: kv.at[ctx_at(p, d), pl.ds(0, 256)], 256, ctx_peers, kv_halves, kv_wholes, kv_last, k_send, k_recv
    )
    pair_keys = PairReduce(
        lambda p, d: kv.at[ctx_at(p, d), pl.ds(256, 256)], 256, ctx_peers, kp_pairs, kp_halves, kp_wholes, kp_send, kp_recv
    )
    wq_sum = Reduce(
        lambda p, d: wq.at[ctx_at(p, d), pl.ds(0, 128)], 128, ctx_peers, wq_halves, wq_wholes, wq_last, wq_send, wq_recv
    )
    wp_sum = PairReduce(
        lambda p, d: wq.at[ctx_at(p, d), pl.ds(128, 128)], 128, ctx_peers, wp_pairs, wp_halves, wp_wholes, wp_send, wp_recv
    )
    wk_sum = Reduce(lambda p, d: wk.at[ctx_at(p, d)], 128, ctx_peers, wk_halves, wk_wholes, wk_last, wk_send, wk_recv)
    copies[1].wait()
    lax.fori_loop(0, 1, query_terms, 0)
    wq_sum.start(0, 1)
    wp_sum.start(0)
    copies[0].wait()
    for n, d in enumerate(steps):
        swap[n].wait_recv()
        for p in (1, 0):
            add_into(kv.at[ctx_at(p, d)], kv_in.at[ctx_at(p, d)])
        pair_keys.start(n)
        if d == 2:
            keys.start(0, 1, 2, 3)
    lax.fori_loop(1, 2, query_terms, 0)
    wq_sum.start(2, 3)
    lax.fori_loop(2, 4, query_terms, 0)
    wp_sum.start(1)
    keys.second(1)
    keys.second(0)
    pair_keys.paired(0)
    pair_keys.start(4, 5)
    lax.fori_loop(4, 6, query_terms, 0)
    pair_keys.paired(1, 2)
    pair_keys.second()
    wq_sum.second(1)
    keys.third()
    lax.fori_loop(6, 8, query_terms, 0)
    wp_sum.start(2, 3)
    copies[2].wait()

    def query_part(c, carry):
        px[c] = lax.dot_general(qb[...], wqbuf[c], nt, preferred_element_type=f32)
        return carry

    lax.fori_loop(0, 8, query_part, 0)
    wq_sum.second(0)
    wp_sum.paired(0)
    wp_sum.start(4, 5)
    copies[3].wait()
    keys.arrived(6, 7, 8)
    total = jnp.concatenate([keys.total(...), pair_keys.total(...)], axis=0)
    copies[4].wait()
    copies[5].wait()
    back = total * cos_sc[...] - pltpu.roll(total, 64, 1) * sin_sc[...]
    total = jnp.where(core == 0, back, total)
    kvg[...] = total.astype(bf16)

    def level_of(d):
        return lax.rem(tp // 2 + d + 4, 4)

    count = len(TOKEN_PARTS)
    swaps = [
        [
            remote(parts_out[h].at[1 - core, level_of(d)], parts_in[h].at[level_of(d)], e_send, e_recv, 4 * h + n, twin)
            for n, d in enumerate(steps)
        ]
        for h in range(count)
    ]

    def tg_block(h):
        return lambda p, d: parts_out[h].at[core, level_of(d), 1 - side if p else side]

    toks = [
        Reduce(
            tg_block(h), 32, tp_peers, parts_halves[h], parts_wholes[h], parts_last[h], t_send.at[h], t_recv.at[h]
        )
        for h in range(2)
    ]
    pair_toks = PairReduce(
        tg_block(2), 32, tp_peers, pair_parts, parts_halves[2], parts_wholes[2], t_send.at[2], t_recv.at[2]
    )

    def merged(h, *which):
        for n in which:
            swaps[h][n].wait_recv()
            for p in (1, 0):
                add_into(tg_block(h)(p, steps[n]), parts_in[h].at[level_of(steps[n]), 1 - side if p else side])

    def keyval_part(h):
        first, tiles = TOKEN_PARTS[h]

        def one(c, carry):
            part = px[c] + lax.dot_general(kvg[...], wkbuf[c], nt, preferred_element_type=f32)
            part = part.astype(bf16).reshape(2, 4, 2, 32, 512)
            cols = pl.ds(pl.multiple_of((c - first) * 512, 512), 512)
            for s in range(2):
                for level in range(4):
                    for k in range(2):
                        parts_out[h][k, level, s, :, cols] = part[s, level, k]
            return carry

        lax.fori_loop(first, first + tiles, one, 0)
        for s in swaps[h]:
            s.start()

    def keyval_terms(i, carry):
        c = chosen(i, order)
        wk[c] = jnp.dot(turned_q[0:128, :], tok_cols(c), preferred_element_type=f32).astype(bf16)
        return carry

    keyval_part(0)
    turned_q[0:128, :] = total.T.astype(bf16)
    keyval_part(2)
    merged(0, 0)
    toks[0].start(0, 1, 2, 3)
    lax.fori_loop(0, 2, keyval_terms, 0)
    wk_sum.start(0, 1, 2, 3)
    for n in range(4):
        merged(2, n)
        pair_toks.start(n)
    keyval_part(1)
    merged(1, 0)
    toks[1].start(0, 1, 2, 3)
    merged(0, 1, 2, 3)
    toks[0].second(1)
    toks[0].second(0)
    wp_sum.paired(1, 2)
    wp_sum.second()
    lax.fori_loop(2, 8, keyval_terms, 0)
    pair_toks.paired(0)
    pair_toks.start(4, 5)
    merged(1, 1, 2, 3)
    toks[1].second(1)
    toks[1].second(0)
    wk_sum.second(1)
    wk_sum.second(0)
    wq_sum.third()
    pair_toks.paired(1, 2)
    pair_toks.second()
    toks[0].third()
    toks[1].third()
    wk_sum.third()
    wq_sum.arrived(6, 7, 8)
    sum_ref[0:128, :] = wq_sum.total(...)
    sum_ref[128:256, :] = wp_sum.total(...)
    for h in (0, 2, 1):
        first, tiles = TOKEN_PARTS[h]
        if h < 2:
            toks[h].arrived(6, 7, 8)
        part = toks[h] if h < 2 else pair_toks
        tg_ref[:, first * 512:(first + tiles) * 512] = part.total(...).astype(bf16)
    wk_sum.arrived(6, 7, 8)
    sum_ref[256:384, :] = wk_sum.total(...)
    for s in swap + sum(swaps, []):
        s.wait_send()
    for r in [keys, pair_keys, wq_sum, wp_sum, wk_sum, pair_toks] + toks:
        r.finish()


def reduce(tok_full, wq_full, wk_full, query_back, dkv, cosine, sine):
    bf16 = jnp.bfloat16
    f32 = jnp.float32
    vmem = pl.BlockSpec(memory_space=pltpu.VMEM)
    hbm = pl.BlockSpec(memory_space=pltpu.HBM)
    dma = pltpu.SemaphoreType.DMA
    return pl.pallas_call(
        reduce_kernel,
        out_shape=(
            jax.ShapeDtypeStruct((32, 4096), bf16),
            jax.ShapeDtypeStruct((384, 512), f32),
        ),
        in_specs=[hbm] * 7,
        out_specs=(vmem, vmem),
        scratch_shapes=[
            pltpu.VMEM((16, 32, 4096), bf16),
            pltpu.VMEM((8, 512, 256), bf16),
            pltpu.VMEM((8, 512, 128), bf16),
            pltpu.VMEM((8, 512, 128), bf16),
            pltpu.VMEM((8, 512, 128), bf16),
            pltpu.VMEM((4, 128, 128), bf16),
            pltpu.VMEM((4, 256, 128), bf16),
            pltpu.VMEM((256, 128), bf16),
            pltpu.VMEM((4, 256, 128), bf16),
            pltpu.VMEM((2, 128, 128), bf16),
            pltpu.VMEM((2, 256, 128), bf16),
            pltpu.VMEM((256, 512), bf16),
            pltpu.VMEM((512, 128), bf16),
            pltpu.VMEM((8, 256, 512), bf16),
            pltpu.VMEM((4, 64, 512), bf16),
            pltpu.VMEM((4, 128, 512), bf16),
            pltpu.VMEM((128, 512), bf16),
            pltpu.VMEM((4, 128, 512), bf16),
            pltpu.VMEM((2, 64, 512), bf16),
            pltpu.VMEM((2, 128, 512), bf16),
            pltpu.VMEM((8, 128, 512), bf16),
            pltpu.VMEM((4, 64, 512), bf16),
            pltpu.VMEM((4, 128, 512), bf16),
            pltpu.VMEM((128, 512), bf16),
            pltpu.VMEM((512, 256), bf16),
            pltpu.VMEM((512, 128), f32),
            pltpu.VMEM((512, 128), f32),
            pltpu.VMEM((8, 512, 512), f32),
            [pltpu.VMEM((2, 4, 2, 32, 512 * n), bf16) for _, n in TOKEN_PARTS],
            [pltpu.VMEM((4, 2, 32, 512 * n), bf16) for _, n in TOKEN_PARTS],
            [pltpu.VMEM((4, 16, 512 * n), bf16) for _, n in TOKEN_PARTS],
            [pltpu.VMEM((4, 32, 512 * n), bf16) for _, n in TOKEN_PARTS],
            [pltpu.VMEM((32, 512 * n), bf16) for _, n in TOKEN_PARTS],
            pltpu.VMEM((4, 32, 512 * TOKEN_PARTS[2][1]), bf16),
            dma((9,)), dma((9,)), dma((8,)), dma((8,)), dma((8,)), dma((8,)),
            dma((9,)), dma((9,)), dma((9,)), dma((9,)), dma((3, 9)), dma((3, 9)),
            dma((16,)), dma((16,)), dma((7,)),
        ],
        compiler_params=pltpu.CompilerParams(collective_id=1, has_side_effects=True, vmem_limit_bytes=VMEM_LIMIT),
        name="reduce",
    )(tok_full, wq_full, wk_full, query_back, dkv, cosine, sine)


def finish_kernel(tg_ref, sum_ref, token_ref, gq_ref, gk_ref):
    token_ref[...] = tg_ref[...]
    gq_ref[...] = sum_ref[0:256, :].T
    gk_ref[...] = sum_ref[256:384, :].T


def finish(token_grad, weight_grad):
    return pl.pallas_call(
        finish_kernel,
        grid=(2,),
        out_shape=(
            jax.ShapeDtypeStruct((32, 4096), jnp.bfloat16),
            jax.ShapeDtypeStruct((512, 256), jnp.float32),
            jax.ShapeDtypeStruct((512, 128), jnp.float32),
        ),
        in_specs=[pl.BlockSpec((32, 2048), lambda i: (0, i)), pl.BlockSpec((384, 256), lambda i: (0, i))],
        out_specs=(
            pl.BlockSpec((32, 2048), lambda i: (0, i)),
            pl.BlockSpec((256, 256), lambda i: (i, 0)),
            pl.BlockSpec((256, 128), lambda i: (i, 0)),
        ),
        name="finish",
    )(token_grad, weight_grad)


def shards(tokens, upstream, w_query, w_keyval, positions, documents):
    powers = np.arange(HEAD_DIMENSION // 2, dtype=np.float32) * np.float32(2.0 / HEAD_DIMENSION)
    frequency = np.power(np.float32(rope_base), -powers).astype(np.float32)
    frequency = jnp.asarray(np.concatenate([frequency, frequency])[None, :])
    query, cosine, sine, key_value, tok_full, wq_full, wk_full = project(positions, frequency, tokens, w_query, w_keyval)
    query_back, dkv = attend(positions, documents, query, upstream, key_value, cosine, sine)
    return finish(*reduce(tok_full, wq_full, wk_full, query_back, dkv.reshape(2, 8, 512, 128), cosine, sine))


def solution(mesh):
    return jax.shard_map(
        shards,
        mesh=mesh,
        in_specs=(P(("ctx", "tp"), None), P("ctx", "tp"), P("ctx", "tp"), P("ctx", "tp"), P(), P()),
        out_specs=(P(("ctx", "tp"), None), P("ctx", "tp"), P("ctx", "tp")),
        check_vma=False,
    )
```

```python
import jax
import jax.numpy as jnp
import numpy as np
from jax import lax
from jax.experimental import pallas as pl
from jax.experimental.pallas import tpu as pltpu
from jax.sharding import PartitionSpec as P

HEAD_DIMENSION = 128


rope_base = 500000.0


def attend_kernel(pos_ref, doc_ref, q_ref, up_ref, kv_ref, cos_ref, sin_ref, qb_ref, dkv_ref,
                  score_sc, grad_sc, q2_sc, up2_sc, dq_sc, dk_sc, dv_sc, where_sm):
    f32 = jnp.float32
    bf16 = jnp.bfloat16
    run = 256
    rows = 2 * run
    scaling = HEAD_DIMENSION ** (-0.5)
    log2e = 1.4426950408889634
    nt = (((1,), (1,)), ((), ()))
    tn = (((0,), (0,)), ((), ()))
    nn = (((1,), (0,)), ((), ()))
    ctx = lax.axis_index("ctx")

    for s in range(16):
        where_sm[lax.shift_right_logical(pos_ref[s * run], 8)] = s
    doc = doc_ref[...]
    starts = [jnp.sum(jnp.where(doc < d, 1.0, 0.0)).astype(jnp.int32) for d in (1, 2, 3)]
    dk_sc[...] = jnp.zeros_like(dk_sc)
    dv_sc[...] = jnp.zeros_like(dv_sc)

    def one_run(t, carry):
        base = pos_ref[(ctx * 2 + t) * run]
        mine = pl.ds(pl.multiple_of(t * run, run), run)
        first = jnp.int32(0)
        for start in starts:
            first = jnp.where(start <= base, jnp.maximum(first, start), first)
        low = lax.shift_right_logical(first, 8)
        high = lax.shift_right_logical(base, 8) + 1
        q_pos = base + (lax.broadcasted_iota(jnp.int32, (1, rows), 1) & (run - 1))
        q_low = jnp.zeros_like(q_pos)
        for start in starts:
            q_low = jnp.where(start <= q_pos, jnp.maximum(q_low, start), q_low)
        for h in range(2):
            q2_sc[h * run:(h + 1) * run, :] = q_ref[mine, h * 128:(h + 1) * 128]
            up2_sc[h * run:(h + 1) * run, :] = up_ref[mine, h * 128:(h + 1) * 128]

        def keys_at(j):
            return pl.ds(pl.multiple_of(where_sm[j] * run, run), run)

        def in_pairs(one, carry):
            at = low
            for size in (4, 2, 1):
                count = (high - at) // size
                carry = lax.fori_loop(
                    0, count, lambda i, c, at=at, size=size: one([at + size * i + n for n in range(size)], c), carry
                )
                at = at + count * size
            return carry

        def scan_scores(js, peak):
            for j in js:
                at = keys_at(j)
                score = lax.dot_general(kv_ref[0, at, :], q2_sc[...], nt, preferred_element_type=f32)
                k_pos = j * run + lax.broadcasted_iota(jnp.int32, (run, 1), 0)
                score = jnp.where((k_pos >= q_low) & (k_pos <= q_pos), score, -1e30)
                score_sc[j - low] = score
                grad_sc[j - low] = lax.dot_general(kv_ref[1, at, :], up2_sc[...], nt, preferred_element_type=f32)
                peak = jnp.maximum(peak, jnp.max(score, axis=0, keepdims=True))
            return peak

        peak = in_pairs(scan_scores, jnp.full((1, rows), -1e30, f32))

        def scan_sums(js, sums):
            total, delta = sums
            for j in js:
                exponent = jnp.exp2((score_sc[j - low] - peak) * (scaling * log2e))
                score_sc[j - low] = exponent
                total = total + jnp.sum(exponent, axis=0, keepdims=True)
                delta = delta + jnp.sum(exponent * grad_sc[j - low], axis=0, keepdims=True)
            return total, delta

        zero = jnp.zeros((1, rows), f32)
        total, delta = in_pairs(scan_sums, (zero, zero))
        inverse = 1.0 / total
        delta = delta * inverse
        dq_sc[...] = jnp.zeros_like(dq_sc)

        def scan_grads(js, c):
            ats = [keys_at(j) for j in js]
            dvs = [dv_sc[at, :] for at in ats]
            dks = [dk_sc[at, :] for at in ats]
            dq = dq_sc[...]
            for n, j in enumerate(js):
                probs = score_sc[j - low] * inverse
                score_grad = (probs * (grad_sc[j - low] - delta)).astype(bf16)
                dvs[n] += lax.dot_general(probs.astype(bf16), up2_sc[...], nn, preferred_element_type=f32)
                dks[n] += lax.dot_general(score_grad, q2_sc[...], nn, preferred_element_type=f32)
                dq += lax.dot_general(kv_ref[0, ats[n], :], score_grad, tn, preferred_element_type=f32)
            dq_sc[...] = dq
            for n, at in enumerate(ats):
                dv_sc[at, :] = dvs[n]
                dk_sc[at, :] = dks[n]
            return c

        in_pairs(scan_grads, 0)
        cosine, sine = cos_ref[mine, :], sin_ref[mine, :]
        for h in range(2):
            grad = dq_sc[:, h * run:(h + 1) * run].T * scaling
            back = grad * cosine - pltpu.roll(grad, 64, 1) * sine
            qb_ref[mine, h * 128:(h + 1) * 128] = back.astype(bf16)
        return carry

    lax.fori_loop(0, 2, one_run, 0)

    def put_out(i, carry):
        at = pl.ds(pl.multiple_of(i * run, run), run)
        dkv_ref[0, at, :] = (dk_sc[at, :] * scaling).astype(bf16)
        dkv_ref[1, at, :] = dv_sc[at, :].astype(bf16)
        return carry

    lax.fori_loop(0, 16, put_out, 0)


def attend(positions, documents, query, upstream, key_value, cosine, sine):
    f32 = jnp.float32
    vmem = pl.BlockSpec(memory_space=pltpu.VMEM)
    return pl.pallas_call(
        attend_kernel,
        out_shape=(
            jax.ShapeDtypeStruct((512, 256), jnp.bfloat16),
            jax.ShapeDtypeStruct((2, 4096, 128), jnp.bfloat16),
        ),
        in_specs=[pl.BlockSpec(memory_space=pltpu.SMEM)] + [vmem] * 6,
        out_specs=(vmem, vmem),
        scratch_shapes=[
            pltpu.VMEM((16, 256, 512), f32),
            pltpu.VMEM((16, 256, 512), f32),
            pltpu.VMEM((512, 128), jnp.bfloat16),
            pltpu.VMEM((512, 128), jnp.bfloat16),
            pltpu.VMEM((128, 512), f32),
            pltpu.VMEM((4096, 128), f32),
            pltpu.VMEM((4096, 128), f32),
            pltpu.SMEM((16,), jnp.int32),
        ],
        compiler_params=pltpu.CompilerParams(vmem_limit_bytes=60 * 1024 * 1024),
        name="attend",
    )(positions, documents.reshape(32, 128), query, upstream, key_value.reshape(2, 4096, 128), cosine, sine)


MESH = pl.DeviceIdType.MESH
VMEM_LIMIT = 60 * 1024 * 1024


def places():
    ctx = lax.axis_index("ctx")
    tp = lax.axis_index("tp")
    y, x_lo = ctx // 2, lax.rem(ctx, 2)
    x_hi, z, core = tp // 8, lax.rem(tp // 2, 4), lax.rem(tp, 2)

    def ctx_at(pair, step):
        return lax.rem(y + step + 4, 4) * 2 + (1 - x_lo if pair else x_lo)

    def tp_at(pair, step, other=0):
        side = 1 - x_hi if pair else x_hi
        return side * 8 + lax.rem(z + step + 4, 4) * 2 + (1 - core if other else core)

    ctx_peers = [(ctx_at(1, 0), tp), (ctx_at(0, 1), tp), (ctx_at(0, -1), tp)]
    tp_peers = [(ctx, tp_at(1, 0)), (ctx, tp_at(0, 1)), (ctx, tp_at(0, -1))]
    twin = (ctx, tp_at(0, 0, 1))
    return ctx, tp, core, ctx_at, tp_at, ctx_peers, tp_peers, twin


def greet(peers):
    barrier = pltpu.get_barrier_semaphore()
    for peer in peers:
        pl.semaphore_signal(barrier, inc=1, device_id=peer, device_id_type=MESH)


def met(peers):
    pl.semaphore_wait(pltpu.get_barrier_semaphore(), len(peers))


def remote(src, dst, send, recv, n, peer):
    return pltpu.make_async_remote_copy(
        src_ref=src, dst_ref=dst, send_sem=send.at[n], recv_sem=recv.at[n],
        device_id=peer, device_id_type=MESH,
    )


class Gather:
    def __init__(self, block, rows, peers, send, recv):
        half = rows // 2

        def part(pair, step, h):
            return block(pair, step).at[pl.ds(h * half, half)]

        pair, after, before = peers
        self.out = [
            (part(0, 0, 0), pair), (part(0, 0, 1), pair), (block(0, 0), after), (block(0, 0), before),
            (part(1, 0, 0), after), (part(1, 0, 0), before), (part(1, 0, 1), after), (part(1, 0, 1), before),
            (part(0, -1, 0), after), (part(0, 1, 1), before),
            (part(1, -1, 0), after), (part(1, 1, 1), before),
        ]
        self.into = [
            part(1, 0, 0), part(1, 0, 1), block(0, -1), block(0, 1),
            part(1, -1, 0), part(1, 1, 0), part(1, -1, 1), part(1, 1, 1),
            part(0, 2, 0), part(0, 2, 1), part(1, 2, 0), part(1, 2, 1),
        ]
        self.sems = (send, recv)

    def start(self, *which):
        for n in which:
            ref, peer = self.out[n]
            remote(ref, ref, *self.sems, n, peer).start()

    def arrived(self, *which):
        for n in which:
            ref = self.into[n]
            remote(ref, ref, *self.sems, n, self.out[n][1]).wait_recv()

    def finish(self):
        for n, (ref, peer) in enumerate(self.out):
            remote(ref, ref, *self.sems, n, peer).wait_send()


class RingGather:
    def __init__(self, block, rows, peers, send, recv):
        half = rows // 2

        def part(pair, step, h):
            return block(pair, step).at[pl.ds(h * half, half)]

        pair, after, before = peers
        self.out = [
            (block(0, 0), after), (block(0, 0), before), (part(0, -1, 0), after), (part(0, 1, 1), before),
            (block(0, 0), pair), (block(0, -1), pair), (block(0, 1), pair), (part(0, 2, 0), pair), (part(0, 2, 1), pair),
        ]
        self.into = [
            block(0, -1), block(0, 1), part(0, 2, 0), part(0, 2, 1),
            block(1, 0), block(1, -1), block(1, 1), part(1, 2, 0), part(1, 2, 1),
        ]
        self.sems = (send, recv)

    start = Gather.start
    arrived = Gather.arrived
    finish = Gather.finish


class Share:
    order = [(0, 0), (1, 0), (0, -1), (0, 1), (1, -1), (1, 1), (0, 2), (1, 2)]

    def __init__(self, mine, theirs, twin, send, recv):
        self.mine = [mine(*p) for p in self.order]
        self.theirs = [theirs(*p) for p in self.order]
        self.twin = twin
        self.sems = (send, recv)

    def start(self, *which):
        for n in which:
            remote(self.mine[n], self.mine[n], *self.sems, n, self.twin).start()

    def arrived(self, *which):
        for n in which or range(8):
            remote(self.theirs[n], self.theirs[n], *self.sems, n, self.twin).wait_recv()

    def finish(self):
        for n, ref in enumerate(self.mine):
            remote(ref, ref, *self.sems, n, self.twin).wait_send()


class Reduce:
    def __init__(self, block, rows, peers, halves, wholes, last, send, recv):
        half = rows // 2
        pair, after, before = peers

        def part(p, step, h):
            return block(p, step).at[pl.ds(h * half, half)]

        self.block = block
        self.part = part
        self.halves, self.wholes, self.last = halves, wholes, last
        self.out = [
            (part(1, 2, 0), halves.at[0], after), (part(1, 2, 1), halves.at[1], before),
            (part(0, 2, 0), halves.at[2], after), (part(0, 2, 1), halves.at[3], before),
            (block(1, 1), wholes.at[0], after), (block(1, -1), wholes.at[1], before),
            (block(0, 1), wholes.at[2], after), (block(0, -1), wholes.at[3], before),
            (block(1, 0), last, pair),
        ]
        self.sems = (send, recv)

    def start(self, *which):
        for n in which:
            src, dst, peer = self.out[n]
            remote(src, dst, *self.sems, n, peer).start()

    def arrived(self, *which):
        for n in which:
            src, dst, peer = self.out[n]
            remote(src, dst, *self.sems, n, peer).wait_recv()

    def finish(self):
        for n in range(9):
            src, dst, peer = self.out[n]
            remote(src, dst, *self.sems, n, peer).wait_send()

    def second(self, p):
        n = 0 if p else 2
        for k, (step, h) in enumerate(((1, 0), (-1, 1))):
            self.arrived(n + k)
            add_into(self.part(p, step, h), self.halves.at[n + k])
            self.start(4 + n + k)

    def third(self):
        self.arrived(4, 5)
        add_into(self.block(1, 0), self.wholes.at[0], self.wholes.at[1])
        self.start(8)

    def total(self, at):
        f32 = jnp.float32
        parts = [self.block(0, 0), self.wholes.at[2], self.wholes.at[3], self.last]
        return sum(r[at].astype(f32) for r in parts)


class PairReduce:
    steps = (2, 1, -1, 0)

    def __init__(self, block, rows, peers, pairs, halves, wholes, send, recv):
        half = rows // 2
        pair, after, before = peers

        def part(p, step, h):
            return block(p, step).at[pl.ds(h * half, half)]

        self.block = block
        self.part = part
        self.pairs, self.halves, self.wholes = pairs, halves, wholes
        self.out = [(block(1, d), pairs.at[n], pair) for n, d in enumerate(self.steps)] + [
            (part(0, 2, 0), halves.at[0], after), (part(0, 2, 1), halves.at[1], before),
            (block(0, 1), wholes.at[0], after), (block(0, -1), wholes.at[1], before),
        ]
        self.sems = (send, recv)

    start = Reduce.start
    arrived = Reduce.arrived

    def finish(self):
        for n, (src, dst, peer) in enumerate(self.out):
            remote(src, dst, *self.sems, n, peer).wait_send()

    def paired(self, *which):
        for n in which:
            self.arrived(n)
            add_into(self.block(0, self.steps[n]), self.pairs.at[n])

    def second(self):
        for k, (step, h) in enumerate(((1, 0), (-1, 1))):
            self.arrived(4 + k)
            add_into(self.part(0, step, h), self.halves.at[k])
            self.start(6 + k)

    def total(self, at):
        f32 = jnp.float32
        self.arrived(3, 6, 7)
        parts = [self.block(0, 0), self.pairs.at[3], self.wholes.at[0], self.wholes.at[1]]
        return sum(r[at].astype(f32) for r in parts)


def add_into(dst, *terms):
    rows, cols = dst.shape
    tile = next(t for t in (256, 128, 64, 32, 16) if rows % t == 0 and (t * cols <= 32768 or t == 16))

    def one(i, carry):
        at = pl.ds(pl.multiple_of(i * tile, tile), tile)
        total = dst[at, :].astype(jnp.float32)
        for t in terms:
            total = total + t[at, :].astype(jnp.float32)
        dst[at, :] = total.astype(dst.dtype)
        return carry

    lax.fori_loop(0, rows // tile, one, 0)


def chosen(t, values):
    at = values[0]
    for n, v in enumerate(values[1:]):
        at = jnp.where(t == n + 1, v, at)
    return at


def project_kernel(pos_ref, freq_ref, tok_ref, wq_ref, wk_ref, q_ref, cos_ref, sin_ref, kv_ref, tok_out, wq_out, wk_out,
                   tbuf, wqbuf, wkbuf, kvbuf, acc, acc_kv, pos_sc, freq_sc, cos_sc, sin_sc, t_send, t_recv, u_send, u_recv, c_send, c_recv, wa_send, wa_recv, wb_send, wb_recv, wk_send, wk_recv,
                   k_send, k_recv, r_send, r_recv, f_send, f_recv, local, outs):
    f32 = jnp.float32
    bf16 = jnp.bfloat16
    ctx, tp, core, ctx_at, tp_at, ctx_peers, tp_peers, twin = places()
    copies = [
        pltpu.make_async_copy(wk_ref, wkbuf.at[ctx], local.at[0]),
        pltpu.make_async_copy(tok_ref, tbuf.at[tp], local.at[1]),
        pltpu.make_async_copy(wq_ref, wqbuf.at[ctx], local.at[2]),
    ]
    small = [pltpu.make_async_copy(pos_ref, pos_sc, local.at[6]), pltpu.make_async_copy(freq_ref, freq_sc, local.at[7])]
    greet(ctx_peers + tp_peers + [twin])
    for c in copies + small:
        c.start()
    met(ctx_peers + tp_peers + [twin])
    toks = Gather(lambda p, d: tbuf.at[tp_at(p, d), :, pl.ds(0, 3584)], 32, tp_peers, t_send, t_recv)
    round_toks = RingGather(lambda p, d: tbuf.at[tp_at(p, d), :, pl.ds(3584, 512)], 32, tp_peers, u_send, u_recv)
    tshare = Share(lambda p, d: tbuf.at[tp_at(p, d)], lambda p, d: tbuf.at[tp_at(p, d, 1)], twin, c_send, c_recv)
    wqa = Gather(lambda p, d: wqbuf.at[ctx_at(p, d), pl.ds(0, 320)], 320, ctx_peers, wa_send, wa_recv)
    wqb = RingGather(lambda p, d: wqbuf.at[ctx_at(p, d), pl.ds(320, 192)], 192, ctx_peers, wb_send, wb_recv)
    wk = Gather(lambda p, d: wkbuf.at[ctx_at(p, d)], 512, ctx_peers, wk_send, wk_recv)
    for c in copies:
        c.wait()
    toks.start(0, 1)
    wk.start(2, 3)
    round_toks.start(0, 1)
    toks.start(2, 3)
    round_toks.start(4)
    wk.start(0, 1)
    wqb.start(0, 1)
    wqa.start(2, 3)
    tshare.start(0)

    row = lax.broadcasted_iota(jnp.int32, (512, 128), 0)
    for c in small:
        c.wait()
    begin = [pos_sc[pl.ds(ctx * 4 + 2 * t, 1), :][:, 0:1] for t in range(2)]
    place = jnp.where(row < 256, begin[0], begin[1]) + (row & 255)
    angle = place.astype(f32) * freq_sc[...]
    cos_sc[...] = jnp.cos(angle)
    sine = jnp.sin(angle)
    sin_sc[...] = jnp.where(lax.broadcasted_iota(jnp.int32, (512, 128), 1) < 64, -sine, sine)
    acc[...] = jnp.zeros_like(acc)

    round_toks.arrived(0, 1)
    round_toks.start(2, 3, 5, 6)
    wk.arrived(2, 3)
    wk.start(8, 9)
    toks.arrived(0)
    toks.start(4, 5)
    toks.arrived(1)
    toks.start(6, 7)
    toks.arrived(2, 3)
    toks.start(8, 9)
    tshare.start(2, 3)
    round_toks.arrived(4)
    tshare.start(1)
    wqa.arrived(2, 3)
    round_toks.arrived(2, 3)
    round_toks.start(7, 8)
    wqa.start(0, 1)
    wqa.start(8, 9)
    wqb.start(4)
    wk.arrived(0, 1)
    wk.start(4, 5, 6, 7)
    wqb.arrived(0, 1)
    wqb.start(2, 3)
    toks.arrived(4)
    toks.start(10)
    toks.arrived(7)
    toks.start(11)
    toks.arrived(5, 6)
    round_toks.arrived(5, 6)
    tshare.start(4, 5)
    toks.arrived(8, 9)
    tshare.start(6)
    wk.arrived(4)
    wk.start(10)
    wk.arrived(7)
    wk.start(11)
    wqb.start(5, 6)
    wqb.arrived(2, 3)
    wqb.start(7, 8)
    toks.arrived(10, 11)
    round_toks.arrived(7, 8)
    tshare.start(7)
    wk.arrived(5, 6, 8, 9, 10, 11)
    out_wk = pltpu.make_async_copy(wkbuf, wk_out, local.at[3])
    out_wk.start()
    out_cos = pltpu.make_async_copy(cos_sc, cos_ref, local.at[6])
    out_sin = pltpu.make_async_copy(sin_sc, sin_ref, local.at[7])
    out_cos.start()
    out_sin.start()
    wqa.arrived(0, 1)
    wqa.start(4, 5, 6, 7)
    tshare.arrived()
    out_tok = pltpu.make_async_copy(tbuf, tok_out, local.at[4])
    out_tok.start()

    def multiply(total, wbuf, blocks):
        def one(i, carry):
            c = chosen(i // 2, blocks)
            m = lax.rem(i, 2)
            cols = pl.ds(pl.multiple_of(c * 512, 512), 512)
            left = tbuf[pl.ds(m * 8, 8), :, cols].reshape(256, 512)
            rows = pl.ds(pl.multiple_of(m * 256, 256), 256)
            total[rows, :] += jnp.dot(left, wbuf[c], preferred_element_type=f32)
            return carry

        lax.fori_loop(0, 2 * len(blocks), one, 0)

    def keyval(m, carry):
        left = tbuf[pl.ds(m * 8, 8)].reshape(256, 4096)
        rows = pl.ds(pl.multiple_of(m * 256, 256), 256)
        acc_kv[rows, :] = jnp.dot(left, wkbuf[...].reshape(4096, 128), preferred_element_type=f32)
        return carry

    lax.fori_loop(0, 2, keyval, 0)
    cosine, sine = cos_sc[...], sin_sc[...]
    held = acc_kv[...].astype(bf16).astype(f32)
    turned = held * cosine + pltpu.roll(held, 64, 1) * sine
    kvbuf[core, ctx] = jnp.where(core == 0, turned, held).astype(bf16)
    keys = Gather(lambda p, d: kvbuf.at[core, ctx_at(p, d), pl.ds(0, 256)], 256, ctx_peers, k_send, k_recv)
    round_keys = RingGather(lambda p, d: kvbuf.at[core, ctx_at(p, d), pl.ds(256, 256)], 256, ctx_peers, r_send, r_recv)
    kshare = Share(lambda p, d: kvbuf.at[core, ctx_at(p, d)], lambda p, d: kvbuf.at[1 - core, ctx_at(p, d)], twin, f_send, f_recv)
    keys.start(0, 1)
    round_keys.start(0, 1)
    keys.start(2, 3)
    round_keys.start(4)
    kshare.start(0)
    wqa.arrived(8, 9)
    multiply(acc, wqbuf, [ctx_at(0, 0), ctx_at(0, -1), ctx_at(0, 1), ctx_at(0, 2)])
    round_keys.arrived(0, 1)
    round_keys.start(2, 3, 5, 6)
    keys.arrived(0, 1)
    keys.start(4, 5, 6, 7)
    keys.arrived(2, 3)
    keys.start(8, 9)
    kshare.start(2, 3)
    round_keys.arrived(4)
    kshare.start(1)
    wqa.arrived(4)
    wqa.start(10)
    wqa.arrived(7)
    wqa.start(11)
    wqa.arrived(5, 6)
    wqb.arrived(4, 5, 6)
    multiply(acc, wqbuf, [ctx_at(1, 0), ctx_at(1, -1), ctx_at(1, 1)])
    round_keys.arrived(2, 3)
    round_keys.start(7, 8)
    keys.arrived(4)
    keys.start(10)
    keys.arrived(7)
    keys.start(11)
    wqa.arrived(10, 11)
    wqb.arrived(7, 8)
    out_wq = pltpu.make_async_copy(wqbuf, wq_out, local.at[5])
    out_wq.start()
    multiply(acc, wqbuf, [ctx_at(1, 2)])
    for h in range(2):
        raw = acc[:, h * 128:(h + 1) * 128]
        q_ref[:, h * 128:(h + 1) * 128] = (raw * cosine + pltpu.roll(raw, 64, 1) * sine).astype(bf16)
    def block_out(mine, n):
        p, d = Share.order[n]
        plane = core if mine else 1 - core
        at = ctx_at(p, d)
        return pltpu.make_async_copy(kvbuf.at[plane, at], kv_ref.at[plane, at], outs.at[8 * mine + n])

    for n in range(4):
        block_out(1, n).start()
    keys.arrived(5, 6)
    round_keys.arrived(5, 6)
    kshare.start(4, 5)
    keys.arrived(8, 9)
    kshare.start(6)
    for n in (4, 5, 6):
        block_out(1, n).start()
    keys.arrived(10, 11)
    round_keys.arrived(7, 8)
    kshare.start(7)
    block_out(1, 7).start()
    for n in range(8):
        kshare.arrived(n)
        block_out(0, n).start()
    toks.finish()
    round_toks.finish()
    tshare.finish()
    wqa.finish()
    wqb.finish()
    wk.finish()
    keys.finish()
    round_keys.finish()
    kshare.finish()
    out_tok.wait()
    out_wq.wait()
    out_wk.wait()
    out_cos.wait()
    out_sin.wait()
    for n in range(8):
        block_out(0, n).wait()
        block_out(1, n).wait()


def project(positions, frequency, tokens, w_query, w_keyval):
    bf16 = jnp.bfloat16
    f32 = jnp.float32
    vmem = pl.BlockSpec(memory_space=pltpu.VMEM)
    hbm = pl.BlockSpec(memory_space=pltpu.HBM)
    dma = pltpu.SemaphoreType.DMA
    return pl.pallas_call(
        project_kernel,
        out_shape=(
            jax.ShapeDtypeStruct((512, 256), bf16),
            jax.ShapeDtypeStruct((512, 128), f32),
            jax.ShapeDtypeStruct((512, 128), f32),
            jax.ShapeDtypeStruct((2, 8, 512, 128), bf16),
            jax.ShapeDtypeStruct((16, 32, 4096), bf16),
            jax.ShapeDtypeStruct((8, 512, 256), bf16),
            jax.ShapeDtypeStruct((8, 512, 128), bf16),
        ),
        in_specs=[hbm] * 5,
        out_specs=(vmem, hbm, hbm, hbm, hbm, hbm, hbm),
        scratch_shapes=[
            pltpu.VMEM((16, 32, 4096), bf16),
            pltpu.VMEM((8, 512, 256), bf16),
            pltpu.VMEM((8, 512, 128), bf16),
            pltpu.VMEM((2, 8, 512, 128), bf16),
            pltpu.VMEM((512, 256), f32),
            pltpu.VMEM((512, 128), f32),
            pltpu.VMEM((32, 128), jnp.int32),
            pltpu.VMEM((1, 128), f32),
            pltpu.VMEM((512, 128), f32),
            pltpu.VMEM((512, 128), f32),
            dma((12,)), dma((12,)), dma((9,)), dma((9,)), dma((8,)), dma((8,)),
            dma((12,)), dma((12,)), dma((9,)), dma((9,)), dma((12,)), dma((12,)),
            dma((12,)), dma((12,)), dma((9,)), dma((9,)), dma((8,)), dma((8,)), dma((8,)), dma((16,)),
        ],
        compiler_params=pltpu.CompilerParams(collective_id=0, has_side_effects=True, vmem_limit_bytes=VMEM_LIMIT),
        name="project",
    )(positions.reshape(32, 128), frequency, tokens, w_query, w_keyval)


TOKEN_PARTS = ((0, 2), (2, 3), (5, 3))


def reduce_kernel(tok_ref, wq_ref, wk_ref, qb_ref, dkv_ref, cos_ref, sin_ref, tg_ref, sum_ref,
                  tbuf, wqbuf, wkbuf, kv, kv_in, kv_halves, kv_wholes, kv_last, kp_pairs, kp_halves, kp_wholes, turned_q, kvg,
                  wq, wq_halves, wq_wholes, wq_last, wp_pairs, wp_halves, wp_wholes, wk, wk_halves, wk_wholes, wk_last,
                  qb, cos_sc, sin_sc, px, parts_out, parts_in, parts_halves, parts_wholes, parts_last, pair_parts,
                  k_send, k_recv, kp_send, kp_recv, wp_send, wp_recv, wq_send, wq_recv, wk_send, wk_recv,
                  t_send, t_recv, e_send, e_recv, local):
    f32 = jnp.float32
    bf16 = jnp.bfloat16
    nt = (((1,), (1,)), ((), ()))
    ctx, tp, core, ctx_at, tp_at, ctx_peers, tp_peers, twin = places()
    copies = [
        pltpu.make_async_copy(dkv_ref.at[core], kv, local.at[0]),
        pltpu.make_async_copy(tok_ref, tbuf, local.at[1]),
        pltpu.make_async_copy(wq_ref, wqbuf, local.at[2]),
        pltpu.make_async_copy(wk_ref, wkbuf, local.at[3]),
        pltpu.make_async_copy(cos_ref, cos_sc, local.at[4]),
        pltpu.make_async_copy(sin_ref, sin_sc, local.at[5]),
    ]
    first = pltpu.make_async_copy(qb_ref, qb, local.at[6])
    greet(ctx_peers + tp_peers + [twin])
    first.start()
    for c in copies:
        c.start()
    met(ctx_peers + tp_peers + [twin])
    side = tp // 8
    steps = (2, 1, -1, 0)

    def ring_of(d):
        return lax.rem(ctx // 2 + d + 4, 4)

    def pair_of(d):
        return pl.ds(pl.multiple_of(ring_of(d) * 2, 2), 2)

    swap = [
        remote(dkv_ref.at[1 - core, pair_of(d)], kv_in.at[pair_of(d)], e_send, e_recv, 12 + n, twin)
        for n, d in enumerate(steps)
    ]
    for s in swap:
        s.start()
    first.wait()
    turned_q[...] = qb[...].T
    order = [ctx_at(p, d) for d in steps for p in (1, 0)]

    def tok_cols(c):
        return tbuf[:, :, pl.ds(pl.multiple_of(c * 512, 512), 512)].reshape(512, 512)

    def query_terms(i, carry):
        c = chosen(i, order)
        wq[c] = jnp.dot(turned_q[...], tok_cols(c), preferred_element_type=f32).astype(bf16)
        return carry

    keys = Reduce(
        lambda p, d: kv.at[ctx_at(p, d), pl.ds(0, 256)], 256, ctx_peers, kv_halves, kv_wholes, kv_last, k_send, k_recv
    )
    pair_keys = PairReduce(
        lambda p, d: kv.at[ctx_at(p, d), pl.ds(256, 256)], 256, ctx_peers, kp_pairs, kp_halves, kp_wholes, kp_send, kp_recv
    )
    wq_sum = Reduce(
        lambda p, d: wq.at[ctx_at(p, d), pl.ds(0, 128)], 128, ctx_peers, wq_halves, wq_wholes, wq_last, wq_send, wq_recv
    )
    wp_sum = PairReduce(
        lambda p, d: wq.at[ctx_at(p, d), pl.ds(128, 128)], 128, ctx_peers, wp_pairs, wp_halves, wp_wholes, wp_send, wp_recv
    )
    wk_sum = Reduce(lambda p, d: wk.at[ctx_at(p, d)], 128, ctx_peers, wk_halves, wk_wholes, wk_last, wk_send, wk_recv)
    copies[1].wait()
    lax.fori_loop(0, 1, query_terms, 0)
    wq_sum.start(0, 1)
    wp_sum.start(0)
    copies[0].wait()
    for n, d in enumerate(steps):
        swap[n].wait_recv()
        for p in (1, 0):
            add_into(kv.at[ctx_at(p, d)], kv_in.at[ctx_at(p, d)])
        pair_keys.start(n)
        if d == 2:
            keys.start(0, 1, 2, 3)
    lax.fori_loop(1, 2, query_terms, 0)
    wq_sum.start(2, 3)
    lax.fori_loop(2, 4, query_terms, 0)
    wp_sum.start(1)
    keys.second(1)
    keys.second(0)
    pair_keys.paired(0)
    pair_keys.start(4, 5)
    lax.fori_loop(4, 6, query_terms, 0)
    pair_keys.paired(1, 2)
    pair_keys.second()
    wq_sum.second(1)
    keys.third()
    lax.fori_loop(6, 8, query_terms, 0)
    wp_sum.start(2, 3)
    copies[2].wait()

    def query_part(c, carry):
        px[c] = lax.dot_general(qb[...], wqbuf[c], nt, preferred_element_type=f32)
        return carry

    lax.fori_loop(0, 8, query_part, 0)
    wq_sum.second(0)
    wp_sum.paired(0)
    wp_sum.start(4, 5)
    copies[3].wait()
    keys.arrived(6, 7, 8)
    total = jnp.concatenate([keys.total(...), pair_keys.total(...)], axis=0)
    copies[4].wait()
    copies[5].wait()
    back = total * cos_sc[...] - pltpu.roll(total, 64, 1) * sin_sc[...]
    total = jnp.where(core == 0, back, total)
    kvg[...] = total.astype(bf16)

    def level_of(d):
        return lax.rem(tp // 2 + d + 4, 4)

    count = len(TOKEN_PARTS)
    swaps = [
        [
            remote(parts_out[h].at[1 - core, level_of(d)], parts_in[h].at[level_of(d)], e_send, e_recv, 4 * h + n, twin)
            for n, d in enumerate(steps)
        ]
        for h in range(count)
    ]

    def tg_block(h):
        return lambda p, d: parts_out[h].at[core, level_of(d), 1 - side if p else side]

    toks = [
        Reduce(
            tg_block(h), 32, tp_peers, parts_halves[h], parts_wholes[h], parts_last[h], t_send.at[h], t_recv.at[h]
        )
        for h in range(2)
    ]
    pair_toks = PairReduce(
        tg_block(2), 32, tp_peers, pair_parts, parts_halves[2], parts_wholes[2], t_send.at[2], t_recv.at[2]
    )

    def merged(h, *which):
        for n in which:
            swaps[h][n].wait_recv()
            for p in (1, 0):
                add_into(tg_block(h)(p, steps[n]), parts_in[h].at[level_of(steps[n]), 1 - side if p else side])

    def keyval_part(h):
        first, tiles = TOKEN_PARTS[h]

        def one(c, carry):
            part = px[c] + lax.dot_general(kvg[...], wkbuf[c], nt, preferred_element_type=f32)
            part = part.astype(bf16).reshape(2, 4, 2, 32, 512)
            cols = pl.ds(pl.multiple_of((c - first) * 512, 512), 512)
            for s in range(2):
                for level in range(4):
                    for k in range(2):
                        parts_out[h][k, level, s, :, cols] = part[s, level, k]
            return carry

        lax.fori_loop(first, first + tiles, one, 0)
        for s in swaps[h]:
            s.start()

    def keyval_terms(i, carry):
        c = chosen(i, order)
        wk[c] = jnp.dot(turned_q[0:128, :], tok_cols(c), preferred_element_type=f32).astype(bf16)
        return carry

    keyval_part(0)
    turned_q[0:128, :] = total.T.astype(bf16)
    keyval_part(2)
    merged(0, 0)
    toks[0].start(0, 1, 2, 3)
    lax.fori_loop(0, 2, keyval_terms, 0)
    wk_sum.start(0, 1, 2, 3)
    for n in range(4):
        merged(2, n)
        pair_toks.start(n)
    keyval_part(1)
    merged(1, 0)
    toks[1].start(0, 1, 2, 3)
    merged(0, 1, 2, 3)
    toks[0].second(1)
    toks[0].second(0)
    wp_sum.paired(1, 2)
    wp_sum.second()
    lax.fori_loop(2, 8, keyval_terms, 0)
    pair_toks.paired(0)
    pair_toks.start(4, 5)
    merged(1, 1, 2, 3)
    toks[1].second(1)
    toks[1].second(0)
    wk_sum.second(1)
    wk_sum.second(0)
    wq_sum.third()
    pair_toks.paired(1, 2)
    pair_toks.second()
    toks[0].third()
    toks[1].third()
    wk_sum.third()
    wq_sum.arrived(6, 7, 8)
    sum_ref[0:128, :] = wq_sum.total(...)
    sum_ref[128:256, :] = wp_sum.total(...)
    for h in (0, 2, 1):
        first, tiles = TOKEN_PARTS[h]
        if h < 2:
            toks[h].arrived(6, 7, 8)
        part = toks[h] if h < 2 else pair_toks
        tg_ref[:, first * 512:(first + tiles) * 512] = part.total(...).astype(bf16)
    wk_sum.arrived(6, 7, 8)
    sum_ref[256:384, :] = wk_sum.total(...)
    for s in swap + sum(swaps, []):
        s.wait_send()
    for r in [keys, pair_keys, wq_sum, wp_sum, wk_sum, pair_toks] + toks:
        r.finish()


def reduce(tok_full, wq_full, wk_full, query_back, dkv, cosine, sine):
    bf16 = jnp.bfloat16
    f32 = jnp.float32
    vmem = pl.BlockSpec(memory_space=pltpu.VMEM)
    hbm = pl.BlockSpec(memory_space=pltpu.HBM)
    dma = pltpu.SemaphoreType.DMA
    return pl.pallas_call(
        reduce_kernel,
        out_shape=(
            jax.ShapeDtypeStruct((32, 4096), bf16),
            jax.ShapeDtypeStruct((384, 512), f32),
        ),
        in_specs=[hbm] * 7,
        out_specs=(vmem, vmem),
        scratch_shapes=[
            pltpu.VMEM((16, 32, 4096), bf16),
            pltpu.VMEM((8, 512, 256), bf16),
            pltpu.VMEM((8, 512, 128), bf16),
            pltpu.VMEM((8, 512, 128), bf16),
            pltpu.VMEM((8, 512, 128), bf16),
            pltpu.VMEM((4, 128, 128), bf16),
            pltpu.VMEM((4, 256, 128), bf16),
            pltpu.VMEM((256, 128), bf16),
            pltpu.VMEM((4, 256, 128), bf16),
            pltpu.VMEM((2, 128, 128), bf16),
            pltpu.VMEM((2, 256, 128), bf16),
            pltpu.VMEM((256, 512), bf16),
            pltpu.VMEM((512, 128), bf16),
            pltpu.VMEM((8, 256, 512), bf16),
            pltpu.VMEM((4, 64, 512), bf16),
            pltpu.VMEM((4, 128, 512), bf16),
            pltpu.VMEM((128, 512), bf16),
            pltpu.VMEM((4, 128, 512), bf16),
            pltpu.VMEM((2, 64, 512), bf16),
            pltpu.VMEM((2, 128, 512), bf16),
            pltpu.VMEM((8, 128, 512), bf16),
            pltpu.VMEM((4, 64, 512), bf16),
            pltpu.VMEM((4, 128, 512), bf16),
            pltpu.VMEM((128, 512), bf16),
            pltpu.VMEM((512, 256), bf16),
            pltpu.VMEM((512, 128), f32),
            pltpu.VMEM((512, 128), f32),
            pltpu.VMEM((8, 512, 512), f32),
            [pltpu.VMEM((2, 4, 2, 32, 512 * n), bf16) for _, n in TOKEN_PARTS],
            [pltpu.VMEM((4, 2, 32, 512 * n), bf16) for _, n in TOKEN_PARTS],
            [pltpu.VMEM((4, 16, 512 * n), bf16) for _, n in TOKEN_PARTS],
            [pltpu.VMEM((4, 32, 512 * n), bf16) for _, n in TOKEN_PARTS],
            [pltpu.VMEM((32, 512 * n), bf16) for _, n in TOKEN_PARTS],
            pltpu.VMEM((4, 32, 512 * TOKEN_PARTS[2][1]), bf16),
            dma((9,)), dma((9,)), dma((8,)), dma((8,)), dma((8,)), dma((8,)),
            dma((9,)), dma((9,)), dma((9,)), dma((9,)), dma((3, 9)), dma((3, 9)),
            dma((16,)), dma((16,)), dma((7,)),
        ],
        compiler_params=pltpu.CompilerParams(collective_id=1, has_side_effects=True, vmem_limit_bytes=VMEM_LIMIT),
        name="reduce",
    )(tok_full, wq_full, wk_full, query_back, dkv, cosine, sine)


def finish_kernel(tg_ref, sum_ref, token_ref, gq_ref, gk_ref):
    token_ref[...] = tg_ref[...]
    gq_ref[...] = sum_ref[0:256, :].T
    gk_ref[...] = sum_ref[256:384, :].T


def finish(token_grad, weight_grad):
    return pl.pallas_call(
        finish_kernel,
        grid=(2,),
        out_shape=(
            jax.ShapeDtypeStruct((32, 4096), jnp.bfloat16),
            jax.ShapeDtypeStruct((512, 256), jnp.float32),
            jax.ShapeDtypeStruct((512, 128), jnp.float32),
        ),
        in_specs=[pl.BlockSpec((32, 2048), lambda i: (0, i)), pl.BlockSpec((384, 256), lambda i: (0, i))],
        out_specs=(
            pl.BlockSpec((32, 2048), lambda i: (0, i)),
            pl.BlockSpec((256, 256), lambda i: (i, 0)),
            pl.BlockSpec((256, 128), lambda i: (i, 0)),
        ),
        name="finish",
    )(token_grad, weight_grad)


def shards(tokens, upstream, w_query, w_keyval, positions, documents):
    powers = np.arange(HEAD_DIMENSION // 2, dtype=np.float32) * np.float32(2.0 / HEAD_DIMENSION)
    frequency = np.power(np.float32(rope_base), -powers).astype(np.float32)
    frequency = jnp.asarray(np.concatenate([frequency, frequency])[None, :])
    query, cosine, sine, key_value, tok_full, wq_full, wk_full = project(positions, frequency, tokens, w_query, w_keyval)
    query_back, dkv = attend(positions, documents, query, upstream, key_value, cosine, sine)
    return finish(*reduce(tok_full, wq_full, wk_full, query_back, dkv.reshape(2, 8, 512, 128), cosine, sine))


def solution(mesh):
    return jax.shard_map(
        shards,
        mesh=mesh,
        in_specs=(P(("ctx", "tp"), None), P("ctx", "tp"), P("ctx", "tp"), P("ctx", "tp"), P(), P()),
        out_specs=(P(("ctx", "tp"), None), P("ctx", "tp"), P("ctx", "tp")),
        check_vma=False,
    )
```

```python
import jax
import jax.numpy as jnp
import numpy as np
from jax import lax
from jax.experimental import pallas as pl
from jax.experimental.pallas import tpu as pltpu
from jax.sharding import PartitionSpec as P

HEAD_DIMENSION = 128


rope_base = 500000.0


def attend_kernel(pos_ref, doc_ref, q_ref, up_ref, kv_ref, cos_ref, sin_ref, qb_ref, dkv_ref,
                  score_sc, grad_sc, q2_sc, up2_sc, dq_sc, dk_sc, dv_sc, where_sm):
    f32 = jnp.float32
    bf16 = jnp.bfloat16
    run = 256
    rows = 2 * run
    scaling = HEAD_DIMENSION ** (-0.5)
    log2e = 1.4426950408889634
    nt = (((1,), (1,)), ((), ()))
    tn = (((0,), (0,)), ((), ()))
    nn = (((1,), (0,)), ((), ()))
    ctx = lax.axis_index("ctx")

    for s in range(16):
        where_sm[lax.shift_right_logical(pos_ref[s * run], 8)] = s
    doc = doc_ref[...]
    starts = [jnp.sum(jnp.where(doc < d, 1.0, 0.0)).astype(jnp.int32) for d in (1, 2, 3)]
    dk_sc[...] = jnp.zeros_like(dk_sc)
    dv_sc[...] = jnp.zeros_like(dv_sc)

    def one_run(t, carry):
        base = pos_ref[(ctx * 2 + t) * run]
        mine = pl.ds(pl.multiple_of(t * run, run), run)
        first = jnp.int32(0)
        for start in starts:
            first = jnp.where(start <= base, jnp.maximum(first, start), first)
        low = lax.shift_right_logical(first, 8)
        high = lax.shift_right_logical(base, 8) + 1
        q_pos = base + (lax.broadcasted_iota(jnp.int32, (1, rows), 1) & (run - 1))
        q_low = jnp.zeros_like(q_pos)
        for start in starts:
            q_low = jnp.where(start <= q_pos, jnp.maximum(q_low, start), q_low)
        for h in range(2):
            q2_sc[h * run:(h + 1) * run, :] = q_ref[mine, h * 128:(h + 1) * 128]
            up2_sc[h * run:(h + 1) * run, :] = up_ref[mine, h * 128:(h + 1) * 128]

        def keys_at(j):
            return pl.ds(pl.multiple_of(where_sm[j] * run, run), run)

        def in_pairs(one, carry):
            at = low
            for size in (4, 2, 1):
                count = (high - at) // size
                carry = lax.fori_loop(
                    0, count, lambda i, c, at=at, size=size: one([at + size * i + n for n in range(size)], c), carry
                )
                at = at + count * size
            return carry

        def scan_scores(js, peak):
            for j in js:
                at = keys_at(j)
                score = lax.dot_general(kv_ref[0, at, :], q2_sc[...], nt, preferred_element_type=f32)
                k_pos = j * run + lax.broadcasted_iota(jnp.int32, (run, 1), 0)
                score = jnp.where((k_pos >= q_low) & (k_pos <= q_pos), score, -1e30)
                score_sc[j - low] = score
                grad_sc[j - low] = lax.dot_general(kv_ref[1, at, :], up2_sc[...], nt, preferred_element_type=f32)
                peak = jnp.maximum(peak, jnp.max(score, axis=0, keepdims=True))
            return peak

        peak = in_pairs(scan_scores, jnp.full((1, rows), -1e30, f32))

        def scan_sums(js, sums):
            total, delta = sums
            for j in js:
                exponent = jnp.exp2((score_sc[j - low] - peak) * (scaling * log2e))
                score_sc[j - low] = exponent
                total = total + jnp.sum(exponent, axis=0, keepdims=True)
                delta = delta + jnp.sum(exponent * grad_sc[j - low], axis=0, keepdims=True)
            return total, delta

        zero = jnp.zeros((1, rows), f32)
        total, delta = in_pairs(scan_sums, (zero, zero))
        inverse = 1.0 / total
        delta = delta * inverse
        dq_sc[...] = jnp.zeros_like(dq_sc)

        def scan_grads(js, c):
            ats = [keys_at(j) for j in js]
            dvs = [dv_sc[at, :] for at in ats]
            dks = [dk_sc[at, :] for at in ats]
            dq = dq_sc[...]
            for n, j in enumerate(js):
                probs = score_sc[j - low] * inverse
                score_grad = (probs * (grad_sc[j - low] - delta)).astype(bf16)
                dvs[n] += lax.dot_general(probs.astype(bf16), up2_sc[...], nn, preferred_element_type=f32)
                dks[n] += lax.dot_general(score_grad, q2_sc[...], nn, preferred_element_type=f32)
                dq += lax.dot_general(kv_ref[0, ats[n], :], score_grad, tn, preferred_element_type=f32)
            dq_sc[...] = dq
            for n, at in enumerate(ats):
                dv_sc[at, :] = dvs[n]
                dk_sc[at, :] = dks[n]
            return c

        in_pairs(scan_grads, 0)
        cosine, sine = cos_ref[mine, :], sin_ref[mine, :]
        for h in range(2):
            grad = dq_sc[:, h * run:(h + 1) * run].T * scaling
            back = grad * cosine - pltpu.roll(grad, 64, 1) * sine
            qb_ref[mine, h * 128:(h + 1) * 128] = back.astype(bf16)
        return carry

    lax.fori_loop(0, 2, one_run, 0)

    def put_out(i, carry):
        at = pl.ds(pl.multiple_of(i * run, run), run)
        dkv_ref[0, at, :] = (dk_sc[at, :] * scaling).astype(bf16)
        dkv_ref[1, at, :] = dv_sc[at, :].astype(bf16)
        return carry

    lax.fori_loop(0, 16, put_out, 0)


def attend(positions, documents, query, upstream, key_value, cosine, sine):
    f32 = jnp.float32
    vmem = pl.BlockSpec(memory_space=pltpu.VMEM)
    return pl.pallas_call(
        attend_kernel,
        out_shape=(
            jax.ShapeDtypeStruct((512, 256), jnp.bfloat16),
            jax.ShapeDtypeStruct((2, 4096, 128), jnp.bfloat16),
        ),
        in_specs=[pl.BlockSpec(memory_space=pltpu.SMEM)] + [vmem] * 6,
        out_specs=(vmem, vmem),
        scratch_shapes=[
            pltpu.VMEM((16, 256, 512), f32),
            pltpu.VMEM((16, 256, 512), f32),
            pltpu.VMEM((512, 128), jnp.bfloat16),
            pltpu.VMEM((512, 128), jnp.bfloat16),
            pltpu.VMEM((128, 512), f32),
            pltpu.VMEM((4096, 128), f32),
            pltpu.VMEM((4096, 128), f32),
            pltpu.SMEM((16,), jnp.int32),
        ],
        compiler_params=pltpu.CompilerParams(vmem_limit_bytes=60 * 1024 * 1024),
        name="attend",
    )(positions, documents.reshape(32, 128), query, upstream, key_value.reshape(2, 4096, 128), cosine, sine)


MESH = pl.DeviceIdType.MESH
VMEM_LIMIT = 60 * 1024 * 1024


def places():
    ctx = lax.axis_index("ctx")
    tp = lax.axis_index("tp")
    y, x_lo = ctx // 2, lax.rem(ctx, 2)
    x_hi, z, core = tp // 8, lax.rem(tp // 2, 4), lax.rem(tp, 2)

    def ctx_at(pair, step):
        return lax.rem(y + step + 4, 4) * 2 + (1 - x_lo if pair else x_lo)

    def tp_at(pair, step, other=0):
        side = 1 - x_hi if pair else x_hi
        return side * 8 + lax.rem(z + step + 4, 4) * 2 + (1 - core if other else core)

    ctx_peers = [(ctx_at(1, 0), tp), (ctx_at(0, 1), tp), (ctx_at(0, -1), tp)]
    tp_peers = [(ctx, tp_at(1, 0)), (ctx, tp_at(0, 1)), (ctx, tp_at(0, -1))]
    twin = (ctx, tp_at(0, 0, 1))
    return ctx, tp, core, ctx_at, tp_at, ctx_peers, tp_peers, twin


def greet(peers):
    barrier = pltpu.get_barrier_semaphore()
    for peer in peers:
        pl.semaphore_signal(barrier, inc=1, device_id=peer, device_id_type=MESH)


def met(peers):
    pl.semaphore_wait(pltpu.get_barrier_semaphore(), len(peers))


def remote(src, dst, send, recv, n, peer):
    return pltpu.make_async_remote_copy(
        src_ref=src, dst_ref=dst, send_sem=send.at[n], recv_sem=recv.at[n],
        device_id=peer, device_id_type=MESH,
    )


class Gather:
    def __init__(self, block, rows, peers, send, recv):
        half = rows // 2

        def part(pair, step, h):
            return block(pair, step).at[pl.ds(h * half, half)]

        pair, after, before = peers
        self.out = [
            (part(0, 0, 0), pair), (part(0, 0, 1), pair), (block(0, 0), after), (block(0, 0), before),
            (part(1, 0, 0), after), (part(1, 0, 0), before), (part(1, 0, 1), after), (part(1, 0, 1), before),
            (part(0, -1, 0), after), (part(0, 1, 1), before),
            (part(1, -1, 0), after), (part(1, 1, 1), before),
        ]
        self.into = [
            part(1, 0, 0), part(1, 0, 1), block(0, -1), block(0, 1),
            part(1, -1, 0), part(1, 1, 0), part(1, -1, 1), part(1, 1, 1),
            part(0, 2, 0), part(0, 2, 1), part(1, 2, 0), part(1, 2, 1),
        ]
        self.sems = (send, recv)

    def start(self, *which):
        for n in which:
            ref, peer = self.out[n]
            remote(ref, ref, *self.sems, n, peer).start()

    def arrived(self, *which):
        for n in which:
            ref = self.into[n]
            remote(ref, ref, *self.sems, n, self.out[n][1]).wait_recv()

    def finish(self):
        for n, (ref, peer) in enumerate(self.out):
            remote(ref, ref, *self.sems, n, peer).wait_send()


class RingGather:
    def __init__(self, block, rows, peers, send, recv):
        half = rows // 2

        def part(pair, step, h):
            return block(pair, step).at[pl.ds(h * half, half)]

        pair, after, before = peers
        self.out = [
            (block(0, 0), after), (block(0, 0), before), (part(0, -1, 0), after), (part(0, 1, 1), before),
            (block(0, 0), pair), (block(0, -1), pair), (block(0, 1), pair), (part(0, 2, 0), pair), (part(0, 2, 1), pair),
        ]
        self.into = [
            block(0, -1), block(0, 1), part(0, 2, 0), part(0, 2, 1),
            block(1, 0), block(1, -1), block(1, 1), part(1, 2, 0), part(1, 2, 1),
        ]
        self.sems = (send, recv)

    start = Gather.start
    arrived = Gather.arrived
    finish = Gather.finish


class Share:
    order = [(0, 0), (1, 0), (0, -1), (0, 1), (1, -1), (1, 1), (0, 2), (1, 2)]

    def __init__(self, mine, theirs, twin, send, recv):
        self.mine = [mine(*p) for p in self.order]
        self.theirs = [theirs(*p) for p in self.order]
        self.twin = twin
        self.sems = (send, recv)

    def start(self, *which):
        for n in which:
            remote(self.mine[n], self.mine[n], *self.sems, n, self.twin).start()

    def arrived(self, *which):
        for n in which or range(8):
            remote(self.theirs[n], self.theirs[n], *self.sems, n, self.twin).wait_recv()

    def finish(self):
        for n, ref in enumerate(self.mine):
            remote(ref, ref, *self.sems, n, self.twin).wait_send()


class Reduce:
    def __init__(self, block, rows, peers, halves, wholes, last, send, recv):
        half = rows // 2
        pair, after, before = peers

        def part(p, step, h):
            return block(p, step).at[pl.ds(h * half, half)]

        self.block = block
        self.part = part
        self.halves, self.wholes, self.last = halves, wholes, last
        self.out = [
            (part(1, 2, 0), halves.at[0], after), (part(1, 2, 1), halves.at[1], before),
            (part(0, 2, 0), halves.at[2], after), (part(0, 2, 1), halves.at[3], before),
            (block(1, 1), wholes.at[0], after), (block(1, -1), wholes.at[1], before),
            (block(0, 1), wholes.at[2], after), (block(0, -1), wholes.at[3], before),
            (block(1, 0), last, pair),
        ]
        self.sems = (send, recv)

    def start(self, *which):
        for n in which:
            src, dst, peer = self.out[n]
            remote(src, dst, *self.sems, n, peer).start()

    def arrived(self, *which):
        for n in which:
            src, dst, peer = self.out[n]
            remote(src, dst, *self.sems, n, peer).wait_recv()

    def finish(self):
        for n in range(9):
            src, dst, peer = self.out[n]
            remote(src, dst, *self.sems, n, peer).wait_send()

    def second(self, p):
        n = 0 if p else 2
        for k, (step, h) in enumerate(((1, 0), (-1, 1))):
            self.arrived(n + k)
            add_into(self.part(p, step, h), self.halves.at[n + k])
            self.start(4 + n + k)

    def third(self):
        self.arrived(4, 5)
        add_into(self.block(1, 0), self.wholes.at[0], self.wholes.at[1])
        self.start(8)

    def total(self, at):
        f32 = jnp.float32
        parts = [self.block(0, 0), self.wholes.at[2], self.wholes.at[3], self.last]
        return sum(r[at].astype(f32) for r in parts)


class PairReduce:
    steps = (2, 1, -1, 0)

    def __init__(self, block, rows, peers, pairs, halves, wholes, send, recv):
        half = rows // 2
        pair, after, before = peers

        def part(p, step, h):
            return block(p, step).at[pl.ds(h * half, half)]

        self.block = block
        self.part = part
        self.pairs, self.halves, self.wholes = pairs, halves, wholes
        self.out = [(block(1, d), pairs.at[n], pair) for n, d in enumerate(self.steps)] + [
            (part(0, 2, 0), halves.at[0], after), (part(0, 2, 1), halves.at[1], before),
            (block(0, 1), wholes.at[0], after), (block(0, -1), wholes.at[1], before),
        ]
        self.sems = (send, recv)

    start = Reduce.start
    arrived = Reduce.arrived

    def finish(self):
        for n, (src, dst, peer) in enumerate(self.out):
            remote(src, dst, *self.sems, n, peer).wait_send()

    def paired(self, *which):
        for n in which:
            self.arrived(n)
            add_into(self.block(0, self.steps[n]), self.pairs.at[n])

    def second(self):
        for k, (step, h) in enumerate(((1, 0), (-1, 1))):
            self.arrived(4 + k)
            add_into(self.part(0, step, h), self.halves.at[k])
            self.start(6 + k)

    def total(self, at):
        f32 = jnp.float32
        self.arrived(3, 6, 7)
        parts = [self.block(0, 0), self.pairs.at[3], self.wholes.at[0], self.wholes.at[1]]
        return sum(r[at].astype(f32) for r in parts)


def add_into(dst, *terms):
    rows, cols = dst.shape
    tile = next(t for t in (256, 128, 64, 32, 16) if rows % t == 0 and (t * cols <= 32768 or t == 16))

    def one(i, carry):
        at = pl.ds(pl.multiple_of(i * tile, tile), tile)
        total = dst[at, :].astype(jnp.float32)
        for t in terms:
            total = total + t[at, :].astype(jnp.float32)
        dst[at, :] = total.astype(dst.dtype)
        return carry

    lax.fori_loop(0, rows // tile, one, 0)


def chosen(t, values):
    at = values[0]
    for n, v in enumerate(values[1:]):
        at = jnp.where(t == n + 1, v, at)
    return at


def project_kernel(pos_ref, freq_ref, tok_ref, wq_ref, wk_ref, q_ref, cos_ref, sin_ref, kv_ref, tok_out, wq_out, wk_out,
                   tbuf, wqbuf, wkbuf, kvbuf, acc, acc_kv, pos_sc, freq_sc, cos_sc, sin_sc, t_send, t_recv, u_send, u_recv, c_send, c_recv, wa_send, wa_recv, wb_send, wb_recv, wk_send, wk_recv,
                   k_send, k_recv, r_send, r_recv, f_send, f_recv, local, outs):
    f32 = jnp.float32
    bf16 = jnp.bfloat16
    ctx, tp, core, ctx_at, tp_at, ctx_peers, tp_peers, twin = places()
    copies = [
        pltpu.make_async_copy(wk_ref, wkbuf.at[ctx], local.at[0]),
        pltpu.make_async_copy(tok_ref, tbuf.at[tp], local.at[1]),
        pltpu.make_async_copy(wq_ref, wqbuf.at[ctx], local.at[2]),
    ]
    small = [pltpu.make_async_copy(pos_ref, pos_sc, local.at[6]), pltpu.make_async_copy(freq_ref, freq_sc, local.at[7])]
    greet(ctx_peers + tp_peers + [twin])
    for c in copies + small:
        c.start()
    met(ctx_peers + tp_peers + [twin])
    toks = Gather(lambda p, d: tbuf.at[tp_at(p, d), :, pl.ds(0, 3584)], 32, tp_peers, t_send, t_recv)
    round_toks = RingGather(lambda p, d: tbuf.at[tp_at(p, d), :, pl.ds(3584, 512)], 32, tp_peers, u_send, u_recv)
    tshare = Share(lambda p, d: tbuf.at[tp_at(p, d)], lambda p, d: tbuf.at[tp_at(p, d, 1)], twin, c_send, c_recv)
    wqa = Gather(lambda p, d: wqbuf.at[ctx_at(p, d), pl.ds(0, 320)], 320, ctx_peers, wa_send, wa_recv)
    wqb = RingGather(lambda p, d: wqbuf.at[ctx_at(p, d), pl.ds(320, 192)], 192, ctx_peers, wb_send, wb_recv)
    wk = Gather(lambda p, d: wkbuf.at[ctx_at(p, d)], 512, ctx_peers, wk_send, wk_recv)
    for c in copies:
        c.wait()
    toks.start(0, 1)
    wk.start(2, 3)
    round_toks.start(0, 1)
    toks.start(2, 3)
    round_toks.start(4)
    wk.start(0, 1)
    wqb.start(0, 1)
    wqa.start(2, 3)
    tshare.start(0)

    row = lax.broadcasted_iota(jnp.int32, (512, 128), 0)
    for c in small:
        c.wait()
    begin = [pos_sc[pl.ds(ctx * 4 + 2 * t, 1), :][:, 0:1] for t in range(2)]
    place = jnp.where(row < 256, begin[0], begin[1]) + (row & 255)
    angle = place.astype(f32) * freq_sc[...]
    cos_sc[...] = jnp.cos(angle)
    sine = jnp.sin(angle)
    sin_sc[...] = jnp.where(lax.broadcasted_iota(jnp.int32, (512, 128), 1) < 64, -sine, sine)
    acc[...] = jnp.zeros_like(acc)

    round_toks.arrived(0, 1)
    round_toks.start(2, 3, 5, 6)
    wk.arrived(2, 3)
    wk.start(8, 9)
    toks.arrived(0)
    toks.start(4, 5)
    toks.arrived(1)
    toks.start(6, 7)
    toks.arrived(2, 3)
    toks.start(8, 9)
    tshare.start(2, 3)
    round_toks.arrived(4)
    tshare.start(1)
    wqa.arrived(2, 3)
    round_toks.arrived(2, 3)
    round_toks.start(7, 8)
    wqa.start(0, 1)
    wqa.start(8, 9)
    wqb.start(4)
    wk.arrived(0, 1)
    wk.start(4, 5, 6, 7)
    wqb.arrived(0, 1)
    wqb.start(2, 3)
    toks.arrived(4)
    toks.start(10)
    toks.arrived(7)
    toks.start(11)
    toks.arrived(5, 6)
    round_toks.arrived(5, 6)
    tshare.start(4, 5)
    toks.arrived(8, 9)
    tshare.start(6)
    wk.arrived(4)
    wk.start(10)
    wk.arrived(7)
    wk.start(11)
    wqb.start(5, 6)
    wqb.arrived(2, 3)
    wqb.start(7, 8)
    toks.arrived(10, 11)
    round_toks.arrived(7, 8)
    tshare.start(7)
    wk.arrived(5, 6, 8, 9, 10, 11)
    out_wk = pltpu.make_async_copy(wkbuf, wk_out, local.at[3])
    out_wk.start()
    out_cos = pltpu.make_async_copy(cos_sc, cos_ref, local.at[6])
    out_sin = pltpu.make_async_copy(sin_sc, sin_ref, local.at[7])
    out_cos.start()
    out_sin.start()
    wqa.arrived(0, 1)
    wqa.start(4, 5, 6, 7)
    tshare.arrived()
    out_tok = pltpu.make_async_copy(tbuf, tok_out, local.at[4])
    out_tok.start()

    def multiply(total, wbuf, blocks):
        def one(i, carry):
            c = chosen(i // 2, blocks)
            m = lax.rem(i, 2)
            cols = pl.ds(pl.multiple_of(c * 512, 512), 512)
            left = tbuf[pl.ds(m * 8, 8), :, cols].reshape(256, 512)
            rows = pl.ds(pl.multiple_of(m * 256, 256), 256)
            total[rows, :] += jnp.dot(left, wbuf[c], preferred_element_type=f32)
            return carry

        lax.fori_loop(0, 2 * len(blocks), one, 0)

    def keyval(m, carry):
        left = tbuf[pl.ds(m * 8, 8)].reshape(256, 4096)
        rows = pl.ds(pl.multiple_of(m * 256, 256), 256)
        acc_kv[rows, :] = jnp.dot(left, wkbuf[...].reshape(4096, 128), preferred_element_type=f32)
        return carry

    lax.fori_loop(0, 2, keyval, 0)
    cosine, sine = cos_sc[...], sin_sc[...]
    held = acc_kv[...].astype(bf16).astype(f32)
    turned = held * cosine + pltpu.roll(held, 64, 1) * sine
    kvbuf[core, ctx] = jnp.where(core == 0, turned, held).astype(bf16)
    keys = Gather(lambda p, d: kvbuf.at[core, ctx_at(p, d), pl.ds(0, 256)], 256, ctx_peers, k_send, k_recv)
    round_keys = RingGather(lambda p, d: kvbuf.at[core, ctx_at(p, d), pl.ds(256, 256)], 256, ctx_peers, r_send, r_recv)
    kshare = Share(lambda p, d: kvbuf.at[core, ctx_at(p, d)], lambda p, d: kvbuf.at[1 - core, ctx_at(p, d)], twin, f_send, f_recv)
    keys.start(0, 1)
    round_keys.start(0, 1)
    keys.start(2, 3)
    round_keys.start(4)
    kshare.start(0)
    wqa.arrived(8, 9)
    multiply(acc, wqbuf, [ctx_at(0, 0), ctx_at(0, -1), ctx_at(0, 1), ctx_at(0, 2)])
    round_keys.arrived(0, 1)
    round_keys.start(2, 3, 5, 6)
    keys.arrived(0, 1)
    keys.start(4, 5, 6, 7)
    keys.arrived(2, 3)
    keys.start(8, 9)
    kshare.start(2, 3)
    round_keys.arrived(4)
    kshare.start(1)
    wqa.arrived(4)
    wqa.start(10)
    wqa.arrived(7)
    wqa.start(11)
    wqa.arrived(5, 6)
    wqb.arrived(4, 5, 6)
    multiply(acc, wqbuf, [ctx_at(1, 0), ctx_at(1, -1), ctx_at(1, 1)])
    round_keys.arrived(2, 3)
    round_keys.start(7, 8)
    keys.arrived(4)
    keys.start(10)
    keys.arrived(7)
    keys.start(11)
    wqa.arrived(10, 11)
    wqb.arrived(7, 8)
    out_wq = pltpu.make_async_copy(wqbuf, wq_out, local.at[5])
    out_wq.start()
    multiply(acc, wqbuf, [ctx_at(1, 2)])
    for h in range(2):
        raw = acc[:, h * 128:(h + 1) * 128]
        q_ref[:, h * 128:(h + 1) * 128] = (raw * cosine + pltpu.roll(raw, 64, 1) * sine).astype(bf16)
    def block_out(mine, n):
        p, d = Share.order[n]
        plane = core if mine else 1 - core
        at = ctx_at(p, d)
        return pltpu.make_async_copy(kvbuf.at[plane, at], kv_ref.at[plane, at], outs.at[8 * mine + n])

    for n in range(4):
        block_out(1, n).start()
    keys.arrived(5, 6)
    round_keys.arrived(5, 6)
    kshare.start(4, 5)
    keys.arrived(8, 9)
    kshare.start(6)
    for n in (4, 5, 6):
        block_out(1, n).start()
    keys.arrived(10, 11)
    round_keys.arrived(7, 8)
    kshare.start(7)
    block_out(1, 7).start()
    for n in range(8):
        kshare.arrived(n)
        block_out(0, n).start()
    toks.finish()
    round_toks.finish()
    tshare.finish()
    wqa.finish()
    wqb.finish()
    wk.finish()
    keys.finish()
    round_keys.finish()
    kshare.finish()
    out_tok.wait()
    out_wq.wait()
    out_wk.wait()
    out_cos.wait()
    out_sin.wait()
    for n in range(8):
        block_out(0, n).wait()
        block_out(1, n).wait()


def project(positions, frequency, tokens, w_query, w_keyval):
    bf16 = jnp.bfloat16
    f32 = jnp.float32
    vmem = pl.BlockSpec(memory_space=pltpu.VMEM)
    hbm = pl.BlockSpec(memory_space=pltpu.HBM)
    dma = pltpu.SemaphoreType.DMA
    return pl.pallas_call(
        project_kernel,
        out_shape=(
            jax.ShapeDtypeStruct((512, 256), bf16),
            jax.ShapeDtypeStruct((512, 128), f32),
            jax.ShapeDtypeStruct((512, 128), f32),
            jax.ShapeDtypeStruct((2, 8, 512, 128), bf16),
            jax.ShapeDtypeStruct((16, 32, 4096), bf16),
            jax.ShapeDtypeStruct((8, 512, 256), bf16),
            jax.ShapeDtypeStruct((8, 512, 128), bf16),
        ),
        in_specs=[hbm] * 5,
        out_specs=(vmem, hbm, hbm, hbm, hbm, hbm, hbm),
        scratch_shapes=[
            pltpu.VMEM((16, 32, 4096), bf16),
            pltpu.VMEM((8, 512, 256), bf16),
            pltpu.VMEM((8, 512, 128), bf16),
            pltpu.VMEM((2, 8, 512, 128), bf16),
            pltpu.VMEM((512, 256), f32),
            pltpu.VMEM((512, 128), f32),
            pltpu.VMEM((32, 128), jnp.int32),
            pltpu.VMEM((1, 128), f32),
            pltpu.VMEM((512, 128), f32),
            pltpu.VMEM((512, 128), f32),
            dma((12,)), dma((12,)), dma((9,)), dma((9,)), dma((8,)), dma((8,)),
            dma((12,)), dma((12,)), dma((9,)), dma((9,)), dma((12,)), dma((12,)),
            dma((12,)), dma((12,)), dma((9,)), dma((9,)), dma((8,)), dma((8,)), dma((8,)), dma((16,)),
        ],
        compiler_params=pltpu.CompilerParams(collective_id=0, has_side_effects=True, vmem_limit_bytes=VMEM_LIMIT),
        name="project",
    )(positions.reshape(32, 128), frequency, tokens, w_query, w_keyval)


TOKEN_PARTS = ((0, 2), (2, 3), (5, 3))


def reduce_kernel(tok_ref, wq_ref, wk_ref, qb_ref, dkv_ref, cos_ref, sin_ref, tg_ref, sum_ref,
                  tbuf, wqbuf, wkbuf, kv, kv_in, kv_halves, kv_wholes, kv_last, kp_pairs, kp_halves, kp_wholes, turned_q, kvg,
                  wq, wq_halves, wq_wholes, wq_last, wp_pairs, wp_halves, wp_wholes, wk, wk_halves, wk_wholes, wk_last,
                  qb, cos_sc, sin_sc, px, parts_out, parts_in, parts_halves, parts_wholes, parts_last, pair_parts,
                  k_send, k_recv, kp_send, kp_recv, wp_send, wp_recv, wq_send, wq_recv, wk_send, wk_recv,
                  t_send, t_recv, e_send, e_recv, local):
    f32 = jnp.float32
    bf16 = jnp.bfloat16
    nt = (((1,), (1,)), ((), ()))
    ctx, tp, core, ctx_at, tp_at, ctx_peers, tp_peers, twin = places()
    copies = [
        pltpu.make_async_copy(dkv_ref.at[core], kv, local.at[0]),
        pltpu.make_async_copy(tok_ref, tbuf, local.at[1]),
        pltpu.make_async_copy(wq_ref, wqbuf, local.at[2]),
        pltpu.make_async_copy(wk_ref, wkbuf, local.at[3]),
        pltpu.make_async_copy(cos_ref, cos_sc, local.at[4]),
        pltpu.make_async_copy(sin_ref, sin_sc, local.at[5]),
    ]
    first = pltpu.make_async_copy(qb_ref, qb, local.at[6])
    greet(ctx_peers + tp_peers + [twin])
    first.start()
    for c in copies:
        c.start()
    met(ctx_peers + tp_peers + [twin])
    side = tp // 8
    steps = (2, 1, -1, 0)

    def ring_of(d):
        return lax.rem(ctx // 2 + d + 4, 4)

    def pair_of(d):
        return pl.ds(pl.multiple_of(ring_of(d) * 2, 2), 2)

    swap = [
        remote(dkv_ref.at[1 - core, pair_of(d)], kv_in.at[pair_of(d)], e_send, e_recv, 12 + n, twin)
        for n, d in enumerate(steps)
    ]
    for s in swap:
        s.start()
    first.wait()
    turned_q[...] = qb[...].T
    order = [ctx_at(p, d) for d in steps for p in (1, 0)]

    def tok_cols(c):
        return tbuf[:, :, pl.ds(pl.multiple_of(c * 512, 512), 512)].reshape(512, 512)

    def query_terms(i, carry):
        c = chosen(i, order)
        wq[c] = jnp.dot(turned_q[...], tok_cols(c), preferred_element_type=f32).astype(bf16)
        return carry

    keys = Reduce(
        lambda p, d: kv.at[ctx_at(p, d), pl.ds(0, 256)], 256, ctx_peers, kv_halves, kv_wholes, kv_last, k_send, k_recv
    )
    pair_keys = PairReduce(
        lambda p, d: kv.at[ctx_at(p, d), pl.ds(256, 256)], 256, ctx_peers, kp_pairs, kp_halves, kp_wholes, kp_send, kp_recv
    )
    wq_sum = Reduce(
        lambda p, d: wq.at[ctx_at(p, d), pl.ds(0, 128)], 128, ctx_peers, wq_halves, wq_wholes, wq_last, wq_send, wq_recv
    )
    wp_sum = PairReduce(
        lambda p, d: wq.at[ctx_at(p, d), pl.ds(128, 128)], 128, ctx_peers, wp_pairs, wp_halves, wp_wholes, wp_send, wp_recv
    )
    wk_sum = Reduce(lambda p, d: wk.at[ctx_at(p, d)], 128, ctx_peers, wk_halves, wk_wholes, wk_last, wk_send, wk_recv)
    copies[1].wait()
    lax.fori_loop(0, 1, query_terms, 0)
    wq_sum.start(0, 1)
    wp_sum.start(0)
    copies[0].wait()
    for n, d in enumerate(steps):
        swap[n].wait_recv()
        for p in (1, 0):
            add_into(kv.at[ctx_at(p, d)], kv_in.at[ctx_at(p, d)])
        pair_keys.start(n)
        if d == 2:
            keys.start(0, 1, 2, 3)
    lax.fori_loop(1, 2, query_terms, 0)
    wq_sum.start(2, 3)
    lax.fori_loop(2, 4, query_terms, 0)
    keys.second(1)
    keys.second(0)
    wp_sum.start(1)
    pair_keys.paired(0)
    pair_keys.start(4, 5)
    lax.fori_loop(4, 6, query_terms, 0)
    pair_keys.paired(1, 2)
    pair_keys.second()
    wq_sum.second(1)
    keys.third()
    lax.fori_loop(6, 8, query_terms, 0)
    wp_sum.start(2, 3)
    wq_sum.second(0)
    wp_sum.paired(0)
    wp_sum.start(4, 5)
    copies[2].wait()

    def query_part(c, carry):
        px[c] = lax.dot_general(qb[...], wqbuf[c], nt, preferred_element_type=f32)
        return carry

    lax.fori_loop(0, 8, query_part, 0)
    copies[3].wait()
    keys.arrived(6, 7, 8)
    total = jnp.concatenate([keys.total(...), pair_keys.total(...)], axis=0)
    copies[4].wait()
    copies[5].wait()
    back = total * cos_sc[...] - pltpu.roll(total, 64, 1) * sin_sc[...]
    total = jnp.where(core == 0, back, total)
    kvg[...] = total.astype(bf16)

    def level_of(d):
        return lax.rem(tp // 2 + d + 4, 4)

    count = len(TOKEN_PARTS)
    swaps = [
        [
            remote(parts_out[h].at[1 - core, level_of(d)], parts_in[h].at[level_of(d)], e_send, e_recv, 4 * h + n, twin)
            for n, d in enumerate(steps)
        ]
        for h in range(count)
    ]

    def tg_block(h):
        return lambda p, d: parts_out[h].at[core, level_of(d), 1 - side if p else side]

    toks = [
        Reduce(
            tg_block(h), 32, tp_peers, parts_halves[h], parts_wholes[h], parts_last[h], t_send.at[h], t_recv.at[h]
        )
        for h in range(2)
    ]
    pair_toks = PairReduce(
        tg_block(2), 32, tp_peers, pair_parts, parts_halves[2], parts_wholes[2], t_send.at[2], t_recv.at[2]
    )

    def merged(h, *which):
        for n in which:
            swaps[h][n].wait_recv()
            for p in (1, 0):
                add_into(tg_block(h)(p, steps[n]), parts_in[h].at[level_of(steps[n]), 1 - side if p else side])

    def keyval_part(h):
        first, tiles = TOKEN_PARTS[h]

        def one(c, carry):
            part = px[c] + lax.dot_general(kvg[...], wkbuf[c], nt, preferred_element_type=f32)
            part = part.astype(bf16).reshape(2, 4, 2, 32, 512)
            cols = pl.ds(pl.multiple_of((c - first) * 512, 512), 512)
            for s in range(2):
                for level in range(4):
                    for k in range(2):
                        parts_out[h][k, level, s, :, cols] = part[s, level, k]
            return carry

        lax.fori_loop(first, first + tiles, one, 0)
        for s in swaps[h]:
            s.start()

    def keyval_terms(i, carry):
        c = chosen(i, order)
        wk[c] = jnp.dot(turned_q[0:128, :], tok_cols(c), preferred_element_type=f32).astype(bf16)
        return carry

    keyval_part(0)
    turned_q[0:128, :] = total.T.astype(bf16)
    keyval_part(2)
    merged(0, 0)
    toks[0].start(0, 1, 2, 3)
    lax.fori_loop(0, 2, keyval_terms, 0)
    wk_sum.start(0, 1, 2, 3)
    for n in range(4):
        merged(2, n)
        pair_toks.start(n)
    keyval_part(1)
    merged(1, 0)
    toks[1].start(0, 1, 2, 3)
    merged(0, 1, 2, 3)
    toks[0].second(1)
    toks[0].second(0)
    wp_sum.paired(1, 2)
    wp_sum.second()
    lax.fori_loop(2, 8, keyval_terms, 0)
    pair_toks.paired(0)
    pair_toks.start(4, 5)
    merged(1, 1, 2, 3)
    toks[1].second(1)
    toks[1].second(0)
    wk_sum.second(1)
    wk_sum.second(0)
    wq_sum.third()
    pair_toks.paired(1, 2)
    pair_toks.second()
    toks[0].third()
    toks[1].third()
    wk_sum.third()
    wq_sum.arrived(6, 7, 8)
    sum_ref[0:128, :] = wq_sum.total(...)
    sum_ref[128:256, :] = wp_sum.total(...)
    for h in (0, 2, 1):
        first, tiles = TOKEN_PARTS[h]
        if h < 2:
            toks[h].arrived(6, 7, 8)
        part = toks[h] if h < 2 else pair_toks
        tg_ref[:, first * 512:(first + tiles) * 512] = part.total(...).astype(bf16)
    wk_sum.arrived(6, 7, 8)
    sum_ref[256:384, :] = wk_sum.total(...)
    for s in swap + sum(swaps, []):
        s.wait_send()
    for r in [keys, pair_keys, wq_sum, wp_sum, wk_sum, pair_toks] + toks:
        r.finish()


def reduce(tok_full, wq_full, wk_full, query_back, dkv, cosine, sine):
    bf16 = jnp.bfloat16
    f32 = jnp.float32
    vmem = pl.BlockSpec(memory_space=pltpu.VMEM)
    hbm = pl.BlockSpec(memory_space=pltpu.HBM)
    dma = pltpu.SemaphoreType.DMA
    return pl.pallas_call(
        reduce_kernel,
        out_shape=(
            jax.ShapeDtypeStruct((32, 4096), bf16),
            jax.ShapeDtypeStruct((384, 512), f32),
        ),
        in_specs=[hbm] * 7,
        out_specs=(vmem, vmem),
        scratch_shapes=[
            pltpu.VMEM((16, 32, 4096), bf16),
            pltpu.VMEM((8, 512, 256), bf16),
            pltpu.VMEM((8, 512, 128), bf16),
            pltpu.VMEM((8, 512, 128), bf16),
            pltpu.VMEM((8, 512, 128), bf16),
            pltpu.VMEM((4, 128, 128), bf16),
            pltpu.VMEM((4, 256, 128), bf16),
            pltpu.VMEM((256, 128), bf16),
            pltpu.VMEM((4, 256, 128), bf16),
            pltpu.VMEM((2, 128, 128), bf16),
            pltpu.VMEM((2, 256, 128), bf16),
            pltpu.VMEM((256, 512), bf16),
            pltpu.VMEM((512, 128), bf16),
            pltpu.VMEM((8, 256, 512), bf16),
            pltpu.VMEM((4, 64, 512), bf16),
            pltpu.VMEM((4, 128, 512), bf16),
            pltpu.VMEM((128, 512), bf16),
            pltpu.VMEM((4, 128, 512), bf16),
            pltpu.VMEM((2, 64, 512), bf16),
            pltpu.VMEM((2, 128, 512), bf16),
            pltpu.VMEM((8, 128, 512), bf16),
            pltpu.VMEM((4, 64, 512), bf16),
            pltpu.VMEM((4, 128, 512), bf16),
            pltpu.VMEM((128, 512), bf16),
            pltpu.VMEM((512, 256), bf16),
            pltpu.VMEM((512, 128), f32),
            pltpu.VMEM((512, 128), f32),
            pltpu.VMEM((8, 512, 512), f32),
            [pltpu.VMEM((2, 4, 2, 32, 512 * n), bf16) for _, n in TOKEN_PARTS],
            [pltpu.VMEM((4, 2, 32, 512 * n), bf16) for _, n in TOKEN_PARTS],
            [pltpu.VMEM((4, 16, 512 * n), bf16) for _, n in TOKEN_PARTS],
            [pltpu.VMEM((4, 32, 512 * n), bf16) for _, n in TOKEN_PARTS],
            [pltpu.VMEM((32, 512 * n), bf16) for _, n in TOKEN_PARTS],
            pltpu.VMEM((4, 32, 512 * TOKEN_PARTS[2][1]), bf16),
            dma((9,)), dma((9,)), dma((8,)), dma((8,)), dma((8,)), dma((8,)),
            dma((9,)), dma((9,)), dma((9,)), dma((9,)), dma((3, 9)), dma((3, 9)),
            dma((16,)), dma((16,)), dma((7,)),
        ],
        compiler_params=pltpu.CompilerParams(collective_id=1, has_side_effects=True, vmem_limit_bytes=VMEM_LIMIT),
        name="reduce",
    )(tok_full, wq_full, wk_full, query_back, dkv, cosine, sine)


def finish_kernel(tg_ref, sum_ref, token_ref, gq_ref, gk_ref):
    token_ref[...] = tg_ref[...]
    gq_ref[...] = sum_ref[0:256, :].T
    gk_ref[...] = sum_ref[256:384, :].T


def finish(token_grad, weight_grad):
    return pl.pallas_call(
        finish_kernel,
        grid=(2,),
        out_shape=(
            jax.ShapeDtypeStruct((32, 4096), jnp.bfloat16),
            jax.ShapeDtypeStruct((512, 256), jnp.float32),
            jax.ShapeDtypeStruct((512, 128), jnp.float32),
        ),
        in_specs=[pl.BlockSpec((32, 2048), lambda i: (0, i)), pl.BlockSpec((384, 256), lambda i: (0, i))],
        out_specs=(
            pl.BlockSpec((32, 2048), lambda i: (0, i)),
            pl.BlockSpec((256, 256), lambda i: (i, 0)),
            pl.BlockSpec((256, 128), lambda i: (i, 0)),
        ),
        name="finish",
    )(token_grad, weight_grad)


def shards(tokens, upstream, w_query, w_keyval, positions, documents):
    powers = np.arange(HEAD_DIMENSION // 2, dtype=np.float32) * np.float32(2.0 / HEAD_DIMENSION)
    frequency = np.power(np.float32(rope_base), -powers).astype(np.float32)
    frequency = jnp.asarray(np.concatenate([frequency, frequency])[None, :])
    query, cosine, sine, key_value, tok_full, wq_full, wk_full = project(positions, frequency, tokens, w_query, w_keyval)
    query_back, dkv = attend(positions, documents, query, upstream, key_value, cosine, sine)
    return finish(*reduce(tok_full, wq_full, wk_full, query_back, dkv.reshape(2, 8, 512, 128), cosine, sine))


def solution(mesh):
    return jax.shard_map(
        shards,
        mesh=mesh,
        in_specs=(P(("ctx", "tp"), None), P("ctx", "tp"), P("ctx", "tp"), P("ctx", "tp"), P(), P()),
        out_specs=(P(("ctx", "tp"), None), P("ctx", "tp"), P("ctx", "tp")),
        check_vma=False,
    )
```
